32 devices in a mesh: ctx: 16 (over z, x, core), fsdp: 2 (over y).
Axes of the slice: x: 2, y: 2, z: 4, core: 2. Of those that a mesh axis runs over, the one named last changes fastest.
Arguments:
- tokens: bfloat16 [2, 4096, 1024], P('fsdp', 'ctx'), may hold values from -6 to 6
- encoder: bfloat16 [2, 2048, 1024], P('fsdp', 'ctx'), may hold values from -6 to 6
- cotangent: bfloat16 [2, 4096, 1024], P('fsdp', 'ctx'), may hold values from -6 to 6
- seq_lengths: int32 [2, 2], P('fsdp'), may hold values from 1024 to 3072, as said below
- source_lengths: int32 [2, 2], P('fsdp'), may hold values from 512 to 1536, as said below
- pair_order: int32 [2, 16], P('fsdp'), may hold values from 0 to 15, each once within a row
- pair_flip: int32 [2, 16], P('fsdp'), may hold values 0 or 1
- ln_gain: bfloat16 [3, 1024], P(None, 'fsdp'), may hold values from 0.25 to 1.75
- ln_bias: bfloat16 [3, 1024], P(None, 'fsdp'), may hold values from -4 to 4
- attn_bias: bfloat16 [2, 3, 1024], P(None, None, 'fsdp'), may hold values from -4 to 4
- self_qkv: bfloat16 [1024, 3072], P('fsdp'), may hold values from -0.1875 to 0.1875
- self_out: bfloat16 [1024, 1024], P('fsdp'), may hold values from -1.5 to 1.5
- cross_q: bfloat16 [1024, 1024], P('fsdp'), may hold values from -0.1875 to 0.1875
- cross_kv: bfloat16 [1024, 2048], P('fsdp'), may hold values from -0.1875 to 0.1875
- cross_out: bfloat16 [1024, 1024], P('fsdp'), may hold values from -1.5 to 1.5
- w_up: bfloat16 [1024, 8192], P('fsdp'), may hold values from -0.1875 to 0.1875
- up_bias: bfloat16 [8192], P('fsdp'), may hold values from -4 to 4
- w_down: bfloat16 [8192, 1024], P('fsdp'), may hold values from -0.0625 to 0.0625
- down_bias: bfloat16 [1024], P('fsdp'), may hold values from -4 to 4
Outputs:
- output: bfloat16 [2, 4096, 1024], P('fsdp', 'ctx')
- grad_tokens: float32 [2, 4096, 1024], P('fsdp', 'ctx')
- grad_encoder: float32 [2, 2048, 1024], P('fsdp', 'ctx')
- grad_ln_gain: float32 [3, 1024], P(None, ('ctx', 'fsdp'))
- grad_ln_bias: float32 [3, 1024], P(None, ('ctx', 'fsdp'))
- grad_attn_bias: float32 [2, 3, 1024], P(None, None, ('ctx', 'fsdp'))
- grad_self_qkv: float32 [1024, 3072], P(('ctx', 'fsdp'))
- grad_self_out: float32 [1024, 1024], P(('ctx', 'fsdp'))
- grad_cross_q: float32 [1024, 1024], P(('ctx', 'fsdp'))
- grad_cross_kv: float32 [1024, 2048], P(('ctx', 'fsdp'))
- grad_cross_out: float32 [1024, 1024], P(('ctx', 'fsdp'))
- grad_w_up: float32 [1024, 8192], P(('ctx', 'fsdp'))
- grad_up_bias: float32 [8192], P(('ctx', 'fsdp'))
- grad_w_down: float32 [8192, 1024], P(('ctx', 'fsdp'))
- grad_down_bias: float32 [1024], P(('ctx', 'fsdp'))
The draws below stay inside these ranges and needn't reach their ends.
Inputs may be any that keep to these rules, and one draw needn't show every extreme that they name: `seq_lengths`: each row has 2 lengths summing to 4096; the least and the largest are both reached in every row. `source_lengths`: each row has 2 lengths summing to 2048; the least and the largest are both reached in every row. `pair_order`: each row names every pair once; slot j lies on device j // 1 of ctx.
All inputs are finite; a program needn't handle non-finite values. No bound on the sum of `pair_flip` on one device may be relied on, other than what follows from the above.
Results may differ from the reference program's by a relative error of at most 0.025.
Values may be sent and summed in bfloat16 or wider, within the bound.
No kernel may reach another device: no remote copies, remote signals or barrier semaphores. Data moves between devices by JAX's collectives and lax.ppermute only.
A program may use at most 320 MiB of HBM per device.

```python
import jax
import jax.numpy as jnp
from jax import lax

D = 1024
H = 16
FF = 8192
BLOCK = 128
MINLEN = 1024
GROUP = 4096
NB = 32
NSEQ = 2
SRC_MIN = 512
SRC_GROUP = 2048
N_FSDP = 2


def paired_lengths(key, least):
    half = NSEQ // 2
    key_extra, key_forced, key_order = jax.random.split(key, 3)
    extra = jax.random.randint(key_extra, (N_FSDP, half), 0, 2 * least + 1)
    forced = jax.random.randint(key_forced, (N_FSDP, 1), 0, half)
    extra = jnp.where(jnp.arange(half)[None, :] == forced, 0, extra)
    pairs = jnp.stack([least + extra, 3 * least - extra], axis=2).reshape(N_FSDP, NSEQ)
    orders = jax.vmap(lambda k: jax.random.permutation(k, NSEQ))(jax.random.split(key_order, N_FSDP))
    return jnp.take_along_axis(pairs, orders, axis=1).astype(jnp.int32)


def draw_seq_lengths(key, part):
    return paired_lengths(jax.random.fold_in(key, 11), MINLEN)


def draw_source_lengths(key, part):
    return paired_lengths(jax.random.fold_in(key, 23), SRC_MIN)


def place_ends(values, rng, low, high):
    extent = values.shape
    place = [jax.random.randint(jax.random.fold_in(rng, axis), (), 0, extent[axis]) for axis in range(len(extent))]
    values = values.at[tuple(place)].set(low)
    longest = extent.index(max(extent))
    place[longest] = (place[longest] + 1) % extent[longest]
    return values.at[tuple(place)].set(high)


def level_of(stream_key, dims, shards, low, largest):
    level = 1.0
    for position, shards_of in shards:
        heights = jax.random.uniform(jax.random.fold_in(jax.random.fold_in(stream_key, 6), position), (shards_of,), jnp.float32, low / len(shards), largest / len(shards))
        level = level * jnp.repeat(jnp.exp(heights), dims[position] // shards_of).reshape((-1,) + (1,) * (len(dims) - 1 - position))
    return level


def noise(key, dims, deviation, bound, shards=(), held_as=jnp.bfloat16):
    values = deviation * jax.random.normal(key, dims, jnp.float32)
    if shards:
        values = values * level_of(key, dims, shards, -0.22, 0.18)
    return jnp.clip(values, -bound, bound).astype(held_as)


def setup_inputs(seed: int = 0) -> dict:
    arg_keys = jax.random.split(jax.random.key(seed), 20)
    return {
        "tokens": noise(arg_keys[0], (N_FSDP, GROUP, D), 1.0, 6.0, ((0, 2), (1, 16))),
        "encoder": noise(arg_keys[1], (N_FSDP, SRC_GROUP, D), 1.0, 6.0, ((0, 2), (1, 16))),
        "cotangent": noise(arg_keys[2], (N_FSDP, GROUP, D), 1.0, 6.0, ((0, 2), (1, 16))),
        "seq_lengths": draw_seq_lengths(jax.random.fold_in(arg_keys[19], 71), 0),
        "source_lengths": draw_source_lengths(jax.random.fold_in(arg_keys[19], 71), 0),
        "pair_order": jax.vmap(lambda own: jax.random.permutation(own, NB // 2))(jax.random.split(arg_keys[5], N_FSDP)).reshape((N_FSDP, NB // 2)).astype(jnp.int32),
        "pair_flip": place_ends((jax.random.randint(arg_keys[6], (N_FSDP, NB // 2), 0, 2) < 1).astype(jnp.int32), jax.random.fold_in(arg_keys[6], 1), 0, 1),
        "ln_gain": jnp.clip(1.0 + 0.15 * jax.random.normal(arg_keys[7], (3, D), jnp.float32), 0.25, 1.75).astype(jnp.bfloat16),
        "ln_bias": noise(arg_keys[8], (3, D), 0.3, 4.0, ((1, 2),)),
        "attn_bias": noise(arg_keys[9], (2, 3, D), 0.3, 4.0, ((2, 2),)),
        "self_qkv": noise(arg_keys[10], (D, 3 * D), D ** -0.5, 0.1875, ((0, 2),)),
        "self_out": noise(arg_keys[11], (D, D), (D // 64) ** -0.5, 1.5, ((0, 2),)),
        "cross_q": noise(arg_keys[12], (D, D), D ** -0.5, 0.1875, ((0, 2),)),
        "cross_kv": noise(arg_keys[13], (D, 2 * D), D ** -0.5, 0.1875, ((0, 2),)),
        "cross_out": noise(arg_keys[14], (D, D), (D // 64) ** -0.5, 1.5, ((0, 2),)),
        "w_up": noise(arg_keys[15], (D, FF), D ** -0.5, 0.1875, ((0, 2),)),
        "up_bias": noise(arg_keys[16], (FF,), 0.3, 4.0, ((0, 2),)),
        "w_down": noise(arg_keys[17], (FF, D), FF ** -0.5, 0.0625, ((0, 2),)),
        "down_bias": noise(arg_keys[18], (D,), 0.3, 4.0, ((0, 2),)),
    }


@jax.custom_vjp
def low(v):
    return lax.optimization_barrier(v.astype(jnp.bfloat16)).astype(jnp.float32)

@jax.custom_vjp
def low_back(v):
    return v

def low_keep(v):
    return (low(v), None)

def low_pass(kept, grad):
    return (grad,)

def back_keep(v):
    return (v, None)

def back_low(kept, grad):
    return (low(grad),)
low.defvjp(low_keep, low_pass)
low_back.defvjp(back_keep, back_low)
ln_eps = 1e-05
score_scale = 0.125

def layer_norm(v, gain, shift):
    centred = v - lax.optimization_barrier(jnp.mean(v, axis=-1, keepdims=True))
    spread = lax.optimization_barrier(jnp.mean(centred * centred, axis=-1, keepdims=True))
    return centred * lax.rsqrt(spread + ln_eps) * gain + shift

def gelu_tanh(v):
    return 0.5 * v * (1.0 + jnp.tanh(0.7978845608028654 * (v + 0.044715 * v * v * v)))

def rounded(v):
    return low_back(low(v))

def matmul(left, right):
    return jnp.dot(left, right, precision=lax.Precision.HIGHEST)

def token_positions(order, flip):
    lower = order.astype(jnp.int32)
    upper = 2 * order.shape[0] - 1 - lower
    first = jnp.where(flip == 1, upper, lower)
    second = jnp.where(flip == 1, lower, upper)
    blocks = jnp.stack([first, second], axis=1).reshape(-1)
    offsets = jnp.arange(BLOCK, dtype=jnp.int32)
    return (blocks[:, None] * BLOCK + offsets[None, :]).reshape(-1).astype(jnp.int32)

def document_of(places, lengths):
    ends = jnp.cumsum(lengths.astype(jnp.int32), dtype=jnp.int32)
    return lax.optimization_barrier(jnp.sum((ends[None, :] <= places[:, None]).astype(jnp.int32), axis=1, dtype=jnp.int32))

def attend(query, keys, values, places, docs, allow):
    rows = query.shape[0]
    width = min(512, rows)
    count = keys.shape[0]
    key_heads = keys.reshape(count, H, -1)
    value_heads = values.reshape(count, H, -1)

    def block(item):
        part_query, part_places, part_docs = item
        scores = jnp.einsum('rhd,khd->hrk', part_query.reshape(width, H, -1), key_heads, precision=lax.Precision.HIGHEST) * score_scale
        scores = low_back(scores)
        scores = jnp.where(allow(part_places, part_docs)[None], scores, -1e+30)
        top = lax.optimization_barrier(jnp.max(scores, axis=-1, keepdims=True))
        expd = jnp.exp(scores - top)
        probs = low(expd / lax.optimization_barrier(jnp.sum(expd, axis=-1, keepdims=True)))
        mixed = jnp.einsum('hrk,khd->rhd', probs, value_heads, precision=lax.Precision.HIGHEST)
        return mixed.reshape(width, -1)
    outputs = lax.map(jax.checkpoint(block), (query.reshape(rows // width, width, -1), places.reshape(rows // width, width), docs.reshape(rows // width, width)))
    return outputs.reshape(rows, -1)

def layer_forward(x, enc, params, places, docs, src_docs):
    gains, shifts, biases, wqkv, wout, wcq, wckv, wcout, wup, bup, wdown, bdown = params
    width = x.shape[1]

    def self_allow(part_places, part_docs):
        return (part_docs[:, None] == docs[None, :]) & (places[None, :] <= part_places[:, None])

    def cross_allow(part_places, part_docs):
        return part_docs[:, None] == src_docs[None, :]
    normed_one = low(layer_norm(x, gains[0], shifts[0]))
    projected = matmul(normed_one, wqkv)
    query = rounded(projected[:, :width] + biases[0, 0])
    keys = rounded(projected[:, width:2 * width])
    values = rounded(projected[:, 2 * width:] + biases[0, 1])
    self_att = rounded(attend(query, keys, values, places, docs, self_allow))
    mixed_one = x + low_back(matmul(self_att, wout) + biases[0, 2])
    normed_two = low(layer_norm(mixed_one, gains[1], shifts[1]))
    cross_query = rounded(matmul(normed_two, wcq) + biases[1, 0])
    src_proj = matmul(enc, wckv)
    cross_keys = rounded(src_proj[:, :width])
    cross_values = rounded(src_proj[:, width:] + biases[1, 1])
    cross_att = rounded(attend(cross_query, cross_keys, cross_values, places, docs, cross_allow))
    mixed_two = mixed_one + low_back(matmul(cross_att, wcout) + biases[1, 2])
    normed_three = low(layer_norm(mixed_two, gains[2], shifts[2]))
    hidden = low_back(matmul(normed_three, wup) + bup)
    activated = low(gelu_tanh(hidden))
    return mixed_two + low_back(matmul(activated, wdown) + bdown)

def reference(tokens, encoder, cotangent, seq_lengths, source_lengths, pair_order, pair_flip, ln_gain, ln_bias, attn_bias, self_qkv, self_out, cross_q, cross_kv, cross_out, w_up, up_bias, w_down, down_bias):
    weights = tuple((w.astype(jnp.float32) for w in (ln_gain, ln_bias, attn_bias, self_qkv, self_out, cross_q, cross_kv, cross_out, w_up, up_bias, w_down, down_bias)))
    results = []
    grad_inputs = []
    grad_sources = []
    totals = jax.tree.map(jnp.zeros_like, weights)
    for group in range(tokens.shape[0]):
        places = token_positions(pair_order[group], pair_flip[group])
        docs = document_of(places, seq_lengths[group])
        src_docs = document_of(jnp.arange(encoder.shape[1], dtype=jnp.int32), source_lengths[group])

        def forward(x, enc, params):
            return layer_forward(x, enc, params, places, docs, src_docs)
        result, pull = jax.vjp(forward, tokens[group].astype(jnp.float32), encoder[group].astype(jnp.float32), weights)
        grad_x, grad_enc, grad_params = pull(cotangent[group].astype(jnp.float32))
        results.append(result.astype(jnp.bfloat16))
        grad_inputs.append(grad_x)
        grad_sources.append(grad_enc)
        totals = jax.tree.map(lambda a, b: a + b, totals, grad_params)
    return (jnp.stack(results), jnp.stack(grad_inputs), jnp.stack(grad_sources), totals[0], totals[1], totals[2], totals[3], totals[4], totals[5], totals[6], totals[7], totals[8], totals[9], totals[10], totals[11])
```

```python
import functools

import jax
import jax.numpy as jnp
from jax import lax
from jax.experimental import pallas as pl
from jax.experimental.pallas import tpu as pltpu
from jax.sharding import Mesh
from jax.sharding import PartitionSpec as P

H = 16
BLOCK = 128

CHIP = ("part", "hc")
HEADS = ("hc", "core")
CTX = ("part", "hc", "core")
QUAD = ("core", "fsdp")
ALL = ("part", "hc", "core", "fsdp")

ln_eps = 1e-05
score_scale = 0.125
low = jnp.bfloat16
full = jnp.float32
VMEM_BYTES = 56 * 1024 * 1024


def layer_norm(v, gain, shift):
    centred = v - jnp.mean(v, axis=-1, keepdims=True)
    spread = jnp.mean(centred * centred, axis=-1, keepdims=True)
    return centred * lax.rsqrt(spread + ln_eps) * gain + shift


def gelu_tanh(v):
    return 0.5 * v * (1.0 + jnp.tanh(0.7978845608028654 * (v + 0.044715 * v * v * v)))


def contract(left, right, left_dim, right_dim):
    return lax.dot_general(
        left, right, (((left_dim,), (right_dim,)), ((), ())), preferred_element_type=full
    )


def column_sums(values):
    return jnp.sum(values.astype(full), axis=0)


def block_numbers(order, flip):
    upper = 2 * order.shape[0] - 1 - order
    first = jnp.where(flip == 1, upper, order)
    second = jnp.where(flip == 1, order, upper)
    return jnp.stack([first, second], axis=1).reshape(-1)


def sorted_slots(blocks):
    count = blocks.shape[0]
    rank = jnp.sum((blocks[None, :] < blocks[:, None]).astype(jnp.int32), axis=1)
    hit = rank[None, :] == jnp.arange(count, dtype=jnp.int32)[:, None]
    return jnp.sum(jnp.where(hit, jnp.arange(count, dtype=jnp.int32)[None, :], 0), axis=1)


def document_starts(places, lengths):
    ends = jnp.cumsum(lengths, dtype=jnp.int32)
    passed = ends[None, :] <= places[:, None]
    return jnp.max(jnp.where(passed, ends[None, :], 0), axis=1)


def source_range(places, lengths, source_lengths):
    ends = jnp.cumsum(lengths, dtype=jnp.int32)
    passed = ends[None, :] <= places[:, None]
    source_ends = jnp.cumsum(source_lengths, dtype=jnp.int32)
    start = jnp.max(jnp.where(passed, source_ends[None, :], 0), axis=1)
    stop = jnp.min(jnp.where(passed, source_ends[-1], source_ends[None, :]), axis=1)
    return start, stop


def tile_plan(start, stop, query_tile, key_tile):
    start = start.reshape(-1, query_tile)
    stop = stop.reshape(-1, query_tile)
    first = jnp.min(start, axis=1) // key_tile
    last = (jnp.max(stop, axis=1) + key_tile - 1) // key_tile
    inner = jnp.clip((jnp.max(start, axis=1) + key_tile - 1) // key_tile, first, last)
    outer = jnp.clip(jnp.min(stop, axis=1) // key_tile, inner, last)
    return jnp.stack([first, inner, outer, last]).astype(jnp.int32)


def over_tiles(plan, tile_number, step, carry):
    first, inner = plan[0, tile_number], plan[1, tile_number]
    outer, last = plan[2, tile_number], plan[3, tile_number]
    carry = lax.fori_loop(inner, outer, functools.partial(step, masked=False), carry)
    before = inner - first

    def edge(index, state):
        number = jnp.where(index < before, first + index, outer + index - before)
        return step(number, state, masked=True)

    return lax.fori_loop(0, before + last - outer, edge, carry)


def masked_scores(scores, number, tile, start, stop):
    keys = number * tile + lax.broadcasted_iota(jnp.int32, scores.shape, 0)
    return jnp.where((keys >= start) & (keys < stop), scores, -jnp.inf)


def forward_tiles(plan, number, query, start, stop, keys_of, values_of, tile, depth):
    width = query.shape[1]

    def step(j, carry, masked):
        top, total, accum = carry
        scores = contract(keys_of(j), query, 1, 0)
        if masked:
            scores = masked_scores(scores, j, tile, start, stop)
        newtop = jnp.maximum(top, jnp.max(scores, axis=0, keepdims=True))
        weights = jnp.exp(scores - newtop)
        factor = jnp.exp(top - newtop)
        total = total * factor + jnp.sum(weights, axis=0, keepdims=True)
        accum = accum * factor + contract(values_of(j), weights.astype(low), 1, 0)
        return newtop, total, accum

    carry = (
        jnp.full((1, width), -1e30, full),
        jnp.zeros((1, width), full),
        jnp.zeros((depth, width), full),
    )
    top, total, accum = over_tiles(plan, number, step, carry)
    return accum / total, top + jnp.log(total)


def tile_at(number, size):
    return pl.ds(pl.multiple_of(number * size, size), size)


def half_at(slot):
    return pl.ds(pl.multiple_of((slot & 1) * BLOCK, BLOCK), BLOCK)


def self_forward_kernel(
    tile, plan, query_slot, key_slot, range_ref, own_ref, all_ref,
    out_ref, exact_ref, lse_ref, query_s, key_s, value_s,
):
    depth, queries = query_s.shape
    count = value_s.shape[1]

    @pl.loop(0, queries // BLOCK)
    def _(b):
        slot = query_slot[b]
        query_s[:, tile_at(b, BLOCK)] = own_ref[slot >> 1, 0:depth, half_at(slot)] * low(score_scale)

    @pl.loop(0, count // BLOCK)
    def _(b):
        slot = key_slot[b]
        block = all_ref[slot >> 1, depth : 2 * depth, half_at(slot)]
        key_s[tile_at(b, BLOCK), :] = block.T
        value_s[:, tile_at(b, BLOCK)] = all_ref[slot >> 1, 2 * depth : 3 * depth, half_at(slot)]

    @pl.loop(0, queries // tile)
    def _(t):
        here = tile_at(t, tile)
        result, lse = forward_tiles(
            plan, t, query_s[:, here], range_ref[0:1, here], range_ref[1:2, here],
            lambda j: key_s[tile_at(j, tile), :], lambda j: value_s[:, tile_at(j, tile)],
            tile, depth,
        )
        exact_ref[:, here] = result
        lse_ref[0:1, here] = lse

    @pl.loop(0, queries // BLOCK)
    def _(b):
        slot = query_slot[b]
        out_ref[slot >> 1, :, half_at(slot)] = exact_ref[:, tile_at(b, BLOCK)].astype(low)


def self_backward_kernel(
    tile, plan, query_slot, key_slot, range_ref, own_ref, all_ref, grad_ref, exact_ref, lse_ref,
    dq_ref, dkv_ref, query_s, grad_s, key_s, keyt_s, value_s, dq_s, dk_s, dv_s,
):
    depth, queries = query_s.shape
    count = keyt_s.shape[1]

    @pl.loop(0, queries // BLOCK)
    def _(b):
        slot = query_slot[b]
        query_s[:, tile_at(b, BLOCK)] = own_ref[slot >> 1, 0:depth, half_at(slot)] * low(score_scale)
        grad_s[:, tile_at(b, BLOCK)] = grad_ref[slot >> 1, :, half_at(slot)]

    @pl.loop(0, count // BLOCK)
    def _(b):
        slot = key_slot[b]
        block = all_ref[slot >> 1, depth : 2 * depth, half_at(slot)]
        keyt_s[:, tile_at(b, BLOCK)] = block
        key_s[tile_at(b, BLOCK), :] = block.T
        value_s[tile_at(b, BLOCK), :] = all_ref[slot >> 1, 2 * depth : 3 * depth, half_at(slot)].T

    dk_s[...] = jnp.zeros_like(dk_s)
    dv_s[...] = jnp.zeros_like(dv_s)

    @pl.loop(0, queries // tile)
    def _(t):
        here = tile_at(t, tile)
        query, grad = query_s[:, here], grad_s[:, here]
        start, stop = range_ref[0:1, here], range_ref[1:2, here]
        lse = lse_ref[0:1, here]
        delta = jnp.sum(grad.astype(full) * exact_ref[:, here], axis=0, keepdims=True)

        def step(j, dq, masked):
            there = tile_at(j, tile)
            scores = contract(key_s[there, :], query, 1, 0)
            if masked:
                scores = masked_scores(scores, j, tile, start, stop)
            probs = jnp.exp(scores - lse)
            dprobs = contract(value_s[there, :], grad, 1, 0)
            dscores = (probs * (dprobs - delta)).astype(low)
            dv_s[:, there] += contract(grad, probs.astype(low), 1, 1)
            dk_s[:, there] += contract(query, dscores, 1, 1)
            return dq + contract(keyt_s[:, there], dscores, 1, 0)

        dq_s[:, here] = over_tiles(plan, t, step, jnp.zeros((depth, tile), full))

    @pl.loop(0, queries // BLOCK)
    def _(b):
        slot = query_slot[b]
        dq_ref[slot >> 1, :, half_at(slot)] = (dq_s[:, tile_at(b, BLOCK)] * score_scale).astype(low)

    @pl.loop(0, count // BLOCK)
    def _(b):
        slot = key_slot[b]
        dkv_ref[slot >> 1, 0:depth, half_at(slot)] = dk_s[:, tile_at(b, BLOCK)].astype(dkv_ref.dtype)
        dkv_ref[slot >> 1, depth : 2 * depth, half_at(slot)] = dv_s[:, tile_at(b, BLOCK)].astype(dkv_ref.dtype)


def one_head(values, head, depth):
    rows = lax.broadcasted_iota(jnp.int32, values.shape, 0)
    inside = (rows >= head * depth) & (rows < (head + 1) * depth)
    return jnp.where(inside, values, jnp.zeros_like(values))


def cross_forward_kernel(
    tile, plan, range_ref, query_ref, key_ref, value_ref, out_ref, exact_ref, lse_ref, value_s
):
    count = value_s.shape[1]
    depth = value_s.shape[0] // 2

    @pl.loop(0, count // BLOCK)
    def _(b):
        value_s[:, tile_at(b, BLOCK)] = value_ref[tile_at(b, BLOCK), :].T

    query = query_ref[...] * low(score_scale)
    for head in range(2):
        rows = pl.ds(head * depth, depth)
        result, lse = forward_tiles(
            plan, 0, one_head(query, head, depth), range_ref[0:1, :], range_ref[1:2, :],
            lambda j: key_ref[tile_at(j, tile), :],
            lambda j, rows=rows: value_s[rows, tile_at(j, tile)],
            tile, depth,
        )
        exact_ref[rows, :] = result
        out_ref[rows, :] = result.astype(low)
        lse_ref[0, head : head + 1, :] = lse


def cross_backward_kernel(
    tile, plan, range_ref, query_ref, key_ref, value_ref, grad_ref, exact_ref, lse_ref,
    dq_ref, dkv_ref, keyt_s, dk_s, dv_s,
):
    count = keyt_s.shape[1]
    depth = keyt_s.shape[0] // 2
    width = query_ref.shape[1]

    @pl.loop(0, count // BLOCK)
    def _(b):
        keyt_s[:, tile_at(b, BLOCK)] = key_ref[tile_at(b, BLOCK), :].T

    dk_s[...] = jnp.zeros_like(dk_s)
    dv_s[...] = jnp.zeros_like(dv_s)
    start, stop = range_ref[0:1, :], range_ref[1:2, :]
    all_query = query_ref[...] * low(score_scale)
    for head in range(2):
        rows = pl.ds(head * depth, depth)
        query = one_head(all_query, head, depth)
        grad = one_head(grad_ref[...], head, depth)
        lse = lse_ref[0, head : head + 1, :]
        delta = jnp.sum(grad_ref[rows, :].astype(full) * exact_ref[rows, :], axis=0, keepdims=True)

        def step(j, dq, masked, rows=rows, query=query, grad=grad, lse=lse, delta=delta):
            there = tile_at(j, tile)
            scores = contract(key_ref[there, :], query, 1, 0)
            if masked:
                scores = masked_scores(scores, j, tile, start, stop)
            probs = jnp.exp(scores - lse)
            dprobs = contract(value_ref[there, :], grad, 1, 0)
            dscores = (probs * (dprobs - delta)).astype(low)
            dv_s[there, :] += contract(probs.astype(low), grad, 1, 1)
            dk_s[there, :] += contract(dscores, query, 1, 1)
            return dq + contract(keyt_s[rows, there], dscores, 1, 0)

        dq = over_tiles(plan, 0, step, jnp.zeros((depth, width), full))
        dq_ref[rows, :] = (dq * score_scale).astype(low)
    parts, _, part_rows, _ = dkv_ref.shape
    dkv_ref[:, 0] = dk_s[...].astype(low).reshape(parts, part_rows, 2 * depth)
    dkv_ref[:, 1] = dv_s[...].astype(low).reshape(parts, part_rows, 2 * depth)


def smem():
    return pl.BlockSpec(memory_space=pltpu.SMEM)


def vmem():
    return pl.BlockSpec(memory_space=pltpu.VMEM)


def params():
    return pltpu.CompilerParams(vmem_limit_bytes=VMEM_BYTES)


def self_tile(queries):
    return min(512, queries)


def self_forward(plan, query_slot, key_slot, ranges, own, everyone):
    heads, three, rows = own.shape
    depth = three // 3
    queries, count = heads * rows, everyone.shape[0] * rows
    tile = self_tile(queries)
    return pl.pallas_call(
        functools.partial(self_forward_kernel, tile),
        out_shape=(
            jax.ShapeDtypeStruct((heads, depth, rows), low),
            jax.ShapeDtypeStruct((depth, queries), full),
            jax.ShapeDtypeStruct((8, queries), full),
        ),
        in_specs=[smem()] * 3 + [vmem()] * 3,
        out_specs=(vmem(),) * 3,
        scratch_shapes=[
            pltpu.VMEM((depth, queries), low),
            pltpu.VMEM((count, depth), low),
            pltpu.VMEM((depth, count), low),
        ],
        compiler_params=params(),
        cost_estimate=pl.CostEstimate(
            flops=queries * count * 400, bytes_accessed=queries * 3000, transcendentals=0
        ),
        name="self_forward",
    )(plan, query_slot, key_slot, ranges, own, everyone)


def self_backward(plan, query_slot, key_slot, ranges, own, everyone, grad, exact, lse, kv_type):
    heads, three, rows = own.shape
    depth = three // 3
    queries, count = heads * rows, everyone.shape[0] * rows
    tile = self_tile(queries)
    return pl.pallas_call(
        functools.partial(self_backward_kernel, tile),
        out_shape=(
            jax.ShapeDtypeStruct((heads, depth, rows), low),
            jax.ShapeDtypeStruct((everyone.shape[0], 2 * depth, rows), kv_type),
        ),
        in_specs=[smem()] * 3 + [vmem()] * 6,
        out_specs=(vmem(),) * 2,
        scratch_shapes=[
            pltpu.VMEM((depth, queries), low),
            pltpu.VMEM((depth, queries), low),
            pltpu.VMEM((count, depth), low),
            pltpu.VMEM((depth, count), low),
            pltpu.VMEM((count, depth), low),
            pltpu.VMEM((depth, queries), full),
            pltpu.VMEM((depth, count), full),
            pltpu.VMEM((depth, count), full),
        ],
        compiler_params=params(),
        cost_estimate=pl.CostEstimate(
            flops=queries * count * 1000, bytes_accessed=queries * 6000, transcendentals=0
        ),
        name="self_backward",
    )(plan, query_slot, key_slot, ranges, own, everyone, grad, exact, lse)


def cross_tile(count):
    return min(512, count)


def pair_spec(rows, cols):
    return pl.BlockSpec((rows, cols), lambda i: (i, 0))


def cross_forward(plan, ranges, query, keys_values):
    width, rows = query.shape
    count = keys_values.shape[0]
    pairs = H // 2
    wide = width // pairs
    return pl.pallas_call(
        functools.partial(cross_forward_kernel, cross_tile(count)),
        grid=(pairs,),
        out_shape=(
            jax.ShapeDtypeStruct((width, rows), low),
            jax.ShapeDtypeStruct((width, rows), full),
            jax.ShapeDtypeStruct((pairs, 8, rows), full),
        ),
        in_specs=[
            smem(),
            vmem(),
            pair_spec(wide, rows),
            pl.BlockSpec((count, wide), lambda i: (0, i)),
            pl.BlockSpec((count, wide), lambda i: (0, pairs + i)),
        ],
        out_specs=(
            pair_spec(wide, rows),
            pair_spec(wide, rows),
            pl.BlockSpec((1, 8, rows), lambda i: (i, 0, 0)),
        ),
        scratch_shapes=[pltpu.VMEM((wide, count), low)],
        compiler_params=params(),
        cost_estimate=pl.CostEstimate(
            flops=rows * count * width * 8, bytes_accessed=count * width * 4, transcendentals=0
        ),
        name="cross_forward",
    )(plan, ranges, query, keys_values, keys_values)


def cross_backward(plan, ranges, query, keys_values, grad, exact, lse, parts):
    width, rows = query.shape
    count = keys_values.shape[0]
    pairs = H // 2
    wide = width // pairs
    return pl.pallas_call(
        functools.partial(cross_backward_kernel, cross_tile(count)),
        grid=(pairs,),
        out_shape=(
            jax.ShapeDtypeStruct((width, rows), low),
            jax.ShapeDtypeStruct((parts, 2, count // parts, width), low),
        ),
        in_specs=[
            smem(),
            vmem(),
            pair_spec(wide, rows),
            pl.BlockSpec((count, wide), lambda i: (0, i)),
            pl.BlockSpec((count, wide), lambda i: (0, pairs + i)),
            pair_spec(wide, rows),
            pair_spec(wide, rows),
            pl.BlockSpec((1, 8, rows), lambda i: (i, 0, 0)),
        ],
        out_specs=(
            pair_spec(wide, rows),
            pl.BlockSpec((parts, 2, count // parts, wide), lambda i: (0, 0, 0, i)),
        ),
        scratch_shapes=[
            pltpu.VMEM((wide, count), low),
            pltpu.VMEM((count, wide), full),
            pltpu.VMEM((count, wide), full),
        ],
        compiler_params=params(),
        cost_estimate=pl.CostEstimate(
            flops=rows * count * width * 20, bytes_accessed=count * width * 8, transcendentals=0
        ),
        name="cross_backward",
    )(plan, ranges, query, keys_values, keys_values, grad, exact, lse)


class Exchange:
    def __init__(self):
        self.fsdp = lax.axis_size("fsdp")
        self.chips = lax.axis_size(CHIP)
        self.core = lax.axis_index("core")
        self.row = lax.axis_index("fsdp")
        self.chip = lax.axis_index(CHIP)
        self.paired = self.fsdp == 2
        self.cube = self.paired and self.chips == 8

    def swap(self, value, axis):
        return lax.ppermute(value, axis, [(0, 1), (1, 0)])

    def swap_chip(self, value, bit):
        return lax.ppermute(value, CHIP, [(i, i ^ bit) for i in range(self.chips)])

    def gather_weight(self, shard):
        piece = shard.shape[0] // 2
        mine = lax.dynamic_slice_in_dim(shard, self.core * piece, piece, 0)
        return lax.all_gather(mine, ("fsdp", "core"), axis=0, tiled=True)

    def gather_last(self, shard):
        if not self.paired:
            return lax.all_gather(shard, "fsdp", axis=shard.ndim - 1, tiled=True)
        other = self.swap(shard, "fsdp")
        return jnp.where(
            self.row == 0,
            jnp.concatenate([shard, other], axis=-1),
            jnp.concatenate([other, shard], axis=-1),
        )

    def up_slice(self, shard):
        rows, hidden = shard.shape
        wide = hidden // (2 * self.fsdp)
        if not self.paired:
            split = shard.reshape(rows, self.fsdp, 2, wide)
            mine = lax.dynamic_index_in_dim(split, self.core, 2, keepdims=False)
            return lax.all_to_all(mine, "fsdp", 1, 0, tiled=True).reshape(rows * self.fsdp, wide)
        sent = lax.dynamic_slice_in_dim(shard, (2 * (1 - self.row) + self.core) * wide, wide, 1)
        kept = lax.dynamic_slice_in_dim(shard, (2 * self.row + self.core) * wide, wide, 1)
        other = self.swap(sent, "fsdp")
        whole = jnp.concatenate([kept, kept], axis=0)
        return lax.dynamic_update_slice_in_dim(whole, other, (1 - self.row) * rows, 0)

    def quad_gather(self, value):
        if not self.paired:
            return lax.all_gather(value, QUAD, axis=0, tiled=True)
        across = self.swap(value, "fsdp")
        beside = self.swap(value, "core")
        corner = self.swap(across, "core")
        return jnp.concatenate([value, beside, across, corner], axis=0)

    def quad_sum(self, value):
        if not self.paired:
            return lax.psum_scatter(value, QUAD, scatter_dimension=0, tiled=True).astype(full)
        rows = value.shape[0] // 4
        parts = value.reshape(2, 2, rows, value.shape[1])
        theirs = self.swap(parts[:, 1], "core")
        both = parts[:, 0].astype(full) + theirs.astype(full)
        return both[0] + self.swap(both[1].astype(low), "fsdp").astype(full)

    def halve(self, value, axis, bit, swap):
        kept = lax.dynamic_index_in_dim(value, bit, axis, keepdims=False)
        sent = lax.dynamic_index_in_dim(value, 1 - bit, axis, keepdims=False)
        return kept.astype(full) + swap(sent).astype(full)

    def chip_sum(self, value):
        if not self.cube:
            return lax.psum_scatter(value, CHIP, scatter_dimension=0, tiled=True).astype(full)
        rows = value.shape[0] // 8
        value = value.reshape((2, 2, 2, rows) + value.shape[1:])
        value = self.halve(value, 2, self.chip & 1, lambda v: self.swap_chip(v, 1)).astype(low)
        value = self.halve(value, 1, (self.chip >> 1) & 1, lambda v: self.swap_chip(v, 2)).astype(low)
        return self.halve(value, 0, self.chip >> 2, lambda v: self.swap_chip(v, 4))

    def device_sum(self, values):
        count = len(values)
        rows, cols = values[0].shape
        share = rows // (self.chips * 2 * self.fsdp)
        shape = (self.chips, 2, self.fsdp, share, cols)
        if not self.cube:
            stacked = jnp.stack([v.reshape(shape) for v in values], axis=3)
            stacked = lax.psum_scatter(stacked, "core", scatter_dimension=1, tiled=True)
            stacked = lax.psum_scatter(stacked, "fsdp", scatter_dimension=2, tiled=True)
            stacked = lax.psum_scatter(stacked, CHIP, scatter_dimension=0, tiled=True)
            return [stacked[0, 0, 0, i].astype(full) for i in range(count)]
        halves = [
            self.halve(v.reshape(shape), 1, self.core, lambda u: self.swap(u, "core")).astype(low)
            for v in values
        ]
        stacked = jnp.stack(halves, axis=2)
        stacked = self.halve(stacked, 1, self.row, lambda u: self.swap(u, "fsdp")).astype(low)
        summed = self.chip_sum(stacked)[0]
        return [summed[i] for i in range(count)]

    def to_owner(self, value):
        chips, fsdp = self.chips, self.fsdp
        moves = []
        for chip in range(chips):
            for core in range(2):
                for row in range(fsdp):
                    moves.append(
                        ((chip * 2 + core) * fsdp + row, (row * 2 + core) * chips + chip)
                    )
        return lax.ppermute(value, ALL, moves)

    def quad_columns(self, value):
        quad = 2 * self.fsdp
        rows, wide = value.shape
        share = rows // quad
        if not self.paired:
            value = lax.all_to_all(value, QUAD, 0, 1, tiled=True)
            value = value.reshape(share, 2, self.fsdp, wide).transpose(0, 2, 1, 3)
            return value.reshape(share, quad * wide)
        value = value.reshape(2, 2, share, wide)
        core, row = self.core, self.row

        def block(c, f):
            part = lax.dynamic_index_in_dim(value, c, 0, keepdims=False)
            return lax.dynamic_index_in_dim(part, f, 0, keepdims=False)

        got = [
            block(core, row),
            self.swap(block(1 - core, row), "core"),
            self.swap(block(core, 1 - row), "fsdp"),
            lax.ppermute(block(1 - core, 1 - row), QUAD, [(i, 3 - i) for i in range(4)]),
        ]
        got = [jnp.where(core == 0, got[i], got[i ^ 1]) for i in range(4)]
        got = [jnp.where(row == 0, got[i], got[i ^ 2]) for i in range(4)]
        return jnp.concatenate(got, axis=1)


def per_device(
    tokens, encoder, cotangent, seq_lengths, source_lengths, pair_order, pair_flip,
    ln_gain, ln_bias, attn_bias, self_qkv, self_out, cross_q, cross_kv, cross_out,
    w_up, up_bias, w_down, down_bias,
):
    move = Exchange()
    resid = tokens[0].astype(full)
    source = encoder[0]
    grad_low = cotangent[0]
    rows, width = resid.shape
    src_rows = source.shape[0]
    depth = width // H
    ctx_count = lax.axis_size(CTX)
    parts = lax.axis_size("part")
    devices = ctx_count * move.fsdp
    here = lax.axis_index(CTX)
    part = lax.axis_index("part")

    blocks = block_numbers(pair_order[0], pair_flip[0])
    lengths, src_lengths = seq_lengths[0], source_lengths[0]
    offsets = jnp.arange(BLOCK, dtype=jnp.int32)
    part_blocks = lax.dynamic_slice_in_dim(blocks, part * (blocks.shape[0] // parts), blocks.shape[0] // parts)
    query_slot, key_slot = sorted_slots(part_blocks), sorted_slots(blocks)
    query_places = (jnp.sort(part_blocks) if parts > 1 else jnp.arange(part_blocks.shape[0], dtype=jnp.int32))
    query_places = (query_places[:, None] * BLOCK + offsets[None, :]).reshape(-1)
    self_start = document_starts(query_places, lengths)
    self_stop = query_places + 1
    tile = self_tile(query_places.shape[0])
    self_plan = tile_plan(self_start, self_stop, tile, tile)
    self_ranges = jnp.stack([self_start, self_stop])
    my_blocks = lax.dynamic_slice_in_dim(blocks, here * (rows // BLOCK), rows // BLOCK)
    my_places = (my_blocks[:, None] * BLOCK + offsets[None, :]).reshape(-1)
    cross_start, cross_stop = source_range(my_places, lengths, src_lengths)
    cross_plan = tile_plan(cross_start, cross_stop, rows, cross_tile(src_rows * ctx_count))
    cross_ranges = jnp.stack([cross_start, cross_stop])

    small = jnp.concatenate(
        [ln_gain, ln_bias, attn_bias.reshape(6, -1), down_bias[None]], axis=0
    )
    small = move.gather_last(small).astype(full)
    gains, shifts, biases, bias_down = small[0:3], small[3:6], small[6:12].reshape(2, 3, width), small[12]
    w_qkv = move.gather_weight(self_qkv)
    w_ckv = move.gather_weight(cross_kv)
    w_out = move.gather_weight(self_out)
    w_cq = move.gather_weight(cross_q)
    w_cout = move.gather_weight(cross_out)
    w_upper = move.up_slice(w_up)
    wide = w_upper.shape[1]
    w_lower = lax.dynamic_slice_in_dim(w_down, move.core * wide, wide, 0)
    bias_up = lax.dynamic_slice_in_dim(up_bias, move.core * wide, wide, 0).astype(full)

    norm_one, back_one = jax.vjp(layer_norm, resid, gains[0], shifts[0])
    normed_one = norm_one.astype(low)
    projected = contract(w_qkv, normed_one, 0, 1)
    shift_qkv = jnp.concatenate([biases[0, 0], jnp.zeros((width,), full), biases[0, 1]])
    projected = (projected + shift_qkv[:, None]).astype(low)
    projected = projected.reshape(3, H, depth, rows).transpose(1, 0, 2, 3).reshape(H, 3 * depth, rows)
    own_heads = lax.all_to_all(projected, HEADS, 0, 0, tiled=True)
    all_heads = own_heads if parts == 1 else lax.all_gather(own_heads, "part", axis=0, tiled=True)
    self_args = (self_plan, query_slot, key_slot, self_ranges, own_heads, all_heads)
    self_low, self_exact, self_lse = self_forward(*self_args)
    self_att = lax.all_to_all(self_low, HEADS, 0, 0, tiled=True).reshape(width, rows)
    mixed_one = resid + contract(self_att, w_out, 0, 0) + biases[0, 2]

    src_proj = jnp.dot(source, w_ckv, preferred_element_type=full)
    shift_ckv = jnp.concatenate([jnp.zeros((width,), full), biases[1, 1]])
    src_kv = lax.all_gather((src_proj + shift_ckv).astype(low), CTX, axis=0, tiled=True)

    norm_two, back_two = jax.vjp(layer_norm, mixed_one, gains[1], shifts[1])
    normed_two = norm_two.astype(low)
    cross_query = (contract(w_cq, normed_two, 0, 1) + biases[1, 0][:, None]).astype(low)
    cross_att, cross_exact, cross_lse = cross_forward(cross_plan, cross_ranges, cross_query, src_kv)
    mixed_two = mixed_one + contract(cross_att, w_cout, 0, 0) + biases[1, 2]

    norm_three, back_three = jax.vjp(layer_norm, mixed_two, gains[2], shifts[2])
    grad_quad = move.quad_gather(grad_low)
    quad_three = move.quad_gather(norm_three.astype(low))
    hidden_pre = jnp.dot(quad_three, w_upper, preferred_element_type=full) + bias_up
    activated, back_gelu = jax.vjp(gelu_tanh, hidden_pre)
    act_low = activated.astype(low)
    branch = jnp.dot(act_low, w_lower, preferred_element_type=full).astype(low)
    result = mixed_two + move.quad_sum(branch) + bias_down

    grad_out = grad_low.astype(full)
    grad_b_lower = column_sums(grad_low)
    grad_w_lower = contract(act_low, grad_quad, 0, 0).astype(low)
    lower_own = move.to_owner(move.chip_sum(grad_w_lower).astype(low)).astype(full)
    grad_act = contract(grad_quad, w_lower, 1, 1)
    grad_hidden = back_gelu(grad_act)[0].astype(low)
    grad_b_upper = column_sums(grad_hidden)
    grad_three = move.quad_sum(contract(grad_hidden, w_upper, 1, 1).astype(low))
    grad_w_upper = contract(quad_three, grad_hidden, 0, 0).astype(low)
    upper_own = move.quad_columns(move.chip_sum(grad_w_upper).astype(low)).astype(full)
    grad_ln_three, gain_three, shift_three = back_three(grad_three)
    grad_two = grad_out + grad_ln_three

    grad_two_low = grad_two.astype(low)
    grad_b_cout = column_sums(grad_two_low)
    grad_cross_att = contract(w_cout, grad_two_low, 1, 1).astype(low)
    grad_w_cout = contract(cross_att, grad_two_low, 1, 0).astype(low)
    grad_cq, cross_dkv = cross_backward(
        cross_plan, cross_ranges, cross_query, src_kv, grad_cross_att, cross_exact, cross_lse, ctx_count
    )
    own_dkv = lax.psum_scatter(cross_dkv, CTX, scatter_dimension=0, tiled=True)[0]
    grad_source = contract(own_dkv[0], w_ckv[:, :width], 1, 1) + contract(own_dkv[1], w_ckv[:, width:], 1, 1)
    grad_b_cv = column_sums(own_dkv[1])
    grad_b_cq = jnp.sum(grad_cq.astype(full), axis=1)
    grad_w_cq = contract(normed_two, grad_cq, 0, 1).astype(low)
    grad_ln_two, gain_two, shift_two = back_two(contract(grad_cq, w_cq, 0, 1))
    grad_one = grad_two + grad_ln_two

    grad_one_low = grad_one.astype(low)
    grad_b_out = column_sums(grad_one_low)
    grad_self_att = contract(w_out, grad_one_low, 1, 1).astype(low).reshape(H, depth, rows)
    grad_heads = lax.all_to_all(grad_self_att, HEADS, 0, 0, tiled=True)
    grad_w_out = contract(self_att, grad_one_low, 1, 0).astype(low)
    cout_own, cq_own, out_own = move.device_sum([grad_w_cout, grad_w_cq, grad_w_out])
    head_dq, head_dkv = self_backward(
        *self_args, grad_heads, self_exact, self_lse, low if parts == 1 else full
    )
    if parts > 1:
        head_dkv = lax.psum_scatter(head_dkv, "part", scatter_dimension=0, tiled=True).astype(low)
    head_grad = jnp.concatenate([head_dq, head_dkv], axis=1)
    grad_qkv = lax.all_to_all(head_grad, HEADS, 0, 0, tiled=True)
    grad_qkv = grad_qkv.reshape(H, 3, depth, rows).transpose(1, 0, 2, 3).reshape(3 * width, rows)
    sums = jnp.sum(grad_qkv.astype(full), axis=1).reshape(3, width)
    grad_ln_one, gain_one, shift_one = back_one(contract(grad_qkv, w_qkv, 0, 1))
    grad_input = grad_one + grad_ln_one

    group_one = lax.all_gather(normed_one, HEADS, axis=0, tiled=True)
    group_source = lax.all_gather(source, HEADS, axis=0, tiled=True)
    head_rows = head_grad.transpose(1, 0, 2).reshape(3 * depth, H * rows)
    head_w = contract(group_one, head_rows, 0, 1)
    pieces = own_dkv.reshape(2, src_rows, H, depth).transpose(2, 1, 0, 3).reshape(H, src_rows, 2 * depth)
    pieces = lax.all_to_all(pieces, HEADS, 0, 0, tiled=True).reshape(H * src_rows, 2 * depth)
    head_c = contract(group_source, pieces, 0, 0)
    head_all = jnp.concatenate([head_w, head_c], axis=1).astype(low)
    cols = head_all.shape[1]
    share = width // devices

    vectors = jnp.stack(
        [gain_one, gain_two, gain_three, shift_one, shift_two, shift_three,
         sums[0], sums[2], grad_b_out, grad_b_cq, grad_b_cv, grad_b_cout, grad_b_lower]
    )
    vectors = vectors.reshape(13, devices, share).transpose(1, 0, 2).reshape(devices, 13 * share)
    hidden = wide * 2 * move.fsdp
    upper_sums = lax.dynamic_update_slice_in_dim(
        jnp.zeros((hidden,), full), grad_b_upper, (move.row * 2 + move.core) * wide, 0
    ).reshape(devices, hidden // devices)
    vectors = jnp.concatenate([vectors, upper_sums], axis=1)
    used = vectors.shape[1]
    extra = -(-used // cols)
    vectors = jnp.pad(vectors, ((0, 0), (0, extra * cols - used))).reshape(devices, extra, cols)
    outgoing = jnp.concatenate([head_all.reshape(devices, share, cols), vectors.astype(low)], axis=1)
    incoming = lax.all_to_all(outgoing, ALL, 0, 0, tiled=True)
    heads_in = incoming[:, :share].reshape(parts, H, move.fsdp, share, cols)
    heads_in = jnp.sum(heads_in.astype(full), axis=(0, 2))
    qkv_own = heads_in[:, :, : 3 * depth].reshape(H, share, 3, depth).transpose(1, 2, 0, 3).reshape(share, 3 * width)
    ckv_own = heads_in[:, :, 3 * depth :].reshape(H, share, 2, depth).transpose(1, 2, 0, 3).reshape(share, 2 * width)
    tail = jnp.sum(incoming[:, share:].astype(full), axis=0).reshape(-1)
    vec = tail[: 13 * share].reshape(13, share)
    bup_own = tail[13 * share : used]
    return (
        result.astype(low)[None],
        grad_input[None],
        grad_source[None],
        vec[0:3],
        vec[3:6],
        vec[6:12].reshape(2, 3, share),
        qkv_own,
        out_own,
        cq_own,
        ckv_own,
        cout_own,
        upper_own,
        bup_own,
        lower_own,
        vec[12],
    )


def solution(mesh):
    ctx, fsdp = mesh.shape["ctx"], mesh.shape["fsdp"]
    inner = Mesh(mesh.devices.reshape(ctx // H, H // 2, 2, fsdp), ALL)
    tokens = P("fsdp", CTX, None)
    group = P("fsdp", None)
    owned = P(ALL, None)
    return jax.shard_map(
        per_device,
        mesh=inner,
        in_specs=(tokens,) * 3
        + (group,) * 4
        + (P(None, "fsdp"), P(None, "fsdp"), P(None, None, "fsdp"))
        + (group,) * 6
        + (P("fsdp"), group, P("fsdp")),
        out_specs=(tokens,) * 3
        + (P(None, ALL), P(None, ALL), P(None, None, ALL))
        + (owned,) * 6
        + (P(ALL), owned, P(ALL)),
        check_vma=False,
    )
```

```python
import functools

import jax
import jax.numpy as jnp
from jax import lax
from jax.experimental import pallas as pl
from jax.experimental.pallas import tpu as pltpu
from jax.sharding import Mesh
from jax.sharding import PartitionSpec as P

H = 16
BLOCK = 128

CHIP = ("part", "hc")
HEADS = ("hc", "core")
CTX = ("part", "hc", "core")
QUAD = ("core", "fsdp")
ALL = ("part", "hc", "core", "fsdp")

ln_eps = 1e-05
score_scale = 0.125
low = jnp.bfloat16
full = jnp.float32
SELF_TILES = (512, 512)
SELF_CHAINS = 1
CROSS_TILE = 1024
VMEM_BYTES = 56 * 1024 * 1024


def layer_norm(v, gain, shift):
    centred = v - jnp.mean(v, axis=-1, keepdims=True)
    spread = jnp.mean(centred * centred, axis=-1, keepdims=True)
    return centred * lax.rsqrt(spread + ln_eps) * gain + shift


def gelu_tanh(v):
    return 0.5 * v * (1.0 + jnp.tanh(0.7978845608028654 * (v + 0.044715 * v * v * v)))


def contract(left, right, left_dim, right_dim):
    return lax.dot_general(
        left, right, (((left_dim,), (right_dim,)), ((), ())), preferred_element_type=full
    )


def column_sums(values):
    return jnp.sum(values.astype(full), axis=0)


def plan_kernel(
    query_tile, self_key_tile, cross_key_tile, group_key_tile, cross_rows,
    order, flip, lengths, source_lengths, where,
    query_slot, key_slot, self_plan, cross_plan, group_plan, self_ranges, cross_ranges, group_ranges,
    block_of,
):
    pairs, documents = order.shape[0], lengths.shape[0]
    here, part = where[0], where[1]
    ends, source_ends = [], []
    for d in range(documents):
        ends.append(lengths[d] + (ends[-1] if d else 0))
        source_ends.append(source_lengths[d] + (source_ends[-1] if d else 0))

    def start_of(places):
        start = jnp.zeros_like(places)
        for end in ends:
            start = jnp.where(places >= end, end, start)
        return start

    def source_of(places):
        start, stop = jnp.zeros_like(places), jnp.zeros_like(places) + source_ends[0]
        for d in range(documents - 1):
            start = jnp.where(places >= ends[d], source_ends[d], start)
            stop = jnp.where(places >= ends[d], source_ends[d + 1], stop)
        return start, stop

    def stored(i):
        number = order[i >> 1]
        upper = (flip[i >> 1] + i) & 1 == 1
        return jnp.where(upper, 2 * pairs - 1 - number, number)

    @pl.loop(0, 2 * pairs)
    def _(i):
        key_slot[stored(i)] = i

    blocks = query_slot.shape[0]
    lanes = lax.broadcasted_iota(jnp.int32, (1, BLOCK), 1)

    def take(b, count):
        slot = key_slot[b] - part * blocks
        inside = (slot >= 0) & (slot < blocks)

        @pl.when(inside)
        def _():
            query_slot[count] = slot
            block_of[count] = b
            places = lanes + b * BLOCK
            self_ranges[0:1, tile_at(count, BLOCK)] = start_of(places)
            self_ranges[1:2, tile_at(count, BLOCK)] = places + 1
            start, stop = source_of(places)
            group_ranges[0:1, tile_at(count, BLOCK)] = start
            group_ranges[1:2, tile_at(count, BLOCK)] = stop

        return count + jnp.where(inside, 1, 0)

    lax.fori_loop(0, 2 * pairs, take, jnp.int32(0))

    def write(plan, t, low_start, high_start, low_stop, high_stop, key_tile):
        first = lax.div(low_start, key_tile)
        last = lax.div(high_stop + key_tile - 1, key_tile)
        inner = jnp.clip(lax.div(high_start + key_tile - 1, key_tile), first, last)
        plan[0, t] = first
        plan[1, t] = inner
        plan[2, t] = jnp.clip(lax.div(low_stop, key_tile), inner, last)
        plan[3, t] = last

    step = query_tile // BLOCK

    @pl.loop(0, blocks // step)
    def _(t):
        begin = block_of[t * step] * BLOCK
        end = block_of[t * step + step - 1] * BLOCK + BLOCK - 1
        write(self_plan, t, start_of(begin), start_of(end), begin + 1, end + 1, self_key_tile)
        first, last = source_of(begin), source_of(end)
        write(group_plan, t, first[0], last[0], first[1], last[1], group_key_tile)

    edges = []
    for k in range(cross_rows // BLOCK):
        begin = stored(here * (cross_rows // BLOCK) + k) * BLOCK
        low_edge, high_edge = source_of(begin), source_of(begin + BLOCK - 1)
        if k:
            edges = [
                jnp.minimum(edges[0], low_edge[0]), jnp.maximum(edges[1], high_edge[0]),
                jnp.minimum(edges[2], low_edge[1]), jnp.maximum(edges[3], high_edge[1]),
            ]
        else:
            edges = [low_edge[0], high_edge[0], low_edge[1], high_edge[1]]
        start, stop = source_of(lanes + begin)
        cross_ranges[0:1, k * BLOCK : (k + 1) * BLOCK] = start
        cross_ranges[1:2, k * BLOCK : (k + 1) * BLOCK] = stop
    write(cross_plan, 0, *edges, cross_key_tile)


def attention_plan(order, flip, lengths, source_lengths, here, part, parts, rows, sources):
    blocks = 2 * order.shape[0]
    mine = blocks // parts
    query_tile, key_tile = self_tiles(mine * BLOCK)
    group_key_tile = cross_tiles(mine * BLOCK, sources)[1]
    tiles = mine * BLOCK // query_tile
    shapes = ((mine,), (blocks,), (4, tiles), (4, 1), (4, tiles), (2, mine * BLOCK), (2, rows), (2, mine * BLOCK))
    return pl.pallas_call(
        functools.partial(plan_kernel, query_tile, key_tile, cross_tile(sources), group_key_tile, rows),
        out_shape=tuple(jax.ShapeDtypeStruct(shape, jnp.int32) for shape in shapes),
        in_specs=[smem()] * 5,
        out_specs=(smem(),) * 5 + (vmem(),) * 3,
        scratch_shapes=[pltpu.SMEM((mine,), jnp.int32)],
        compiler_params=params(),
        name="attention_plan",
    )(order, flip, lengths, source_lengths, jnp.stack([here, part]).astype(jnp.int32))


def over_tiles(plan, tile_number, step, carry):
    first, inner = plan[0, tile_number], plan[1, tile_number]
    outer, last = plan[2, tile_number], plan[3, tile_number]
    carry = lax.fori_loop(inner, outer, functools.partial(step, masked=False), carry)
    before = inner - first

    def edge(index, state):
        number = jnp.where(index < before, first + index, outer + index - before)
        return step(number, state, masked=True)

    return lax.fori_loop(0, before + last - outer, edge, carry)


def masked_scores(scores, number, tile, start, stop):
    keys = number * tile + lax.broadcasted_iota(jnp.int32, scores.shape, 0)
    return jnp.where((keys >= start) & (keys < stop), scores, -jnp.inf)


def forward_tiles(plan, number, queries, start, stop, keys_of, values_of, tile, depth):
    chains = range(len(queries))
    width = queries[0].shape[1]
    start, stop = as_list(start, len(queries)), as_list(stop, len(queries))

    def step(j, carry, masked):
        top, total, accum = carry
        scores = [contract(keys_of(j), queries[i], 1, 0) for i in chains]
        if masked:
            scores = [masked_scores(scores[i], j, tile, start[i], stop[i]) for i in chains]
        newtop = [jnp.maximum(top[i], jnp.max(scores[i], axis=0, keepdims=True)) for i in chains]
        weights = [jnp.exp(scores[i] - newtop[i]) for i in chains]
        factor = [jnp.exp(top[i] - newtop[i]) for i in chains]
        total = [total[i] * factor[i] + jnp.sum(weights[i], axis=0, keepdims=True) for i in chains]
        accum = [
            accum[i] * factor[i] + contract(values_of(j, i), weights[i].astype(low), 1, 0)
            for i in chains
        ]
        return newtop, total, accum

    carry = (
        [jnp.full((1, width), -1e30, full) for _ in chains],
        [jnp.zeros((1, width), full) for _ in chains],
        [jnp.zeros((depth, width), full) for _ in chains],
    )
    top, total, accum = over_tiles(plan, number, step, carry)
    return [accum[i] / total[i] for i in chains], [top[i] + jnp.log(total[i]) for i in chains]


def as_list(value, count):
    return value if isinstance(value, list) else [value] * count


def identity(size):
    rows = lax.broadcasted_iota(jnp.int32, (size, size), 0)
    cols = lax.broadcasted_iota(jnp.int32, (size, size), 1)
    return jnp.where(rows == cols, 1.0, 0.0).astype(low)


def flipped(eye, block):
    return contract(eye, block, 1, 1).astype(low)


def tile_at(number, size):
    return pl.ds(pl.multiple_of(number * size, size), size)


def half_at(slot):
    return pl.ds(pl.multiple_of((slot & 1) * BLOCK, BLOCK), BLOCK)


def self_forward_kernel(
    tiles, plan, query_slot, key_slot, range_ref, own_ref, all_ref,
    out_ref, exact_ref, lse_ref, query_s, key_s, value_s,
):
    query_tile, tile = tiles
    depth, queries = query_s.shape
    count = value_s.shape[1]

    @pl.loop(0, queries // BLOCK)
    def _(b):
        slot = query_slot[b]
        query_s[:, tile_at(b, BLOCK)] = own_ref[slot >> 1, 0:depth, half_at(slot)] * low(score_scale)

    @pl.loop(0, count // BLOCK)
    def _(b):
        slot = key_slot[b]
        block = all_ref[slot >> 1, depth : 2 * depth, half_at(slot)]
        key_s[tile_at(b, BLOCK), :] = block.T
        value_s[:, tile_at(b, BLOCK)] = all_ref[slot >> 1, 2 * depth : 3 * depth, half_at(slot)]

    chains = SELF_CHAINS
    lanes = query_tile // chains

    @pl.loop(0, queries // query_tile)
    def _(t):
        here = [pl.ds(pl.multiple_of(t * query_tile + i * lanes, lanes), lanes) for i in range(chains)]
        result, lse = forward_tiles(
            plan, t, [query_s[:, at] for at in here], [range_ref[0:1, at] for at in here],
            [range_ref[1:2, at] for at in here],
            lambda j: key_s[tile_at(j, tile), :], lambda j, i: value_s[:, tile_at(j, tile)],
            tile, depth,
        )
        for i in range(chains):
            exact_ref[:, here[i]] = result[i]
            lse_ref[0:1, here[i]] = lse[i]

    @pl.loop(0, queries // BLOCK)
    def _(b):
        slot = query_slot[b]
        out_ref[slot >> 1, :, half_at(slot)] = exact_ref[:, tile_at(b, BLOCK)].astype(low)


def self_backward_kernel(
    tiles, plan, query_slot, key_slot, range_ref, own_ref, all_ref, grad_ref, exact_ref, lse_ref,
    dq_ref, dkv_ref, rows_ref, query_s, grad_s, key_s, keyt_s, value_s, dq_s, dk_s, dv_s,
):
    query_tile, tile = tiles
    depth, queries = query_s.shape
    count = keyt_s.shape[1]

    @pl.loop(0, queries // BLOCK)
    def _(b):
        slot = query_slot[b]
        query_s[:, tile_at(b, BLOCK)] = own_ref[slot >> 1, 0:depth, half_at(slot)] * low(score_scale)
        grad_s[:, tile_at(b, BLOCK)] = grad_ref[slot >> 1, :, half_at(slot)]

    @pl.loop(0, count // BLOCK)
    def _(b):
        slot = key_slot[b]
        block = all_ref[slot >> 1, depth : 2 * depth, half_at(slot)]
        keyt_s[:, tile_at(b, BLOCK)] = block
        key_s[tile_at(b, BLOCK), :] = block.T
        value_s[tile_at(b, BLOCK), :] = all_ref[slot >> 1, 2 * depth : 3 * depth, half_at(slot)].T

    dk_s[...] = jnp.zeros_like(dk_s)
    dv_s[...] = jnp.zeros_like(dv_s)

    @pl.loop(0, queries // query_tile)
    def _(t):
        here = tile_at(t, query_tile)
        query, grad = query_s[:, here], grad_s[:, here]
        start, stop = range_ref[0:1, here], range_ref[1:2, here]
        lse = lse_ref[0:1, here]
        delta = jnp.sum(grad.astype(full) * exact_ref[:, here], axis=0, keepdims=True)

        def step(j, dq, masked):
            there = tile_at(j, tile)
            scores = contract(key_s[there, :], query, 1, 0)
            if masked:
                scores = masked_scores(scores, j, tile, start, stop)
            probs = jnp.exp(scores - lse)
            dprobs = contract(value_s[there, :], grad, 1, 0)
            dscores = (probs * (dprobs - delta)).astype(low)
            dv_s[:, there] += contract(grad, probs.astype(low), 1, 1)
            dk_s[:, there] += contract(query, dscores, 1, 1)
            return dq + contract(keyt_s[:, there], dscores, 1, 0)

        dq_s[:, here] = over_tiles(plan, t, step, jnp.zeros((depth, query_tile), full))

    @pl.loop(0, queries // BLOCK)
    def _(b):
        slot = query_slot[b]
        dq = (dq_s[:, tile_at(b, BLOCK)] * score_scale).astype(low)
        dq_ref[slot >> 1, :, half_at(slot)] = dq
        rows_ref[0:depth, tile_at(slot, BLOCK)] = dq

    @pl.loop(0, count // BLOCK)
    def _(b):
        slot = key_slot[b]
        dk = dk_s[:, tile_at(b, BLOCK)].astype(dkv_ref.dtype)
        dv = dv_s[:, tile_at(b, BLOCK)].astype(dkv_ref.dtype)
        dkv_ref[slot >> 1, 0:depth, half_at(slot)] = dk
        dkv_ref[slot >> 1, depth : 2 * depth, half_at(slot)] = dv
        if count == queries:
            rows_ref[depth : 2 * depth, tile_at(slot, BLOCK)] = dk.astype(low)
            rows_ref[2 * depth : 3 * depth, tile_at(slot, BLOCK)] = dv.astype(low)


def one_head(values, head, depth):
    rows = lax.broadcasted_iota(jnp.int32, values.shape, 0)
    inside = (rows >= head * depth) & (rows < (head + 1) * depth)
    return jnp.where(inside, values, jnp.zeros_like(values))


def cross_forward_kernel(
    tile, plan, range_ref, query_ref, key_ref, value_ref, out_ref, exact_ref, lse_ref, value_s
):
    depth = value_s.shape[0] // 2

    eye = identity(2 * depth)

    def turn(j, _):
        value_s[:, tile_at(j, tile)] = flipped(eye, value_ref[tile_at(j, tile), :])
        return 0

    lax.fori_loop(plan[0, 0], plan[3, 0], turn, 0)
    query = query_ref[...] * low(score_scale)
    rows = [pl.ds(head * depth, depth) for head in range(2)]
    result, lse = forward_tiles(
        plan, 0, [one_head(query, head, depth) for head in range(2)],
        range_ref[0:1, :], range_ref[1:2, :],
        lambda j: key_ref[tile_at(j, tile), :],
        lambda j, i: value_s[rows[i], tile_at(j, tile)],
        tile, depth,
    )
    for head in range(2):
        exact_ref[rows[head], :] = result[head]
        out_ref[rows[head], :] = result[head].astype(low)
        lse_ref[0, head : head + 1, :] = lse[head]


def cross_backward_kernel(
    tiles, plan, query_slot, range_ref, query_ref, keys_values_ref, grad_ref, exact_ref,
    dq_ref, dkv_ref, query_s, grad_s, exact_s, keyt_s, dkv_s,
):
    query_tile, tile = tiles
    depth = query_ref.shape[1]
    queries = query_s.shape[1]
    eye = identity(2 * depth)

    @pl.loop(0, queries // BLOCK)
    def _(b):
        slot = query_slot[b]
        at, there = tile_at(b, BLOCK), half_at(slot)
        query_s[:, at] = query_ref[slot >> 1, :, there] * low(score_scale)
        grad_s[:, at] = grad_ref[slot >> 1, :, there]
        exact_s[:, at] = exact_ref[slot >> 1, :, there]

    @pl.loop(0, keyt_s.shape[1] // tile)
    def _(j):
        at = tile_at(j, tile)
        keyt_s[:, at] = flipped(eye, keys_values_ref[at, :])[0:depth]

    dkv_s[...] = jnp.zeros_like(dkv_s)
    blank = jnp.zeros((depth, query_tile), low)

    @pl.loop(0, queries // query_tile)
    def _(t):
        here = tile_at(t, query_tile)
        grad = grad_s[:, here]
        start, stop = range_ref[0:1, here], range_ref[1:2, here]
        lse = exact_s[depth : depth + 1, here]
        delta = jnp.sum(grad.astype(full) * exact_s[0:depth, here], axis=0, keepdims=True)
        wide_query = jnp.concatenate([query_s[:, here], blank], axis=0)
        wide_grad = jnp.concatenate([blank, grad], axis=0)
        sides = jnp.concatenate([wide_query, wide_grad], axis=1)

        def step(j, dq, masked):
            there = tile_at(j, tile)
            keys_values = keys_values_ref[there, :]
            scores = contract(keys_values, wide_query, 1, 0)
            if masked:
                scores = masked_scores(scores, j, tile, start, stop)
            probs = jnp.exp(scores - lse)
            dprobs = contract(keys_values, wide_grad, 1, 0)
            dscores = (probs * (dprobs - delta)).astype(low)
            both = jnp.concatenate([dscores, probs.astype(low)], axis=1)
            dkv_s[there, :] += contract(both, sides, 1, 1)
            return dq + contract(keyt_s[:, there], dscores, 1, 0)

        dq = over_tiles(plan, t, step, jnp.zeros((depth, query_tile), full))
        query_s[:, here] = (dq * score_scale).astype(low)

    @pl.loop(0, queries // BLOCK)
    def _(b):
        slot = query_slot[b]
        dq_ref[slot >> 1, :, half_at(slot)] = query_s[:, tile_at(b, BLOCK)]

    dkv_ref[...] = dkv_s[...].astype(dkv_ref.dtype)


def smem():
    return pl.BlockSpec(memory_space=pltpu.SMEM)


def vmem():
    return pl.BlockSpec(memory_space=pltpu.VMEM)


def params():
    return pltpu.CompilerParams(vmem_limit_bytes=VMEM_BYTES)


def self_tiles(queries):
    return min(SELF_TILES[0], queries), min(SELF_TILES[1], queries)


def self_forward(plan, query_slot, key_slot, ranges, own, everyone):
    heads, three, rows = own.shape
    depth = three // 3
    queries, count = heads * rows, everyone.shape[0] * rows
    tile = self_tiles(queries)
    return pl.pallas_call(
        functools.partial(self_forward_kernel, tile),
        out_shape=(
            jax.ShapeDtypeStruct((heads, depth, rows), low),
            jax.ShapeDtypeStruct((depth, queries), full),
            jax.ShapeDtypeStruct((8, queries), full),
        ),
        in_specs=[smem()] * 3 + [vmem()] * 3,
        out_specs=(vmem(),) * 3,
        scratch_shapes=[
            pltpu.VMEM((depth, queries), low),
            pltpu.VMEM((count, depth), low),
            pltpu.VMEM((depth, count), low),
        ],
        compiler_params=params(),
        cost_estimate=pl.CostEstimate(flops=1, bytes_accessed=1, transcendentals=0),
        name="self_forward",
    )(plan, query_slot, key_slot, ranges, own, everyone)


def self_backward(plan, query_slot, key_slot, ranges, own, everyone, grad, exact, lse, kv_type):
    heads, three, rows = own.shape
    depth = three // 3
    queries, count = heads * rows, everyone.shape[0] * rows
    tile = self_tiles(queries)
    return pl.pallas_call(
        functools.partial(self_backward_kernel, tile),
        out_shape=(
            jax.ShapeDtypeStruct((heads, depth, rows), low),
            jax.ShapeDtypeStruct((everyone.shape[0], 2 * depth, rows), kv_type),
            jax.ShapeDtypeStruct((3 * depth, queries), low),
        ),
        in_specs=[smem()] * 3 + [vmem()] * 6,
        out_specs=(vmem(),) * 3,
        scratch_shapes=[
            pltpu.VMEM((depth, queries), low),
            pltpu.VMEM((depth, queries), low),
            pltpu.VMEM((count, depth), low),
            pltpu.VMEM((depth, count), low),
            pltpu.VMEM((count, depth), low),
            pltpu.VMEM((depth, queries), full),
            pltpu.VMEM((depth, count), full),
            pltpu.VMEM((depth, count), full),
        ],
        compiler_params=params(),
        cost_estimate=pl.CostEstimate(flops=1, bytes_accessed=1, transcendentals=0),
        name="self_backward",
    )(plan, query_slot, key_slot, ranges, own, everyone, grad, exact, lse)


def cross_tiles(queries, count):
    return min(512, queries), min(512, count)


def cross_tile(count):
    return min(CROSS_TILE, count)


def pair_spec(rows, cols):
    return pl.BlockSpec((rows, cols), lambda i: (i, 0))


def cross_forward(plan, ranges, query, keys_values):
    width, rows = query.shape
    count = keys_values.shape[0]
    pairs = H // 2
    wide = width // pairs
    return pl.pallas_call(
        functools.partial(cross_forward_kernel, cross_tile(count)),
        grid=(pairs,),
        out_shape=(
            jax.ShapeDtypeStruct((width, rows), low),
            jax.ShapeDtypeStruct((width, rows), full),
            jax.ShapeDtypeStruct((pairs, 8, rows), full),
        ),
        in_specs=[
            smem(),
            vmem(),
            pair_spec(wide, rows),
            pl.BlockSpec((count, wide), lambda i: (0, i)),
            pl.BlockSpec((count, wide), lambda i: (0, pairs + i)),
        ],
        out_specs=(
            pair_spec(wide, rows),
            pair_spec(wide, rows),
            pl.BlockSpec((1, 8, rows), lambda i: (i, 0, 0)),
        ),
        scratch_shapes=[pltpu.VMEM((wide, count), low)],
        compiler_params=params(),
        cost_estimate=pl.CostEstimate(flops=1, bytes_accessed=1, transcendentals=0),
        name="cross_forward",
    )(plan, ranges, query, keys_values, keys_values)


def cross_backward(plan, query_slot, ranges, query, keys_values, grad, exact, kv_type):
    heads, depth, rows = query.shape
    queries, count = heads * rows, keys_values.shape[0]
    return pl.pallas_call(
        functools.partial(cross_backward_kernel, cross_tiles(queries, count)),
        out_shape=(
            jax.ShapeDtypeStruct((heads, depth, rows), low),
            jax.ShapeDtypeStruct((count, 2 * depth), kv_type),
        ),
        in_specs=[smem()] * 2 + [vmem()] * 5,
        out_specs=(vmem(),) * 2,
        scratch_shapes=[
            pltpu.VMEM((depth, queries), low),
            pltpu.VMEM((depth, queries), low),
            pltpu.VMEM((exact.shape[1], queries), full),
            pltpu.VMEM((depth, count), low),
            pltpu.VMEM((count, 2 * depth), full),
        ],
        compiler_params=params(),
        cost_estimate=pl.CostEstimate(flops=1, bytes_accessed=1, transcendentals=0),
        name="cross_backward",
    )(plan, query_slot, ranges, query, keys_values, grad, exact)


def copy_kernel(_, value_ref, out_ref):
    out_ref[...] = value_ref[...]


def strided_columns(value, first, step, wide):
    rows, cols = value.shape
    count = cols // (step * wide)
    return pl.pallas_call(
        copy_kernel,
        out_shape=jax.ShapeDtypeStruct((rows, count * wide), value.dtype),
        grid_spec=pltpu.PrefetchScalarGridSpec(
            num_scalar_prefetch=1,
            grid=(count,),
            in_specs=[pl.BlockSpec((rows, wide), lambda i, at: (0, i * step + at[0]))],
            out_specs=pl.BlockSpec((rows, wide), lambda i, at: (0, i)),
        ),
        compiler_params=params(),
        name="strided_columns",
    )(first.astype(jnp.int32).reshape(1), value)


def owned_kernel(depth, pieces_ref, qkv_ref, ckv_ref):
    _, heads, groups, share, _ = pieces_ref.shape
    width = heads * depth
    for head in range(heads):
        total = 0.0
        for p in range(pieces_ref.shape[0]):
            for g in range(groups):
                total = total + pieces_ref[p, head, g].astype(full)
        at = head * depth
        for i in range(3):
            qkv_ref[:, i * width + at : i * width + at + depth] = total[:, i * depth : (i + 1) * depth]
        for i in range(2):
            ckv_ref[:, i * width + at : i * width + at + depth] = total[:, (3 + i) * depth : (4 + i) * depth]


def owned_columns(pieces, depth):
    _, heads, _, share, _ = pieces.shape
    width = heads * depth
    return pl.pallas_call(
        functools.partial(owned_kernel, depth),
        out_shape=(
            jax.ShapeDtypeStruct((share, 3 * width), full),
            jax.ShapeDtypeStruct((share, 2 * width), full),
        ),
        in_specs=[vmem()],
        out_specs=(vmem(),) * 2,
        compiler_params=params(),
        name="owned_columns",
    )(pieces)


def after(value, *others):
    return lax.optimization_barrier((value,) + others)[0]


class Exchange:
    def __init__(self):
        self.fsdp = lax.axis_size("fsdp")
        self.chips = lax.axis_size(CHIP)
        self.core = lax.axis_index("core")
        self.row = lax.axis_index("fsdp")
        self.chip = lax.axis_index(CHIP)
        self.paired = self.fsdp == 2
        self.cube = self.paired and self.chips == 8
        self.near, self.far = (self.chip >> 1) & 1, self.chip >> 2
        self.corner = 2 * (self.chip & 1) + self.core

    def swap(self, value, axis):
        return lax.ppermute(value, axis, [(0, 1), (1, 0)])

    def swap_chip(self, value, bit):
        return lax.ppermute(value, CHIP, [(i, i ^ bit) for i in range(self.chips)])

    def own_piece(self, shard):
        piece = shard.shape[0] // 2
        return lax.dynamic_slice_in_dim(shard, self.core * piece, piece, 0)

    def fetch(self, mine, begin=()):
        if not self.paired:
            return lax.all_gather(mine, ("fsdp", "core"), axis=0, tiled=True)
        return self.swap(after(mine, *begin) if begin else mine, "fsdp")

    def place(self, base, across, hold=()):
        if not self.paired:
            return across
        piece = across.shape[0]
        held = after(across, *hold) if hold else across
        corner = self.swap(held, "core")
        start = (1 - self.row) * 2 * piece
        whole = lax.dynamic_update_slice_in_dim(base, held, start + self.core * piece, 0)
        return lax.dynamic_update_slice_in_dim(whole, corner, start + (1 - self.core) * piece, 0)

    def gather_last(self, shard):
        if not self.paired:
            return lax.all_gather(shard, "fsdp", axis=shard.ndim - 1, tiled=True)
        other = self.swap(shard, "fsdp")
        return jnp.where(
            self.row == 0,
            jnp.concatenate([shard, other], axis=-1),
            jnp.concatenate([other, shard], axis=-1),
        )


    def hidden_parts(self, shard, axis):
        size = shard.shape[axis]
        if not self.cube:
            wide = size // 2
            return lax.dynamic_slice_in_dim(shard, self.core * wide, wide, axis)
        wide = size // 8
        parts = [
            lax.dynamic_slice_in_dim(shard, (4 * z + self.corner) * wide, wide, axis) for z in range(2)
        ]
        return jnp.concatenate(parts, axis=axis)

    def up_part(self, shard):
        rows, hidden = shard.shape
        if self.cube:
            return strided_columns(shard, self.corner, 4, hidden // 16)
        split = shard.reshape(rows, self.fsdp, 2, hidden // (2 * self.fsdp))
        return lax.dynamic_index_in_dim(split, self.core, 2, keepdims=False)

    def trade(self, mine, begin):
        half = mine.shape[0] // 2
        return [
            self.swap(after(mine[i * half : (i + 1) * half], *begin[i]), "fsdp") for i in range(2)
        ]

    def joined(self, base, theirs, hold):
        half = theirs[0].shape[0]
        start = (1 - self.row) * 2 * half
        for i in range(2):
            base = lax.dynamic_update_slice_in_dim(base, after(theirs[i], *hold[i]), start + i * half, 0)
        return base

    def swap_beside(self, value):
        return self.swap_chip(value, 1) if self.cube else self.swap(value, "fsdp")

    def quad_gather(self, value, hold=()):
        if not self.paired:
            return lax.all_gather(value, QUAD, axis=0, tiled=True), ()
        across = self.swap_beside(value)
        held = after(across, *hold)
        beside = self.swap(value, "core")
        corner = self.swap(held, "core")
        return jnp.concatenate([value, beside, held, corner], axis=0), (across,)

    def quad_sum(self, value):
        if not self.paired:
            total = lax.psum_scatter(value, QUAD, scatter_dimension=0, tiled=True)
            return total.astype(full), total
        rows = value.shape[0] // 4
        parts = value.reshape(2, 2, rows, value.shape[1])
        theirs = self.swap(parts[:, 1], "core")
        both = parts[:, 0].astype(full) + theirs.astype(full)
        got = self.swap_beside(both[1].astype(low))
        return (both[0], got), theirs

    def quad_end(self, pending, hold=()):
        if not self.paired:
            return pending
        mine, got = pending
        return (after(mine, *hold) if hold else mine) + got.astype(full)

    def send_half(self, value, axis, bit, swap, *others):
        if others:
            value = after(value, *others)
        sent = lax.dynamic_index_in_dim(value, 1 - bit, axis, keepdims=False)
        kept = lax.dynamic_index_in_dim(value, bit, axis, keepdims=False)
        return sent, (kept, swap(sent))

    def add(self, halves, *others):
        kept, got = halves
        if others:
            kept = after(kept, *others)
        return kept.astype(full) + got.astype(full)

    def chip_step(self, value, number, *others):
        bit = (self.chip >> number) & 1
        return self.send_half(value, 2 - number, bit, lambda v: self.swap_chip(v, 1 << number), *others)

    def chip_shape(self, value):
        return value.reshape((2, 2, 2, value.shape[0] // 8) + value.shape[1:])

    def chip_scatter(self, value):
        return lax.psum_scatter(value, CHIP, scatter_dimension=0, tiled=True).astype(full)

    def device_shape(self, value):
        rows, cols = value.shape
        return value.reshape(self.chips, 2, self.fsdp, rows // (self.chips * 2 * self.fsdp), cols)

    def device_scatter(self, values):
        stacked = jnp.stack([self.device_shape(v) for v in values], axis=3)
        stacked = lax.psum_scatter(stacked, "core", scatter_dimension=1, tiled=True)
        stacked = lax.psum_scatter(stacked, "fsdp", scatter_dimension=2, tiled=True)
        stacked = lax.psum_scatter(stacked, CHIP, scatter_dimension=0, tiled=True)
        return [stacked[0, 0, 0, i].astype(full) for i in range(len(values))]

    def to_owner(self, value):
        chips, fsdp = self.chips, self.fsdp
        moves = []
        for chip in range(chips):
            for core in range(2):
                for row in range(fsdp):
                    moves.append(
                        ((chip * 2 + core) * fsdp + row, (row * 2 + core) * chips + chip)
                    )
        return lax.ppermute(value, ALL, moves)

    def quad_columns(self, value):
        quad = 2 * self.fsdp
        rows, wide = value.shape
        share = rows // quad
        value = lax.all_to_all(value, QUAD, 0, 1, tiled=True)
        value = value.reshape(share, 2, self.fsdp, wide).transpose(0, 2, 1, 3)
        return value.reshape(share, quad * wide)

    def corner_columns(self, value):
        _, share, wide = value.shape

        def block(bits):
            return lax.dynamic_index_in_dim(value, self.corner ^ bits, 0, keepdims=False)

        got = [
            block(0),
            self.swap(block(1), "core"),
            self.swap_chip(block(2), 1),
            lax.ppermute(block(3), CTX, [(i, i ^ 3) for i in range(2 * self.chips)]),
        ]
        got = [jnp.where(self.core == 0, got[i], got[i ^ 1]) for i in range(4)]
        got = [jnp.where(self.chip & 1 == 0, got[i], got[i ^ 2]) for i in range(4)]
        got = [piece.astype(full) for piece in got]
        step = wide // 4
        return jnp.concatenate(
            [got[i][:, z * step : (z + 1) * step] for z in range(4) for i in range(4)], axis=1
        )

    def hidden_vector(self, value, hidden):
        devices = self.chips * 2 * self.fsdp
        if not self.cube:
            spread = jnp.zeros((hidden,), full)
            at = (self.row * 2 + self.core) * value.shape[0]
            return lax.dynamic_update_slice_in_dim(spread, value, at, 0).reshape(devices, -1)
        spread = jnp.zeros((4, 4, hidden // 16), full)
        spread = lax.dynamic_update_slice_in_dim(spread, value.reshape(4, 1, -1), self.corner, 1)
        return spread.reshape(devices, -1)


def per_device(
    tokens, encoder, cotangent, seq_lengths, source_lengths, pair_order, pair_flip,
    ln_gain, ln_bias, attn_bias, self_qkv, self_out, cross_q, cross_kv, cross_out,
    w_up, up_bias, w_down, down_bias,
):
    move = Exchange()
    resid = tokens[0].astype(full)
    source = encoder[0]
    grad_low = cotangent[0]
    rows, width = resid.shape
    src_rows = source.shape[0]
    depth = width // H
    ctx_count = lax.axis_size(CTX)
    parts = lax.axis_size("part")
    devices = ctx_count * move.fsdp
    here = lax.axis_index(CTX)
    part = lax.axis_index("part")

    plan = attention_plan(
        pair_order[0], pair_flip[0], seq_lengths[0], source_lengths[0],
        here, part, parts, rows, src_rows * ctx_count,
    )
    query_slot, key_slot, self_plan, cross_plan, group_plan, self_ranges, cross_ranges, group_ranges = plan

    small = [ln_gain, ln_bias, attn_bias.reshape(6, -1), down_bias[None]]
    bias_up = move.hidden_parts(up_bias, 0)
    if move.cube:
        small.append(bias_up.reshape(2, -1))
    small = move.gather_last(jnp.concatenate(small, axis=0)).astype(full)
    if move.cube:
        half = small.shape[1] // 2
        bias_up = jnp.concatenate([small[13, :half], small[14, :half], small[13, half:], small[14, half:]])
    bias_up = bias_up.astype(full)
    gains, shifts, biases, bias_down = small[0:3], small[3:6], small[6:12].reshape(2, 3, width), small[12]
    shards = (cross_kv, self_qkv, self_out, cross_q, cross_out)
    ckv_piece, qkv_piece, out_piece, cq_piece, cout_piece = [move.own_piece(w) for w in shards]
    bases = [jnp.concatenate([w, w], axis=0) if move.paired else w for w in shards]
    up_mine = move.up_part(w_up)
    down_mine = move.hidden_parts(w_down, 0)
    up_base = jnp.concatenate([up_mine, up_mine], axis=0)
    down_base = jnp.concatenate([down_mine, down_mine], axis=0)

    got_qkv = move.fetch(qkv_piece)
    group_source = lax.all_gather(source, HEADS, axis=0, tiled=True)

    norm_one, back_one = jax.vjp(layer_norm, resid, gains[0], shifts[0])
    normed_one = norm_one.astype(low)
    w_qkv = move.place(bases[1], got_qkv)
    ready = after(
        normed_one, *plan, bases[1], ckv_piece, out_piece, cq_piece, cout_piece, up_mine
    )
    projected = contract(w_qkv, ready, 0, 1)
    shift_qkv = jnp.concatenate([biases[0, 0], jnp.zeros((width,), full), biases[0, 1]])
    projected = (projected + shift_qkv[:, None]).astype(low)
    projected = projected.reshape(3, H, depth, rows).transpose(1, 0, 2, 3).reshape(H, 3 * depth, rows)
    own_heads = lax.all_to_all(projected, HEADS, 0, 0, tiled=True)

    got_out = move.fetch(out_piece, (got_qkv,))
    got_cq = move.fetch(cq_piece, (got_qkv,))
    got_cout = move.fetch(cout_piece, (own_heads,))
    got_ckv = move.fetch(ckv_piece, (got_qkv,))
    self_in = after(own_heads, got_ckv, bases[0], *bases[2:], up_base, down_base)
    all_heads = self_in if parts == 1 else lax.all_gather(self_in, "part", axis=0, tiled=True)
    self_args = (self_plan, query_slot, key_slot, self_ranges, self_in, all_heads)
    self_low, self_exact, self_lse = self_forward(*self_args)
    grad_quad, got_quad = move.quad_gather(after(grad_low, own_heads), (self_low,))
    out_low = after(self_low, got_out, got_cq, *got_quad)
    self_att = lax.all_to_all(out_low, HEADS, 0, 0, tiled=True).reshape(width, rows)
    w_ckv = move.place(bases[0], got_ckv, (own_heads,))
    w_out = move.place(bases[2], got_out, (self_low,))
    w_cq = move.place(bases[3], got_cq, (self_low,))
    w_cout = move.place(bases[4], got_cout, (self_att,))

    every_source = group_source
    if parts > 1:
        every_source = lax.all_gather(group_source, "part", axis=0, tiled=True)
    shift_ckv = jnp.concatenate([jnp.zeros((width,), full), biases[1, 1]])
    src_kv = (jnp.dot(every_source, w_ckv, preferred_element_type=full) + shift_ckv).astype(low)
    mixed_one = resid + contract(self_att, w_out, 0, 0) + biases[0, 2]

    norm_two, back_two = jax.vjp(layer_norm, mixed_one, gains[1], shifts[1])
    normed_two = norm_two.astype(low)
    cross_query = (contract(w_cq, normed_two, 0, 1) + biases[1, 0][:, None]).astype(low)
    if move.cube:
        got_up = move.trade(up_mine, ((self_low,), (self_att,)))
        cross_query = after(cross_query, got_up[0], got_cout)
    group_one = lax.all_gather(normed_one, HEADS, axis=0, tiled=True)
    cross_att, cross_exact, cross_lse = cross_forward(cross_plan, cross_ranges, cross_query, src_kv)
    mixed_two = mixed_one + contract(cross_att, w_cout, 0, 0) + biases[1, 2]

    head = lax.axis_index(HEADS)
    lse_rows = cross_lse[:, 0:2].reshape(H, 1, rows)
    kept = jnp.concatenate(
        [cross_exact.reshape(H, depth, rows), jnp.broadcast_to(lse_rows, (H, 8, rows))], axis=1
    )
    head_exact = lax.all_to_all(kept, HEADS, 0, 0, tiled=True)
    head_query = lax.all_to_all(cross_query.reshape(H, depth, rows), HEADS, 0, 0, tiled=True)
    head_cols = [
        lax.dynamic_slice_in_dim(w_ckv, i * width + head * depth, depth, 1) for i in range(2)
    ]
    head_shift = jnp.concatenate(
        [jnp.zeros((depth,), full), lax.dynamic_slice_in_dim(biases[1, 1], head * depth, depth, 0)]
    )
    head_kv = jnp.dot(every_source, jnp.concatenate(head_cols, axis=1), preferred_element_type=full)
    head_kv = (head_kv + head_shift).astype(low)

    norm_three, back_three = jax.vjp(layer_norm, mixed_two, gains[2], shifts[2])
    three_low = norm_three.astype(low)
    if move.cube:
        got_down = move.trade(down_mine, ((self_att,), (cross_att,)))
        three_low = after(three_low, got_up[1], got_down[0])
        w_upper = move.joined(up_base, got_up, ((self_att,), (cross_att,)))
    else:
        w_upper = lax.all_to_all(up_mine, "fsdp", 1, 0, tiled=True).reshape(width, -1)
        w_lower = down_mine
    wide = w_upper.shape[1]
    quad_three, _ = move.quad_gather(three_low)
    hidden_pre = jnp.dot(quad_three, w_upper, preferred_element_type=full) + bias_up
    if move.cube:
        w_lower = move.joined(down_base, got_down, ((cross_att,), (cross_att,)))
    activated, back_gelu = jax.vjp(gelu_tanh, hidden_pre)
    act_low = activated.astype(low)
    grad_act = contract(grad_quad, w_lower, 1, 1)
    grad_hidden = back_gelu(grad_act)[0].astype(low)
    grad_three, met = move.quad_sum(contract(grad_hidden, w_upper, 1, 1).astype(low))

    grad_out = grad_low.astype(full)
    grad_b_lower = column_sums(grad_low)
    grad_w_lower = contract(after(act_low, met), grad_quad, 0, 0).astype(low)
    grad_b_upper = column_sums(grad_hidden)
    sent = ()
    if move.cube:
        lower = grad_w_lower.reshape(2, 2, 2, -1, width)
        sent_a, lower = move.send_half(lower, 2, move.row, lambda v: move.swap(v, "fsdp"))
        sent = (sent_a,)
    grad_three = move.quad_end(grad_three, sent)
    grad_ln_three, gain_three, shift_three = back_three(grad_three)
    grad_two = grad_out + grad_ln_three

    grad_two_low = grad_two.astype(low)
    grad_b_cout = column_sums(grad_two_low)
    grad_cross_att = contract(w_cout, grad_two_low, 1, 1).astype(low)
    sent_cross = after(grad_cross_att.reshape(H, depth, rows), *sent) if sent else grad_cross_att.reshape(H, depth, rows)
    grad_head = lax.all_to_all(sent_cross, HEADS, 0, 0, tiled=True)
    grad_w_upper = contract(after(quad_three, grad_cross_att), grad_hidden, 0, 0).astype(low)
    got_lower = lower[1] if move.cube else grad_head
    head_in = after(grad_head, head_exact, head_query, head_kv, grad_w_upper, group_one)
    head_cq, head_dkv_rows = cross_backward(
        group_plan, query_slot, group_ranges, head_query, head_kv, head_in, head_exact,
        low if parts == 1 else full,
    )
    if parts > 1:
        head_dkv_rows = lax.psum_scatter(head_dkv_rows, "part", scatter_dimension=0, tiled=True).astype(low)
    head_cq_sent = after(head_cq, got_lower) if move.cube else head_cq
    grad_cq = lax.all_to_all(head_cq_sent, HEADS, 0, 0, tiled=True).reshape(width, rows)
    branch = jnp.dot(after(act_low, head_cq), w_lower, preferred_element_type=full).astype(low)
    result = mixed_two + move.quad_end(move.quad_sum(branch)[0]) + bias_down
    if move.cube:
        lower = move.add(lower, head_cq).astype(low)
        _, lower = move.send_half(lower, 1, move.near, lambda v: move.swap_chip(v, 2))
        upper = grad_w_upper.reshape(2, 2, 4, 2, -1, wide)
        sent_b, upper = move.send_half(upper, 3, move.row, lambda v: move.swap(v, "fsdp"))
    grad_b_cq = jnp.sum(grad_cq.astype(full), axis=1)
    grad_ln_two, gain_two, shift_two = back_two(contract(grad_cq, w_cq, 0, 1))
    grad_one = grad_two + grad_ln_two

    grad_one_low = grad_one.astype(low)
    grad_b_out = column_sums(grad_one_low)
    grad_self_att = contract(w_out, grad_one_low, 1, 1).astype(low).reshape(H, depth, rows)
    grad_heads = lax.all_to_all(grad_self_att, HEADS, 0, 0, tiled=True)
    grad_w_cout = contract(cross_att, grad_two_low, 1, 0).astype(low)
    grad_w_cq = contract(normed_two, grad_cq, 0, 1).astype(low)
    grad_w_out = contract(self_att, grad_one_low, 1, 0).astype(low)
    if move.cube:
        square = []
        for one in (grad_w_cout, grad_w_cq, grad_w_out):
            _, both = move.send_half(move.device_shape(one), 1, move.core, lambda v: move.swap(v, "core"))
            square.append(move.add(both).astype(low))
        square = jnp.stack(square, axis=1)
        square = square.reshape((2, 2, 2) + square.shape[1:])
        _, square = move.send_half(square, 2, move.chip & 1, lambda v: move.swap_chip(v, 1))
        grad_heads = after(grad_heads, square[0], upper[1])
        upper = move.add(upper, grad_self_att).astype(low)
        _, upper = move.send_half(upper, 1, move.near, lambda v: move.swap_chip(v, 2))
    head_dq, head_dkv, head_rows = self_backward(
        *self_args, grad_heads, self_exact, self_lse, low if parts == 1 else full
    )
    if parts > 1:
        head_dkv = lax.psum_scatter(head_dkv, "part", scatter_dimension=0, tiled=True).astype(low)
    head_grad = jnp.concatenate([head_dq, head_dkv], axis=1)
    if parts > 1:
        head_rows = head_grad.transpose(1, 0, 2).reshape(3 * depth, H * rows)
    if move.cube:
        head_grad = after(head_grad, lower[1], upper[1], square[1])
    grad_qkv = lax.all_to_all(head_grad, HEADS, 0, 0, tiled=True)
    if move.cube:
        lower = move.add(lower, head_rows).astype(low)
        _, lower = move.send_half(lower, 0, move.far, lambda v: move.swap_chip(v, 4))
        upper = move.add(upper, head_rows).astype(low)
        _, upper = move.send_half(upper, 0, move.far, lambda v: move.swap_chip(v, 4))
        square = move.add(square, head_rows).astype(low)
        _, square = move.send_half(square, 1, move.near, lambda v: move.swap_chip(v, 2))
    grad_qkv = grad_qkv.reshape(H, 3, depth, rows).transpose(1, 0, 2, 3).reshape(3 * width, rows)
    sums = jnp.sum(grad_qkv.astype(full), axis=1).reshape(3, width)
    grad_ln_one, gain_one, shift_one = back_one(contract(grad_qkv, w_qkv, 0, 1))
    grad_input = grad_one + grad_ln_one

    head_w = contract(head_rows, group_one, 1, 0).astype(low)
    head_c = contract(group_source, head_dkv_rows, 0, 0).astype(low)
    own_dkv = lax.all_to_all(head_dkv_rows.reshape(H, src_rows, 2 * depth), HEADS, 0, 0, tiled=True)
    own_dk = own_dkv[:, :, :depth].transpose(1, 0, 2).reshape(src_rows, width)
    own_dv = own_dkv[:, :, depth:].transpose(1, 0, 2).reshape(src_rows, width)
    head_all = jnp.concatenate([head_w.T, head_c], axis=1)
    grad_source = contract(jnp.concatenate([own_dk, own_dv], axis=1), w_ckv, 1, 1)
    grad_b_cv = column_sums(own_dv)
    cols = head_all.shape[1]
    share = width // devices

    if move.cube:
        lower_own = move.add(lower, grad_qkv)
        square = move.add(square, grad_qkv).astype(low)
        _, square = move.send_half(square, 0, move.far, lambda v: move.swap_chip(v, 4))
        square = move.add(square).astype(low)
        _, square = move.send_half(square, 1, move.row, lambda v: move.swap(v, "fsdp"))
        cout_own, cq_own, out_own = tuple(move.add(square))
        upper_own = move.corner_columns(move.add(upper, grad_qkv).astype(low))
    else:
        lower_own = move.to_owner(move.chip_scatter(grad_w_lower).astype(low)).astype(full)
        upper_own = move.quad_columns(move.chip_scatter(grad_w_upper).astype(low)).astype(full)
        cout_own, cq_own, out_own = move.device_scatter([grad_w_cout, grad_w_cq, grad_w_out])

    vectors = jnp.stack(
        [gain_one, gain_two, gain_three, shift_one, shift_two, shift_three,
         sums[0], sums[2], grad_b_out, grad_b_cq, grad_b_cv, grad_b_cout, grad_b_lower]
    )
    vectors = vectors.reshape(13, devices, share).transpose(1, 0, 2).reshape(devices, 13 * share)
    hidden = wide * 2 * move.fsdp
    upper_sums = move.hidden_vector(grad_b_upper, hidden)
    vectors = jnp.concatenate([vectors, upper_sums], axis=1)
    used = vectors.shape[1]
    extra = -(-used // cols)
    vectors = jnp.pad(vectors, ((0, 0), (0, extra * cols - used))).reshape(devices, extra, cols)
    outgoing = jnp.concatenate([head_all.reshape(devices, share, cols), vectors.astype(low)], axis=1)
    incoming = lax.all_to_all(outgoing, ALL, 0, 0, tiled=True)
    heads_in = incoming[:, :share].reshape(parts, H, move.fsdp, share, cols)
    qkv_own, ckv_own = owned_columns(heads_in, depth)
    tail = jnp.sum(incoming[:, share:].astype(full), axis=0).reshape(-1)
    vec = tail[: 13 * share].reshape(13, share)
    bup_own = tail[13 * share : used]
    return (
        result.astype(low)[None],
        grad_input[None],
        grad_source[None],
        vec[0:3],
        vec[3:6],
        vec[6:12].reshape(2, 3, share),
        qkv_own,
        out_own,
        cq_own,
        ckv_own,
        cout_own,
        upper_own,
        bup_own,
        lower_own,
        vec[12],
    )


def solution(mesh):
    ctx, fsdp = mesh.shape["ctx"], mesh.shape["fsdp"]
    inner = Mesh(mesh.devices.reshape(ctx // H, H // 2, 2, fsdp), ALL)
    tokens = P("fsdp", CTX, None)
    group = P("fsdp", None)
    owned = P(ALL, None)
    return jax.shard_map(
        per_device,
        mesh=inner,
        in_specs=(tokens,) * 3
        + (group,) * 4
        + (P(None, "fsdp"), P(None, "fsdp"), P(None, None, "fsdp"))
        + (group,) * 6
        + (P("fsdp"), group, P("fsdp")),
        out_specs=(tokens,) * 3
        + (P(None, ALL), P(None, ALL), P(None, None, ALL))
        + (owned,) * 6
        + (P(ALL), owned, P(ALL)),
        check_vma=False,
    )
```

```python
import functools

import jax
import jax.numpy as jnp
from jax import lax
from jax.experimental import pallas as pl
from jax.experimental.pallas import tpu as pltpu
from jax.sharding import Mesh
from jax.sharding import PartitionSpec as P

H = 16
BLOCK = 128

CHIP = ("part", "hc")
HEADS = ("hc", "core")
CTX = ("part", "hc", "core")
QUAD = ("core", "fsdp")
ALL = ("part", "hc", "core", "fsdp")

ln_eps = 1e-05
score_scale = 0.125
low = jnp.bfloat16
full = jnp.float32
SELF_TILES = (512, 512)
SELF_CHAINS = 1
CROSS_TILE = 1024
VMEM_BYTES = 56 * 1024 * 1024


def layer_norm(v, gain, shift):
    centred = v - jnp.mean(v, axis=-1, keepdims=True)
    spread = jnp.mean(centred * centred, axis=-1, keepdims=True)
    return centred * lax.rsqrt(spread + ln_eps) * gain + shift


def gelu_tanh(v):
    return 0.5 * v * (1.0 + jnp.tanh(0.7978845608028654 * (v + 0.044715 * v * v * v)))


def in_thirds(value):
    terms = []
    for _ in range(3):
        term = lax.reduce_precision(value, 8, 7)
        terms.append(term.astype(low))
        value = value - term
    return terms


def contract(left, right, left_dim, right_dim):
    return lax.dot_general(
        left, right, (((left_dim,), (right_dim,)), ((), ())), preferred_element_type=full
    )


def column_sums(values):
    return jnp.sum(values.astype(full), axis=0)


def plan_kernel(
    query_tile, self_key_tile, cross_key_tile, group_key_tile, cross_rows,
    order, flip, lengths, source_lengths, where,
    query_slot, key_slot, self_plan, cross_plan, group_plan, self_ranges, cross_ranges, group_ranges,
    block_of,
):
    pairs, documents = order.shape[0], lengths.shape[0]
    here, part = where[0], where[1]
    ends, source_ends = [], []
    for d in range(documents):
        ends.append(lengths[d] + (ends[-1] if d else 0))
        source_ends.append(source_lengths[d] + (source_ends[-1] if d else 0))

    def start_of(places):
        start = jnp.zeros_like(places)
        for end in ends:
            start = jnp.where(places >= end, end, start)
        return start

    def source_of(places):
        start, stop = jnp.zeros_like(places), jnp.zeros_like(places) + source_ends[0]
        for d in range(documents - 1):
            start = jnp.where(places >= ends[d], source_ends[d], start)
            stop = jnp.where(places >= ends[d], source_ends[d + 1], stop)
        return start, stop

    def stored(i):
        number = order[i >> 1]
        upper = (flip[i >> 1] + i) & 1 == 1
        return jnp.where(upper, 2 * pairs - 1 - number, number)

    @pl.loop(0, 2 * pairs)
    def _(i):
        key_slot[stored(i)] = i

    blocks = query_slot.shape[0]
    lanes = lax.broadcasted_iota(jnp.int32, (1, BLOCK), 1)

    def take(b, count):
        slot = key_slot[b] - part * blocks
        inside = (slot >= 0) & (slot < blocks)

        @pl.when(inside)
        def _():
            query_slot[count] = slot
            block_of[count] = b
            places = lanes + b * BLOCK
            self_ranges[0:1, tile_at(count, BLOCK)] = start_of(places)
            self_ranges[1:2, tile_at(count, BLOCK)] = places + 1
            start, stop = source_of(places)
            group_ranges[0:1, tile_at(count, BLOCK)] = start
            group_ranges[1:2, tile_at(count, BLOCK)] = stop

        return count + jnp.where(inside, 1, 0)

    lax.fori_loop(0, 2 * pairs, take, jnp.int32(0))

    def write(plan, t, low_start, high_start, low_stop, high_stop, key_tile):
        first = lax.div(low_start, key_tile)
        last = lax.div(high_stop + key_tile - 1, key_tile)
        inner = jnp.clip(lax.div(high_start + key_tile - 1, key_tile), first, last)
        plan[0, t] = first
        plan[1, t] = inner
        plan[2, t] = jnp.clip(lax.div(low_stop, key_tile), inner, last)
        plan[3, t] = last

    step = query_tile // BLOCK

    @pl.loop(0, blocks // step)
    def _(t):
        begin = block_of[t * step] * BLOCK
        end = block_of[t * step + step - 1] * BLOCK + BLOCK - 1
        write(self_plan, t, start_of(begin), start_of(end), begin + 1, end + 1, self_key_tile)
        first, last = source_of(begin), source_of(end)
        write(group_plan, t, first[0], last[0], first[1], last[1], group_key_tile)

    edges = []
    for k in range(cross_rows // BLOCK):
        begin = stored(here * (cross_rows // BLOCK) + k) * BLOCK
        low_edge, high_edge = source_of(begin), source_of(begin + BLOCK - 1)
        if k:
            edges = [
                jnp.minimum(edges[0], low_edge[0]), jnp.maximum(edges[1], high_edge[0]),
                jnp.minimum(edges[2], low_edge[1]), jnp.maximum(edges[3], high_edge[1]),
            ]
        else:
            edges = [low_edge[0], high_edge[0], low_edge[1], high_edge[1]]
        start, stop = source_of(lanes + begin)
        cross_ranges[0:1, k * BLOCK : (k + 1) * BLOCK] = start
        cross_ranges[1:2, k * BLOCK : (k + 1) * BLOCK] = stop
    write(cross_plan, 0, *edges, cross_key_tile)


def attention_plan(order, flip, lengths, source_lengths, here, part, parts, rows, sources):
    blocks = 2 * order.shape[0]
    mine = blocks // parts
    query_tile, key_tile = self_tiles(mine * BLOCK)
    group_key_tile = cross_tiles(mine * BLOCK, sources)[1]
    tiles = mine * BLOCK // query_tile
    shapes = ((mine,), (blocks,), (4, tiles), (4, 1), (4, tiles), (2, mine * BLOCK), (2, rows), (2, mine * BLOCK))
    return pl.pallas_call(
        functools.partial(plan_kernel, query_tile, key_tile, cross_tile(sources), group_key_tile, rows),
        out_shape=tuple(jax.ShapeDtypeStruct(shape, jnp.int32) for shape in shapes),
        in_specs=[smem()] * 5,
        out_specs=(smem(),) * 5 + (vmem(),) * 3,
        scratch_shapes=[pltpu.SMEM((mine,), jnp.int32)],
        compiler_params=params(),
        name="attention_plan",
    )(order, flip, lengths, source_lengths, jnp.stack([here, part]).astype(jnp.int32))


def over_tiles(plan, tile_number, step, carry):
    first, inner = plan[0, tile_number], plan[1, tile_number]
    outer, last = plan[2, tile_number], plan[3, tile_number]
    carry = lax.fori_loop(inner, outer, functools.partial(step, masked=False), carry)
    before = inner - first

    def edge(index, state):
        number = jnp.where(index < before, first + index, outer + index - before)
        return step(number, state, masked=True)

    return lax.fori_loop(0, before + last - outer, edge, carry)


def masked_scores(scores, number, tile, start, stop):
    keys = number * tile + lax.broadcasted_iota(jnp.int32, scores.shape, 0)
    return jnp.where((keys >= start) & (keys < stop), scores, -jnp.inf)


def forward_tiles(plan, number, queries, start, stop, keys_of, values_of, tile, depth):
    chains = range(len(queries))
    width = queries[0].shape[1]
    start, stop = as_list(start, len(queries)), as_list(stop, len(queries))

    def step(j, carry, masked):
        top, total, accum = carry
        scores = [contract(keys_of(j), queries[i], 1, 0) for i in chains]
        if masked:
            scores = [masked_scores(scores[i], j, tile, start[i], stop[i]) for i in chains]
        newtop = [jnp.maximum(top[i], jnp.max(scores[i], axis=0, keepdims=True)) for i in chains]
        weights = [jnp.exp(scores[i] - newtop[i]) for i in chains]
        factor = [jnp.exp(top[i] - newtop[i]) for i in chains]
        total = [total[i] * factor[i] + jnp.sum(weights[i], axis=0, keepdims=True) for i in chains]
        accum = [
            accum[i] * factor[i] + contract(values_of(j, i), weights[i].astype(low), 1, 0)
            for i in chains
        ]
        return newtop, total, accum

    carry = (
        [jnp.full((1, width), -1e30, full) for _ in chains],
        [jnp.zeros((1, width), full) for _ in chains],
        [jnp.zeros((depth, width), full) for _ in chains],
    )
    top, total, accum = over_tiles(plan, number, step, carry)
    return [accum[i] / total[i] for i in chains], [top[i] + jnp.log(total[i]) for i in chains]


def as_list(value, count):
    return value if isinstance(value, list) else [value] * count


def identity(size):
    rows = lax.broadcasted_iota(jnp.int32, (size, size), 0)
    cols = lax.broadcasted_iota(jnp.int32, (size, size), 1)
    return jnp.where(rows == cols, 1.0, 0.0).astype(low)


def flipped(eye, block):
    return contract(eye, block, 1, 1).astype(low)


def tile_at(number, size):
    return pl.ds(pl.multiple_of(number * size, size), size)


def half_at(slot):
    return pl.ds(pl.multiple_of((slot & 1) * BLOCK, BLOCK), BLOCK)


def self_forward_kernel(
    tiles, plan, query_slot, key_slot, range_ref, own_ref, all_ref,
    out_ref, exact_ref, lse_ref, query_s, key_s, value_s,
):
    query_tile, tile = tiles
    depth, queries = query_s.shape
    count = value_s.shape[1]

    @pl.loop(0, queries // BLOCK)
    def _(b):
        slot = query_slot[b]
        query_s[:, tile_at(b, BLOCK)] = own_ref[slot >> 1, 0:depth, half_at(slot)] * low(score_scale)

    @pl.loop(0, count // BLOCK)
    def _(b):
        slot = key_slot[b]
        block = all_ref[slot >> 1, depth : 2 * depth, half_at(slot)]
        key_s[tile_at(b, BLOCK), :] = block.T
        value_s[:, tile_at(b, BLOCK)] = all_ref[slot >> 1, 2 * depth : 3 * depth, half_at(slot)]

    chains = SELF_CHAINS
    lanes = query_tile // chains

    @pl.loop(0, queries // query_tile)
    def _(t):
        here = [pl.ds(pl.multiple_of(t * query_tile + i * lanes, lanes), lanes) for i in range(chains)]
        result, lse = forward_tiles(
            plan, t, [query_s[:, at] for at in here], [range_ref[0:1, at] for at in here],
            [range_ref[1:2, at] for at in here],
            lambda j: key_s[tile_at(j, tile), :], lambda j, i: value_s[:, tile_at(j, tile)],
            tile, depth,
        )
        for i in range(chains):
            exact_ref[:, here[i]] = result[i]
            lse_ref[0:1, here[i]] = lse[i]

    @pl.loop(0, queries // BLOCK)
    def _(b):
        slot = query_slot[b]
        out_ref[slot >> 1, :, half_at(slot)] = exact_ref[:, tile_at(b, BLOCK)].astype(low)


def self_backward_kernel(
    tiles, joined, plan, query_slot, key_slot, range_ref, own_ref, all_ref, grad_ref, exact_ref, lse_ref,
    *rest,
):
    if joined:
        carried_ref, dq_ref, *rest = rest
        dkv_ref = dq_ref
        dq_ref[:, dq_ref.shape[1] - carried_ref.shape[1] :, :] = carried_ref[...]
    else:
        dq_ref, dkv_ref, *rest = rest
    rows_ref, query_s, grad_s, key_s, keyt_s, value_s, dq_s, dk_s, dv_s = rest
    query_tile, tile = tiles
    depth, queries = query_s.shape
    count = keyt_s.shape[1]

    @pl.loop(0, queries // BLOCK)
    def _(b):
        slot = query_slot[b]
        query_s[:, tile_at(b, BLOCK)] = own_ref[slot >> 1, 0:depth, half_at(slot)] * low(score_scale)
        grad_s[:, tile_at(b, BLOCK)] = grad_ref[slot >> 1, :, half_at(slot)]

    @pl.loop(0, count // BLOCK)
    def _(b):
        slot = key_slot[b]
        block = all_ref[slot >> 1, depth : 2 * depth, half_at(slot)]
        keyt_s[:, tile_at(b, BLOCK)] = block
        key_s[tile_at(b, BLOCK), :] = block.T
        value_s[tile_at(b, BLOCK), :] = all_ref[slot >> 1, 2 * depth : 3 * depth, half_at(slot)].T

    dk_s[...] = jnp.zeros_like(dk_s)
    dv_s[...] = jnp.zeros_like(dv_s)

    @pl.loop(0, queries // query_tile)
    def _(t):
        here = tile_at(t, query_tile)
        query, grad = query_s[:, here], grad_s[:, here]
        start, stop = range_ref[0:1, here], range_ref[1:2, here]
        lse = lse_ref[0:1, here]
        delta = jnp.sum(grad.astype(full) * exact_ref[:, here], axis=0, keepdims=True)

        def step(j, dq, masked):
            there = tile_at(j, tile)
            scores = contract(key_s[there, :], query, 1, 0)
            if masked:
                scores = masked_scores(scores, j, tile, start, stop)
            probs = jnp.exp(scores - lse)
            dprobs = contract(value_s[there, :], grad, 1, 0)
            dscores = (probs * (dprobs - delta)).astype(low)
            dv_s[:, there] += contract(grad, probs.astype(low), 1, 1)
            dk_s[:, there] += contract(query, dscores, 1, 1)
            return dq + contract(keyt_s[:, there], dscores, 1, 0)

        dq_s[:, here] = over_tiles(plan, t, step, jnp.zeros((depth, query_tile), full))

    @pl.loop(0, queries // BLOCK)
    def _(b):
        slot = query_slot[b]
        dq = (dq_s[:, tile_at(b, BLOCK)] * score_scale).astype(low)
        dq_ref[slot >> 1, 0:depth, half_at(slot)] = dq
        rows_ref[0:depth, tile_at(slot, BLOCK)] = dq

    @pl.loop(0, count // BLOCK)
    def _(b):
        slot = key_slot[b]
        dk = dk_s[:, tile_at(b, BLOCK)].astype(dkv_ref.dtype)
        dv = dv_s[:, tile_at(b, BLOCK)].astype(dkv_ref.dtype)
        at = depth if joined else 0
        dkv_ref[slot >> 1, at : at + depth, half_at(slot)] = dk
        dkv_ref[slot >> 1, at + depth : at + 2 * depth, half_at(slot)] = dv
        if count == queries:
            rows_ref[depth : 2 * depth, tile_at(slot, BLOCK)] = dk.astype(low)
            rows_ref[2 * depth : 3 * depth, tile_at(slot, BLOCK)] = dv.astype(low)


def one_head(values, head, depth):
    rows = lax.broadcasted_iota(jnp.int32, values.shape, 0)
    inside = (rows >= head * depth) & (rows < (head + 1) * depth)
    return jnp.where(inside, values, jnp.zeros_like(values))


def cross_forward_kernel(
    tile, plan, range_ref, query_ref, key_ref, value_ref, out_ref, exact_ref, lse_ref, value_s
):
    depth = value_s.shape[0] // 2

    eye = identity(2 * depth)

    def turn(j, _):
        value_s[:, tile_at(j, tile)] = flipped(eye, value_ref[tile_at(j, tile), :])
        return 0

    lax.fori_loop(plan[0, 0], plan[3, 0], turn, 0)
    query = query_ref[...] * low(score_scale)
    rows = [pl.ds(head * depth, depth) for head in range(2)]
    result, lse = forward_tiles(
        plan, 0, [one_head(query, head, depth) for head in range(2)],
        range_ref[0:1, :], range_ref[1:2, :],
        lambda j: key_ref[tile_at(j, tile), :],
        lambda j, i: value_s[rows[i], tile_at(j, tile)],
        tile, depth,
    )
    for head in range(2):
        exact_ref[rows[head], :] = result[head]
        out_ref[rows[head], :] = result[head].astype(low)
        lse_ref[0, head : head + 1, :] = lse[head]


def cross_backward_kernel(
    tiles, plan, query_slot, range_ref, query_ref, keys_values_ref, grad_ref,
    dq_ref, dkv_ref, packed_ref, query_s, grad_s, keyt_s, dkv_s,
):
    query_tile, tile = tiles
    depth = query_ref.shape[1]
    queries = query_s.shape[1]
    eye = identity(2 * depth)

    @pl.loop(0, queries // BLOCK)
    def _(b):
        slot = query_slot[b]
        at, there = tile_at(b, BLOCK), half_at(slot)
        query_s[:, at] = query_ref[slot >> 1, :, there] * low(score_scale)
        grad_s[:, at] = grad_ref[slot >> 1, :, there]

    @pl.loop(0, keyt_s.shape[1] // tile)
    def _(j):
        at = tile_at(j, tile)
        keyt_s[:, at] = flipped(eye, keys_values_ref[at, :])[0:depth]

    dkv_s[...] = jnp.zeros_like(dkv_s)
    blank = jnp.zeros((depth, query_tile), low)

    @pl.loop(0, queries // query_tile)
    def _(t):
        here = tile_at(t, query_tile)
        grad = grad_s[0:depth, here]
        start, stop = range_ref[0:1, here], range_ref[1:2, here]
        extra = grad_s[depth : depth + 16, here].astype(full)
        lse = extra[0:1] + extra[1:2] + extra[2:3]
        delta = extra[3:4] + extra[4:5] + extra[5:6]
        wide_query = jnp.concatenate([query_s[:, here], blank], axis=0)
        wide_grad = jnp.concatenate([blank, grad], axis=0)
        sides = jnp.concatenate([wide_query, wide_grad], axis=1)

        def step(j, dq, masked):
            there = tile_at(j, tile)
            keys_values = keys_values_ref[there, :]
            scores = contract(keys_values, wide_query, 1, 0)
            if masked:
                scores = masked_scores(scores, j, tile, start, stop)
            probs = jnp.exp(scores - lse)
            dprobs = contract(keys_values, wide_grad, 1, 0)
            dscores = (probs * (dprobs - delta)).astype(low)
            both = jnp.concatenate([dscores, probs.astype(low)], axis=1)
            dkv_s[there, :] += contract(both, sides, 1, 1)
            return dq + contract(keyt_s[:, there], dscores, 1, 0)

        dq = over_tiles(plan, t, step, jnp.zeros((depth, query_tile), full))
        query_s[:, here] = (dq * score_scale).astype(low)

    @pl.loop(0, queries // BLOCK)
    def _(b):
        slot = query_slot[b]
        dq_ref[slot >> 1, :, half_at(slot)] = query_s[:, tile_at(b, BLOCK)]

    total = dkv_s[...].astype(dkv_ref.dtype)
    dkv_ref[...] = total
    devices, half, _ = packed_ref.shape
    total = total.reshape(devices, 2, half, 2 * depth)
    packed_ref[:, :, 0 : 2 * depth] = total[:, 0].astype(low)
    packed_ref[:, :, 2 * depth : 4 * depth] = total[:, 1].astype(low)


def smem():
    return pl.BlockSpec(memory_space=pltpu.SMEM)


def vmem():
    return pl.BlockSpec(memory_space=pltpu.VMEM)


def params():
    return pltpu.CompilerParams(vmem_limit_bytes=VMEM_BYTES)


def self_tiles(queries):
    return min(SELF_TILES[0], queries), min(SELF_TILES[1], queries)


def self_forward(plan, query_slot, key_slot, ranges, own, everyone):
    heads, three, rows = own.shape
    depth = three // 3
    queries, count = heads * rows, everyone.shape[0] * rows
    tile = self_tiles(queries)
    return pl.pallas_call(
        functools.partial(self_forward_kernel, tile),
        out_shape=(
            jax.ShapeDtypeStruct((heads, depth, rows), low),
            jax.ShapeDtypeStruct((depth, queries), full),
            jax.ShapeDtypeStruct((8, queries), full),
        ),
        in_specs=[smem()] * 3 + [vmem()] * 3,
        out_specs=(vmem(),) * 3,
        scratch_shapes=[
            pltpu.VMEM((depth, queries), low),
            pltpu.VMEM((count, depth), low),
            pltpu.VMEM((depth, count), low),
        ],
        compiler_params=params(),
        cost_estimate=pl.CostEstimate(flops=1, bytes_accessed=1, transcendentals=0),
        name="self_forward",
    )(plan, query_slot, key_slot, ranges, own, everyone)


def self_backward(plan, query_slot, key_slot, ranges, own, everyone, grad, exact, lse, kv_type, carried):
    heads, three, rows = own.shape
    depth = three // 3
    queries, count = heads * rows, everyone.shape[0] * rows
    tile = self_tiles(queries)
    joined = heads == everyone.shape[0]
    if joined:
        shapes = (jax.ShapeDtypeStruct((heads, 3 * depth + carried.shape[1], rows), low),)
        extra = (carried,)
    else:
        shapes = (
            jax.ShapeDtypeStruct((heads, depth, rows), low),
            jax.ShapeDtypeStruct((everyone.shape[0], 2 * depth, rows), kv_type),
        )
        extra = ()
    return pl.pallas_call(
        functools.partial(self_backward_kernel, tile, joined),
        out_shape=shapes + (jax.ShapeDtypeStruct((3 * depth, queries), low),),
        in_specs=[smem()] * 3 + [vmem()] * (6 + len(extra)),
        out_specs=(vmem(),) * (len(shapes) + 1),
        scratch_shapes=[
            pltpu.VMEM((depth, queries), low),
            pltpu.VMEM((depth, queries), low),
            pltpu.VMEM((count, depth), low),
            pltpu.VMEM((depth, count), low),
            pltpu.VMEM((count, depth), low),
            pltpu.VMEM((depth, queries), full),
            pltpu.VMEM((depth, count), full),
            pltpu.VMEM((depth, count), full),
        ],
        compiler_params=params(),
        cost_estimate=pl.CostEstimate(flops=1, bytes_accessed=1, transcendentals=0),
        name="self_backward",
    )(plan, query_slot, key_slot, ranges, own, everyone, grad, exact, lse, *extra)


def cross_tiles(queries, count):
    return min(512, queries), min(512, count)


def cross_tile(count):
    return min(CROSS_TILE, count)


def pair_spec(rows, cols):
    return pl.BlockSpec((rows, cols), lambda i: (i, 0))


def cross_forward(plan, ranges, query, keys_values):
    width, rows = query.shape
    count = keys_values.shape[0]
    pairs = H // 2
    wide = width // pairs
    return pl.pallas_call(
        functools.partial(cross_forward_kernel, cross_tile(count)),
        grid=(pairs,),
        out_shape=(
            jax.ShapeDtypeStruct((width, rows), low),
            jax.ShapeDtypeStruct((width, rows), full),
            jax.ShapeDtypeStruct((pairs, 8, rows), full),
        ),
        in_specs=[
            smem(),
            vmem(),
            pair_spec(wide, rows),
            pl.BlockSpec((count, wide), lambda i: (0, i)),
            pl.BlockSpec((count, wide), lambda i: (0, pairs + i)),
        ],
        out_specs=(
            pair_spec(wide, rows),
            pair_spec(wide, rows),
            pl.BlockSpec((1, 8, rows), lambda i: (i, 0, 0)),
        ),
        scratch_shapes=[pltpu.VMEM((wide, count), low)],
        compiler_params=params(),
        cost_estimate=pl.CostEstimate(flops=1, bytes_accessed=1, transcendentals=0),
        name="cross_forward",
    )(plan, ranges, query, keys_values, keys_values)


def cross_backward(plan, query_slot, ranges, query, keys_values, grad, kv_type, parts):
    heads, depth, rows = query.shape
    queries, count = heads * rows, keys_values.shape[0]
    return pl.pallas_call(
        functools.partial(cross_backward_kernel, cross_tiles(queries, count)),
        out_shape=(
            jax.ShapeDtypeStruct((heads, depth, rows), low),
            jax.ShapeDtypeStruct((count, 2 * depth), kv_type),
            jax.ShapeDtypeStruct((parts, count // parts // 2, 4 * depth), low),
        ),
        in_specs=[smem()] * 2 + [vmem()] * 4,
        out_specs=(vmem(),) * 3,
        scratch_shapes=[
            pltpu.VMEM((depth, queries), low),
            pltpu.VMEM((grad.shape[1], queries), low),
            pltpu.VMEM((depth, count), low),
            pltpu.VMEM((count, 2 * depth), full),
        ],
        compiler_params=params(),
        cost_estimate=pl.CostEstimate(flops=1, bytes_accessed=1, transcendentals=0),
        name="cross_backward",
    )(plan, query_slot, ranges, query, keys_values, grad)


def copy_kernel(_, value_ref, square_ref, row_ref):
    square_ref[...] = value_ref[...]
    row_ref[...] = value_ref[...]


def strided_columns(value, first, step, wide):
    rows, cols = value.shape
    count = cols // (step * wide)
    return pl.pallas_call(
        copy_kernel,
        out_shape=(
            jax.ShapeDtypeStruct((2 * rows, count // 2 * wide), value.dtype),
            jax.ShapeDtypeStruct((rows, count * wide), value.dtype),
        ),
        grid_spec=pltpu.PrefetchScalarGridSpec(
            num_scalar_prefetch=1,
            grid=(count,),
            in_specs=[pl.BlockSpec((rows, wide), lambda i, at: (0, i * step + at[0]))],
            out_specs=(
                pl.BlockSpec((rows, wide), lambda i, at: (i // 2, i % 2)),
                pl.BlockSpec((rows, wide), lambda i, at: (0, i)),
            ),
        ),
        compiler_params=params(),
        name="strided_columns",
    )(first.astype(jnp.int32).reshape(1), value)


def owned_kernel(depth, pieces_ref, qkv_ref, ckv_ref):
    _, heads, groups, share, _ = pieces_ref.shape
    width = heads * depth
    for head in range(heads):
        total = 0.0
        for p in range(pieces_ref.shape[0]):
            for g in range(groups):
                total = total + pieces_ref[p, head, g].astype(full)
        at = head * depth
        for i in range(3):
            qkv_ref[:, i * width + at : i * width + at + depth] = total[:, i * depth : (i + 1) * depth]
        for i in range(2):
            ckv_ref[:, i * width + at : i * width + at + depth] = total[:, (3 + i) * depth : (4 + i) * depth]


def owned_columns(pieces, depth):
    _, heads, _, share, _ = pieces.shape
    width = heads * depth
    return pl.pallas_call(
        functools.partial(owned_kernel, depth),
        out_shape=(
            jax.ShapeDtypeStruct((share, 3 * width), full),
            jax.ShapeDtypeStruct((share, 2 * width), full),
        ),
        in_specs=[vmem()],
        out_specs=(vmem(),) * 2,
        compiler_params=params(),
        name="owned_columns",
    )(pieces)


def after(value, *others):
    return lax.optimization_barrier((value,) + others)[0]


class Exchange:
    def __init__(self):
        self.fsdp = lax.axis_size("fsdp")
        self.chips = lax.axis_size(CHIP)
        self.core = lax.axis_index("core")
        self.row = lax.axis_index("fsdp")
        self.chip = lax.axis_index(CHIP)
        self.paired = self.fsdp == 2
        self.cube = self.paired and self.chips == 8
        self.near, self.far = (self.chip >> 1) & 1, self.chip >> 2
        self.corner = 2 * (self.chip & 1) + self.core

    def swap(self, value, axis):
        return lax.ppermute(value, axis, [(0, 1), (1, 0)])

    def swap_chip(self, value, bit):
        return lax.ppermute(value, CHIP, [(i, i ^ bit) for i in range(self.chips)])

    def own_piece(self, shard):
        piece = shard.shape[0] // 2
        return lax.dynamic_slice_in_dim(shard, self.core * piece, piece, 0)

    def fetch(self, mine, begin=()):
        if not self.paired:
            return lax.all_gather(mine, ("fsdp", "core"), axis=0, tiled=True)
        return self.swap(after(mine, *begin) if begin else mine, "fsdp")

    def place(self, base, across, corner):
        if not self.paired:
            return across
        piece = across.shape[0]
        start = (1 - self.row) * 2 * piece
        whole = lax.dynamic_update_slice_in_dim(base, across, start + self.core * piece, 0)
        return lax.dynamic_update_slice_in_dim(whole, corner, start + (1 - self.core) * piece, 0)

    def place_all(self, bases, across):
        corner = self.swap(across, "core") if self.paired else across
        placed, at = [], 0
        for base in bases:
            cols = slice(at, at + base.shape[1])
            placed.append(self.place(base, across[:, cols], corner[:, cols]))
            at += base.shape[1]
        return placed

    def gather_last(self, shard):
        if not self.paired:
            return lax.all_gather(shard, "fsdp", axis=shard.ndim - 1, tiled=True)
        other = self.swap(shard, "fsdp")
        return jnp.where(
            self.row == 0,
            jnp.concatenate([shard, other], axis=-1),
            jnp.concatenate([other, shard], axis=-1),
        )


    def hidden_parts(self, shard, axis):
        size = shard.shape[axis]
        if not self.cube:
            wide = size // 2
            return lax.dynamic_slice_in_dim(shard, self.core * wide, wide, axis)
        wide = size // 8
        parts = [
            lax.dynamic_slice_in_dim(shard, (4 * z + self.corner) * wide, wide, axis) for z in range(2)
        ]
        return jnp.concatenate(parts, axis=axis)

    def up_part(self, shard):
        rows, hidden = shard.shape
        if self.cube:
            return strided_columns(shard, self.corner, 4, hidden // 16)
        split = shard.reshape(rows, self.fsdp, 2, hidden // (2 * self.fsdp))
        mine = lax.dynamic_index_in_dim(split, self.core, 2, keepdims=False)
        return mine, mine

    def swap_beside(self, value):
        return self.swap_chip(value, 1) if self.cube else self.swap(value, "fsdp")

    def quad_gather(self, value, hold=()):
        if not self.paired:
            return lax.all_gather(value, QUAD, axis=0, tiled=True), ()
        across = self.swap_beside(value)
        held = after(across, *hold)
        beside = self.swap(value, "core")
        corner = self.swap(held, "core")
        return jnp.concatenate([value, beside, held, corner], axis=0), (across,)

    def quad_sum(self, value):
        if not self.paired:
            total = lax.psum_scatter(value, QUAD, scatter_dimension=0, tiled=True)
            return total.astype(full), total
        rows = value.shape[0] // 4
        parts = value.reshape(2, 2, rows, value.shape[1])
        theirs = self.swap(parts[:, 1], "core")
        both = parts[:, 0].astype(full) + theirs.astype(full)
        got = self.swap_beside(both[1].astype(low))
        return (both[0], got), theirs

    def quad_direct(self, value):
        if not self.paired:
            return lax.psum_scatter(value, QUAD, scatter_dimension=0, tiled=True).astype(full)
        rows = value.shape[0] // 4
        mine, beside, across, corner = [value[i * rows : (i + 1) * rows] for i in range(4)]
        if self.cube:
            moves = [(i, i ^ 3) for i in range(2 * self.chips)]
            far = lax.ppermute(corner, CTX, moves)
        else:
            far = lax.ppermute(corner, QUAD, [(i, 3 - i) for i in range(4)])
        return mine, self.swap(beside, "core"), self.swap_beside(across), far

    def quad_total(self, pending, hold):
        if not self.paired:
            return pending
        mine = after(pending[0], *hold)
        return sum(piece.astype(full) for piece in (mine,) + pending[1:])

    def quad_end(self, pending, hold=()):
        if not self.paired:
            return pending
        mine, got = pending
        return (after(mine, *hold) if hold else mine) + got.astype(full)

    def send_half(self, value, axis, bit, swap, *others):
        if others:
            value = after(value, *others)
        sent = lax.dynamic_index_in_dim(value, 1 - bit, axis, keepdims=False)
        kept = lax.dynamic_index_in_dim(value, bit, axis, keepdims=False)
        return sent, (kept, swap(sent))

    def add(self, halves, *others):
        kept, got = halves
        if others:
            kept = after(kept, *others)
        return kept.astype(full) + got.astype(full)

    def chip_step(self, value, number, *others):
        bit = (self.chip >> number) & 1
        return self.send_half(value, 2 - number, bit, lambda v: self.swap_chip(v, 1 << number), *others)

    def chip_shape(self, value):
        return value.reshape((2, 2, 2, value.shape[0] // 8) + value.shape[1:])

    def chip_scatter(self, value):
        return lax.psum_scatter(value, CHIP, scatter_dimension=0, tiled=True).astype(full)

    def device_shape(self, value):
        rows, cols = value.shape
        return value.reshape(self.chips, 2, self.fsdp, rows // (self.chips * 2 * self.fsdp), cols)

    def device_scatter(self, values):
        stacked = jnp.stack([self.device_shape(v) for v in values], axis=3)
        stacked = lax.psum_scatter(stacked, "core", scatter_dimension=1, tiled=True)
        stacked = lax.psum_scatter(stacked, "fsdp", scatter_dimension=2, tiled=True)
        stacked = lax.psum_scatter(stacked, CHIP, scatter_dimension=0, tiled=True)
        return [stacked[0, 0, 0, i].astype(full) for i in range(len(values))]

    def to_owner(self, value):
        chips, fsdp = self.chips, self.fsdp
        moves = []
        for chip in range(chips):
            for core in range(2):
                for row in range(fsdp):
                    moves.append(
                        ((chip * 2 + core) * fsdp + row, (row * 2 + core) * chips + chip)
                    )
        return lax.ppermute(value, ALL, moves)

    def quad_columns(self, value):
        quad = 2 * self.fsdp
        rows, wide = value.shape
        share = rows // quad
        value = lax.all_to_all(value, QUAD, 0, 1, tiled=True)
        value = value.reshape(share, 2, self.fsdp, wide).transpose(0, 2, 1, 3)
        return value.reshape(share, quad * wide)

    def corner_columns(self, value, hold):
        def block(bits):
            return lax.dynamic_index_in_dim(value, self.corner ^ bits, 0, keepdims=False)

        got = [
            block(0),
            self.swap(block(1), "core"),
            self.swap_chip(block(2), 1),
            lax.ppermute(block(3), CTX, [(i, i ^ 3) for i in range(2 * self.chips)]),
        ]
        got = [after(piece, *hold) for piece in got]
        got = [jnp.where(self.core == 0, got[i], got[i ^ 1]) for i in range(4)]
        got = [jnp.where(self.chip & 1 == 0, got[i], got[i ^ 2]) for i in range(4)]
        got = [piece.astype(full) for piece in got]
        step = value.shape[2] // 4
        return jnp.concatenate(
            [got[i][:, z * step : (z + 1) * step] for z in range(4) for i in range(4)], axis=1
        )

    def hidden_vector(self, value, hidden):
        devices = self.chips * 2 * self.fsdp
        if not self.cube:
            spread = jnp.zeros((hidden,), full)
            at = (self.row * 2 + self.core) * value.shape[0]
            return lax.dynamic_update_slice_in_dim(spread, value, at, 0).reshape(devices, -1)
        spread = jnp.zeros((4, 4, hidden // 16), full)
        spread = lax.dynamic_update_slice_in_dim(spread, value.reshape(4, 1, -1), self.corner, 1)
        return spread.reshape(devices, -1)


def per_device(
    tokens, encoder, cotangent, seq_lengths, source_lengths, pair_order, pair_flip,
    ln_gain, ln_bias, attn_bias, self_qkv, self_out, cross_q, cross_kv, cross_out,
    w_up, up_bias, w_down, down_bias,
):
    move = Exchange()
    resid = tokens[0].astype(full)
    source = encoder[0]
    grad_low = cotangent[0]
    rows, width = resid.shape
    src_rows = source.shape[0]
    depth = width // H
    ctx_count = lax.axis_size(CTX)
    parts = lax.axis_size("part")
    devices = ctx_count * move.fsdp
    here = lax.axis_index(CTX)
    part = lax.axis_index("part")

    plan = attention_plan(
        pair_order[0], pair_flip[0], seq_lengths[0], source_lengths[0],
        here, part, parts, rows, src_rows * ctx_count,
    )
    query_slot, key_slot, self_plan, cross_plan, group_plan, self_ranges, cross_ranges, group_ranges = plan

    small = [ln_gain, ln_bias, attn_bias.reshape(6, -1), down_bias[None]]
    bias_up = move.hidden_parts(up_bias, 0)
    if move.cube:
        small.append(bias_up.reshape(2, -1))
    small = move.gather_last(jnp.concatenate(small, axis=0)).astype(full)
    if move.cube:
        half = small.shape[1] // 2
        bias_up = jnp.concatenate([small[13, :half], small[14, :half], small[13, half:], small[14, half:]])
    bias_up = bias_up.astype(full)
    gains, shifts, biases, bias_down = small[0:3], small[3:6], small[6:12].reshape(2, 3, width), small[12]
    shards = (cross_kv, self_out, cross_q, cross_out)
    middle = jnp.concatenate([move.own_piece(w) for w in shards], axis=1)
    qkv_piece = move.own_piece(self_qkv)
    bases = [jnp.concatenate([w, w], axis=0) if move.paired else w for w in shards]
    qkv_base = jnp.concatenate([self_qkv, self_qkv], axis=0) if move.paired else self_qkv
    up_mine, up_local = move.up_part(w_up)
    down_mine = move.hidden_parts(w_down, 0)
    if move.cube:
        shard_rows = w_up.shape[0]
        branch_piece = jnp.concatenate([up_mine, down_mine], axis=0)
        up_base = jnp.concatenate([up_local, up_local], axis=0)
        down_base = jnp.concatenate([down_mine, down_mine], axis=0)
        later = (up_base, down_base, branch_piece)
    else:
        later = ()

    got_qkv = move.fetch(qkv_piece)
    group_source = lax.all_gather(source, HEADS, axis=0, tiled=True)

    norm_one, back_one = jax.vjp(layer_norm, resid, gains[0], shifts[0])
    normed_one = norm_one.astype(low)
    w_qkv, = move.place_all([qkv_base], after(got_qkv, *plan, *bases, middle, up_mine))
    projected = contract(w_qkv, normed_one, 0, 1)
    shift_qkv = jnp.concatenate([biases[0, 0], jnp.zeros((width,), full), biases[0, 1]])
    projected = (projected + shift_qkv[:, None]).astype(low)
    projected = projected.reshape(3, H, depth, rows).transpose(1, 0, 2, 3).reshape(H, 3 * depth, rows)
    own_heads = lax.all_to_all(projected, HEADS, 0, 0, tiled=True)

    got_middle = move.fetch(middle, (got_qkv,))
    self_in = after(own_heads, *later)
    all_heads = self_in if parts == 1 else lax.all_gather(self_in, "part", axis=0, tiled=True)
    self_args = (self_plan, query_slot, key_slot, self_ranges, self_in, all_heads)
    self_low, self_exact, self_lse = self_forward(*self_args)
    self_att = lax.all_to_all(self_low, HEADS, 0, 0, tiled=True).reshape(width, rows)
    w_ckv, w_out, w_cq, w_cout = move.place_all(bases, after(got_middle, self_low))
    grad_quad, got_quad = move.quad_gather(after(grad_low, self_low), (self_att,))

    every_source = group_source
    if parts > 1:
        every_source = lax.all_gather(group_source, "part", axis=0, tiled=True)
    shift_ckv = jnp.concatenate([jnp.zeros((width,), full), biases[1, 1]])
    src_kv = (jnp.dot(every_source, w_ckv, preferred_element_type=full) + shift_ckv).astype(low)
    mixed_one = resid + contract(self_att, w_out, 0, 0) + biases[0, 2]

    norm_two, back_two = jax.vjp(layer_norm, mixed_one, gains[1], shifts[1])
    normed_two = norm_two.astype(low)
    cross_query = (contract(w_cq, normed_two, 0, 1) + biases[1, 0][:, None]).astype(low)
    cross_query = after(cross_query, *got_quad) if move.cube else cross_query
    group_one = lax.all_gather(after(norm_one, self_att).astype(low), HEADS, axis=0, tiled=True)
    cross_att, cross_exact, cross_lse = cross_forward(cross_plan, cross_ranges, cross_query, src_kv)
    mixed_two = mixed_one + contract(cross_att, w_cout, 0, 0) + biases[1, 2]

    head = lax.axis_index(HEADS)
    head_cols = [
        lax.dynamic_slice_in_dim(w_ckv, i * width + head * depth, depth, 1) for i in range(2)
    ]
    head_shift = jnp.concatenate(
        [jnp.zeros((depth,), full), lax.dynamic_slice_in_dim(biases[1, 1], head * depth, depth, 0)]
    )
    head_kv = jnp.dot(after(every_source, cross_att), jnp.concatenate(head_cols, axis=1), preferred_element_type=full)
    head_kv = (head_kv + head_shift).astype(low)

    norm_three, back_three = jax.vjp(layer_norm, mixed_two, gains[2], shifts[2])
    three_low = norm_three.astype(low)
    if move.cube:
        got_branch = move.swap(after(branch_piece, got_middle), "fsdp")
        theirs = after(got_branch, cross_att)
        start = (1 - move.row) * shard_rows
        half = up_mine.shape[1]
        w_upper = lax.dynamic_update_slice(up_base, theirs[:shard_rows], (start, 0))
        w_upper = lax.dynamic_update_slice(w_upper, theirs[shard_rows : 2 * shard_rows], (start, half))
        w_lower = lax.dynamic_update_slice_in_dim(
            down_base, theirs[2 * shard_rows :], (1 - move.row) * down_mine.shape[0], 0
        )
    else:
        w_upper = lax.all_to_all(up_mine, "fsdp", 1, 0, tiled=True).reshape(width, -1)
        w_lower = down_mine
    wide = w_upper.shape[1]
    quad_three, _ = move.quad_gather(three_low)
    if move.cube:
        quad_three = after(quad_three, got_branch, head_kv)
    hidden_pre = jnp.dot(quad_three, w_upper, preferred_element_type=full) + bias_up
    head_query = after(cross_query.reshape(H, depth, rows), quad_three)
    head_query = lax.all_to_all(head_query, HEADS, 0, 0, tiled=True)
    activated, back_gelu = jax.vjp(gelu_tanh, hidden_pre)
    act_low = activated.astype(low)
    grad_act = contract(grad_quad, w_lower, 1, 1)
    grad_hidden = back_gelu(grad_act)[0].astype(low)
    grad_three, met = move.quad_sum(contract(after(grad_hidden, head_query), w_upper, 1, 1).astype(low))

    grad_out = grad_low.astype(full)
    grad_b_lower = column_sums(grad_low)
    grad_w_lower = contract(after(act_low, met), grad_quad, 0, 0).astype(low)
    grad_b_upper = column_sums(grad_hidden)
    sent = ()
    if move.cube:
        lower = grad_w_lower.reshape(2, 2, 2, -1, width)
        sent_a, lower = move.send_half(lower, 2, move.row, lambda v: move.swap(v, "fsdp"))
        sent = (sent_a,)
    grad_three = move.quad_end(grad_three, sent)
    grad_ln_three, gain_three, shift_three = back_three(grad_three)
    grad_two = grad_out + grad_ln_three

    grad_two_low = grad_two.astype(low)
    grad_b_cout = column_sums(grad_two_low)
    grad_cross_att = contract(w_cout, grad_two_low, 1, 1).astype(low)
    cross_rows = grad_cross_att.reshape(H, depth, rows)
    deltas = jnp.sum(cross_rows.astype(full) * cross_exact.reshape(H, depth, rows), axis=1)
    lse_rows = cross_lse[:, 0:2].reshape(H, rows)
    extra = jnp.stack(in_thirds(lse_rows) + in_thirds(deltas), axis=1)
    extra = jnp.pad(extra, ((0, 0), (0, 10), (0, 0)))
    cross_rows = jnp.concatenate([cross_rows, extra], axis=1)
    grad_head = lax.all_to_all(cross_rows, HEADS, 0, 0, tiled=True)
    grad_w_upper = contract(after(quad_three, grad_cross_att), grad_hidden, 0, 0).astype(low)
    branch = jnp.dot(after(act_low, grad_cross_att), w_lower, preferred_element_type=full).astype(low)
    branch_sum = move.quad_direct(branch)
    sent_b = grad_w_upper
    if move.cube:
        upper = grad_w_upper.reshape(2, 2, 4, 2, -1, wide)
        sent_b, upper = move.send_half(upper, 3, move.row, lambda v: move.swap(v, "fsdp"))
    head_in = after(grad_head, head_query, head_kv, sent_b, group_one)
    head_cq, head_dkv_rows, packed_dkv = cross_backward(
        group_plan, query_slot, group_ranges, head_query, head_kv, head_in,
        low if parts == 1 else full, ctx_count,
    )
    if parts > 1:
        head_dkv_rows = lax.psum_scatter(head_dkv_rows, "part", scatter_dimension=0, tiled=True).astype(low)
    head_cq_sent = after(head_cq, lower[1]) if move.cube else head_cq
    grad_cq = lax.all_to_all(head_cq_sent, HEADS, 0, 0, tiled=True).reshape(width, rows)
    if move.cube:
        lower = move.add(lower, head_cq).astype(low)
        _, lower = move.send_half(lower, 1, move.near, lambda v: move.swap_chip(v, 2))
    grad_b_cq = jnp.sum(grad_cq.astype(full), axis=1)
    grad_ln_two, gain_two, shift_two = back_two(contract(grad_cq, w_cq, 0, 1))
    grad_one = grad_two + grad_ln_two

    grad_one_low = grad_one.astype(low)
    grad_b_out = column_sums(grad_one_low)
    grad_self_att = contract(w_out, grad_one_low, 1, 1).astype(low).reshape(H, depth, rows)
    grad_heads = lax.all_to_all(grad_self_att, HEADS, 0, 0, tiled=True)
    grad_w_cout = contract(after(cross_att, head_cq), grad_two_low, 1, 0).astype(low)
    grad_w_cq = contract(after(normed_two, grad_self_att), grad_cq, 0, 1).astype(low)
    grad_w_out = contract(after(self_att, grad_self_att), grad_one_low, 1, 0).astype(low)
    if move.cube:
        square = []
        for one in (grad_w_cout, grad_w_cq, grad_w_out):
            _, both = move.send_half(move.device_shape(one), 1, move.core, lambda v: move.swap(v, "core"))
            square.append(move.add(both).astype(low))
        sent_c, square = move.send_half(jnp.stack(square, axis=1), 2, move.row, lambda v: move.swap(v, "fsdp"))
        upper = move.add(upper, grad_self_att).astype(low)
        sent_b, upper = move.send_half(upper, 1, move.near, lambda v: move.swap_chip(v, 2))
        grad_heads = after(grad_heads, sent_b, sent_c)
    *head_grads, head_rows = self_backward(
        *self_args, grad_heads, self_exact, self_lse, low if parts == 1 else full, packed_dkv
    )
    if parts > 1:
        head_dkv = lax.psum_scatter(head_grads[1], "part", scatter_dimension=0, tiled=True).astype(low)
        head_grad = jnp.concatenate([head_grads[0], head_dkv], axis=1)
        head_rows = head_grad.transpose(1, 0, 2).reshape(3 * depth, H * rows)
        own_dkv = lax.all_to_all(head_dkv_rows.reshape(H, src_rows, 2 * depth), HEADS, 0, 0, tiled=True)
    else:
        head_grad = head_grads[0]
    if move.cube:
        head_grad = after(head_grad, upper[1], square[1])
    grad_qkv = lax.all_to_all(head_grad, HEADS, 0, 0, tiled=True)
    if parts == 1:
        packed = grad_qkv[:, 3 * depth :]
        own_dkv = jnp.concatenate([packed[:, :, : 2 * depth], packed[:, :, 2 * depth :]], axis=1)
        grad_qkv = grad_qkv[:, : 3 * depth]
    if move.cube:
        upper = move.add(upper, head_rows).astype(low)
        sent_b, upper = move.send_half(upper, 0, move.far, lambda v: move.swap_chip(v, 4))
        square = move.add(square, head_rows).astype(low)
        square = square.reshape((2, 2, 2) + square.shape[1:])
        sent_c, square = move.send_half(square, 2, move.chip & 1, lambda v: move.swap_chip(v, 1))
        lower = move.add(lower, head_rows).astype(low)
        sent_a, lower = move.send_half(lower, 0, move.far, lambda v: move.swap_chip(v, 4))
        soon = (sent_a, sent_b, sent_c)
    else:
        soon = (head_rows,)
    head_w = contract(after(head_rows, *soon), group_one, 1, 0).astype(low)
    head_c = contract(group_source, after(head_dkv_rows, *soon), 0, 0).astype(low)
    flown = ()
    if move.cube:
        square = move.add(square, head_w).astype(low)
        sent_a, square = move.send_half(square, 1, move.near, lambda v: move.swap_chip(v, 2))
        flown = (sent_a,)
    grad_qkv = grad_qkv.reshape(H, 3, depth, rows).transpose(1, 0, 2, 3).reshape(3 * width, rows)
    grad_ln_one, gain_one, shift_one = back_one(contract(after(grad_qkv, *flown), w_qkv, 0, 1))
    grad_input = grad_one + grad_ln_one

    own_dk = own_dkv[:, :, :depth].transpose(1, 0, 2).reshape(src_rows, width)
    own_dv = own_dkv[:, :, depth:].transpose(1, 0, 2).reshape(src_rows, width)
    head_all = jnp.concatenate([head_w.T, head_c], axis=1)
    grad_source = contract(jnp.concatenate([own_dk, own_dv], axis=1), w_ckv, 1, 1)
    cols = head_all.shape[1]
    share = width // devices

    if not move.cube:
        lower_own = move.to_owner(move.chip_scatter(grad_w_lower).astype(low)).astype(full)
        upper_own = move.quad_columns(move.chip_scatter(grad_w_upper).astype(low)).astype(full)
        cout_own, cq_own, out_own = move.device_scatter([grad_w_cout, grad_w_cq, grad_w_out])

    head_sums = jnp.sum(head_rows.astype(full), axis=1)
    spread = [
        lax.dynamic_update_slice_in_dim(jnp.zeros((width,), full), part, head * depth, 0)
        for part in (head_sums[:depth], head_sums[2 * depth :], column_sums(head_dkv_rows[:, depth:]))
    ]
    early = [gain_two, gain_three, shift_two, shift_three, spread[0], spread[1],
             grad_b_out, grad_b_cq, spread[2], grad_b_cout, grad_b_lower]

    def by_owner(vectors):
        stacked = jnp.stack(vectors).reshape(len(vectors), devices, share)
        return stacked.transpose(1, 0, 2).reshape(devices, len(vectors) * share)

    def in_rows(values):
        count = -(-values.shape[1] // cols)
        values = jnp.pad(values, ((0, 0), (0, count * cols - values.shape[1])))
        return values.astype(low).reshape(devices, count, cols)

    hidden = wide * 2 * move.fsdp
    early_rows = in_rows(
        jnp.concatenate([by_owner(early), move.hidden_vector(grad_b_upper, hidden)], axis=1)
    )
    late_rows = in_rows(by_owner([gain_one, shift_one]))
    outgoing = jnp.concatenate(
        [head_all.reshape(devices, share, cols), early_rows, late_rows], axis=1
    )
    incoming = lax.all_to_all(outgoing, ALL, 0, 0, tiled=True)
    result = mixed_two + move.quad_total(branch_sum, soon) + bias_down
    if move.cube:
        lower_own = move.add(lower, outgoing)
        upper_own = move.corner_columns(move.add(upper, outgoing).astype(low), (incoming,))
        square = move.add(square, outgoing).astype(low)
        _, square = move.send_half(square, 0, move.far, lambda v: move.swap_chip(v, 4))
        cout_own, cq_own, out_own = tuple(move.add(square, incoming))
    heads_in = incoming[:, :share].reshape(parts, H, move.fsdp, share, cols)
    qkv_own, ckv_own = owned_columns(heads_in, depth)
    tail = jnp.sum(incoming[:, share:].astype(full), axis=0)
    at = early_rows.shape[1]
    first = tail[:at].reshape(-1)
    vec = first[: 11 * share].reshape(11, share)
    bup_own = first[11 * share : 11 * share + hidden // devices]
    last = tail[at:].reshape(-1)[: 2 * share].reshape(2, share)
    return (
        result.astype(low)[None],
        grad_input[None],
        grad_source[None],
        jnp.stack([last[0], vec[0], vec[1]]),
        jnp.stack([last[1], vec[2], vec[3]]),
        vec[4:10].reshape(2, 3, share),
        qkv_own,
        out_own,
        cq_own,
        ckv_own,
        cout_own,
        upper_own,
        bup_own,
        lower_own,
        vec[10],
    )


def solution(mesh):
    ctx, fsdp = mesh.shape["ctx"], mesh.shape["fsdp"]
    inner = Mesh(mesh.devices.reshape(ctx // H, H // 2, 2, fsdp), ALL)
    tokens = P("fsdp", CTX, None)
    group = P("fsdp", None)
    owned = P(ALL, None)
    return jax.shard_map(
        per_device,
        mesh=inner,
        in_specs=(tokens,) * 3
        + (group,) * 4
        + (P(None, "fsdp"), P(None, "fsdp"), P(None, None, "fsdp"))
        + (group,) * 6
        + (P("fsdp"), group, P("fsdp")),
        out_specs=(tokens,) * 3
        + (P(None, ALL), P(None, ALL), P(None, None, ALL))
        + (owned,) * 6
        + (P(ALL), owned, P(ALL)),
        check_vma=False,
    )
```

```python
import functools

import jax
import jax.numpy as jnp
from jax import lax
from jax.experimental import pallas as pl
from jax.experimental.pallas import tpu as pltpu
from jax.sharding import Mesh
from jax.sharding import PartitionSpec as P

H = 16
BLOCK = 128

CHIP = ("part", "hc")
HEADS = ("hc", "core")
CTX = ("part", "hc", "core")
QUAD = ("core", "fsdp")
ALL = ("part", "hc", "core", "fsdp")

ln_eps = 1e-05
score_scale = 0.125
low = jnp.bfloat16
full = jnp.float32
SELF_TILES = (512, 512)
SELF_CHAINS = 1
CROSS_TILE = 1024
VMEM_BYTES = 56 * 1024 * 1024


def layer_norm(v, gain, shift):
    centred = v - jnp.mean(v, axis=-1, keepdims=True)
    spread = jnp.mean(centred * centred, axis=-1, keepdims=True)
    return centred * lax.rsqrt(spread + ln_eps) * gain + shift


def gelu_tanh(v):
    return 0.5 * v * (1.0 + jnp.tanh(0.7978845608028654 * (v + 0.044715 * v * v * v)))


def in_thirds(value):
    terms = []
    for _ in range(3):
        term = lax.reduce_precision(value, 8, 7)
        terms.append(term.astype(low))
        value = value - term
    return terms


def contract(left, right, left_dim, right_dim):
    return lax.dot_general(
        left, right, (((left_dim,), (right_dim,)), ((), ())), preferred_element_type=full
    )


def column_sums(values):
    return jnp.sum(values.astype(full), axis=0)


def plan_kernel(
    query_tile, self_key_tile, cross_key_tile, group_key_tile, cross_rows,
    order, flip, lengths, source_lengths, where,
    query_slot, key_slot, self_plan, cross_plan, group_plan, self_ranges, cross_ranges, group_ranges,
    block_of,
):
    pairs, documents = order.shape[0], lengths.shape[0]
    here, part = where[0], where[1]
    ends, source_ends = [], []
    for d in range(documents):
        ends.append(lengths[d] + (ends[-1] if d else 0))
        source_ends.append(source_lengths[d] + (source_ends[-1] if d else 0))

    def start_of(places):
        start = jnp.zeros_like(places)
        for end in ends:
            start = jnp.where(places >= end, end, start)
        return start

    def source_of(places):
        start, stop = jnp.zeros_like(places), jnp.zeros_like(places) + source_ends[0]
        for d in range(documents - 1):
            start = jnp.where(places >= ends[d], source_ends[d], start)
            stop = jnp.where(places >= ends[d], source_ends[d + 1], stop)
        return start, stop

    def stored(i):
        number = order[i >> 1]
        upper = (flip[i >> 1] + i) & 1 == 1
        return jnp.where(upper, 2 * pairs - 1 - number, number)

    @pl.loop(0, 2 * pairs)
    def _(i):
        key_slot[stored(i)] = i

    blocks = query_slot.shape[0]
    lanes = lax.broadcasted_iota(jnp.int32, (1, BLOCK), 1)

    def take(b, count):
        slot = key_slot[b] - part * blocks
        inside = (slot >= 0) & (slot < blocks)

        @pl.when(inside)
        def _():
            query_slot[count] = slot
            block_of[count] = b
            places = lanes + b * BLOCK
            self_ranges[0:1, tile_at(count, BLOCK)] = start_of(places)
            self_ranges[1:2, tile_at(count, BLOCK)] = places + 1
            start, stop = source_of(places)
            group_ranges[0:1, tile_at(count, BLOCK)] = start
            group_ranges[1:2, tile_at(count, BLOCK)] = stop

        return count + jnp.where(inside, 1, 0)

    lax.fori_loop(0, 2 * pairs, take, jnp.int32(0))

    def write(plan, t, low_start, high_start, low_stop, high_stop, key_tile):
        first = lax.div(low_start, key_tile)
        last = lax.div(high_stop + key_tile - 1, key_tile)
        inner = jnp.clip(lax.div(high_start + key_tile - 1, key_tile), first, last)
        plan[0, t] = first
        plan[1, t] = inner
        plan[2, t] = jnp.clip(lax.div(low_stop, key_tile), inner, last)
        plan[3, t] = last

    step = query_tile // BLOCK

    @pl.loop(0, blocks // step)
    def _(t):
        begin = block_of[t * step] * BLOCK
        end = block_of[t * step + step - 1] * BLOCK + BLOCK - 1
        write(self_plan, t, start_of(begin), start_of(end), begin + 1, end + 1, self_key_tile)
        first, last = source_of(begin), source_of(end)
        write(group_plan, t, first[0], last[0], first[1], last[1], group_key_tile)

    edges = []
    for k in range(cross_rows // BLOCK):
        begin = stored(here * (cross_rows // BLOCK) + k) * BLOCK
        low_edge, high_edge = source_of(begin), source_of(begin + BLOCK - 1)
        if k:
            edges = [
                jnp.minimum(edges[0], low_edge[0]), jnp.maximum(edges[1], high_edge[0]),
                jnp.minimum(edges[2], low_edge[1]), jnp.maximum(edges[3], high_edge[1]),
            ]
        else:
            edges = [low_edge[0], high_edge[0], low_edge[1], high_edge[1]]
        start, stop = source_of(lanes + begin)
        cross_ranges[0:1, k * BLOCK : (k + 1) * BLOCK] = start
        cross_ranges[1:2, k * BLOCK : (k + 1) * BLOCK] = stop
    write(cross_plan, 0, *edges, cross_key_tile)


def attention_plan(order, flip, lengths, source_lengths, here, part, parts, rows, sources):
    blocks = 2 * order.shape[0]
    mine = blocks // parts
    query_tile, key_tile = self_tiles(mine * BLOCK)
    group_key_tile = cross_tiles(mine * BLOCK, sources)[1]
    tiles = mine * BLOCK // query_tile
    shapes = ((mine,), (blocks,), (4, tiles), (4, 1), (4, tiles), (2, mine * BLOCK), (2, rows), (2, mine * BLOCK))
    return pl.pallas_call(
        functools.partial(plan_kernel, query_tile, key_tile, cross_tile(sources), group_key_tile, rows),
        out_shape=tuple(jax.ShapeDtypeStruct(shape, jnp.int32) for shape in shapes),
        in_specs=[smem()] * 5,
        out_specs=(smem(),) * 5 + (vmem(),) * 3,
        scratch_shapes=[pltpu.SMEM((mine,), jnp.int32)],
        compiler_params=params(),
        name="attention_plan",
    )(order, flip, lengths, source_lengths, jnp.stack([here, part]).astype(jnp.int32))


def over_tiles(plan, tile_number, step, carry):
    first, inner = plan[0, tile_number], plan[1, tile_number]
    outer, last = plan[2, tile_number], plan[3, tile_number]
    carry = lax.fori_loop(inner, outer, functools.partial(step, masked=False), carry)
    before = inner - first

    def edge(index, state):
        number = jnp.where(index < before, first + index, outer + index - before)
        return step(number, state, masked=True)

    return lax.fori_loop(0, before + last - outer, edge, carry)


def masked_scores(scores, number, tile, start, stop):
    keys = number * tile + lax.broadcasted_iota(jnp.int32, scores.shape, 0)
    return jnp.where((keys >= start) & (keys < stop), scores, -jnp.inf)


def forward_tiles(plan, number, queries, start, stop, keys_of, values_of, tile, depth):
    chains = range(len(queries))
    width = queries[0].shape[1]
    start, stop = as_list(start, len(queries)), as_list(stop, len(queries))

    def step(j, carry, masked):
        top, total, accum = carry
        scores = [contract(keys_of(j), queries[i], 1, 0) for i in chains]
        if masked:
            scores = [masked_scores(scores[i], j, tile, start[i], stop[i]) for i in chains]
        newtop = [jnp.maximum(top[i], jnp.max(scores[i], axis=0, keepdims=True)) for i in chains]
        weights = [jnp.exp(scores[i] - newtop[i]) for i in chains]
        factor = [jnp.exp(top[i] - newtop[i]) for i in chains]
        total = [total[i] * factor[i] + jnp.sum(weights[i], axis=0, keepdims=True) for i in chains]
        accum = [
            accum[i] * factor[i] + contract(values_of(j, i), weights[i].astype(low), 1, 0)
            for i in chains
        ]
        return newtop, total, accum

    carry = (
        [jnp.full((1, width), -1e30, full) for _ in chains],
        [jnp.zeros((1, width), full) for _ in chains],
        [jnp.zeros((depth, width), full) for _ in chains],
    )
    top, total, accum = over_tiles(plan, number, step, carry)
    return [accum[i] / total[i] for i in chains], [top[i] + jnp.log(total[i]) for i in chains]


def as_list(value, count):
    return value if isinstance(value, list) else [value] * count


def identity(size):
    rows = lax.broadcasted_iota(jnp.int32, (size, size), 0)
    cols = lax.broadcasted_iota(jnp.int32, (size, size), 1)
    return jnp.where(rows == cols, 1.0, 0.0).astype(low)


def flipped(eye, block):
    return contract(eye, block, 1, 1).astype(low)


def tile_at(number, size):
    return pl.ds(pl.multiple_of(number * size, size), size)


def half_at(slot):
    return pl.ds(pl.multiple_of((slot & 1) * BLOCK, BLOCK), BLOCK)


def self_forward_kernel(
    tiles, plan, query_slot, key_slot, range_ref, own_ref, all_ref,
    out_ref, exact_ref, lse_ref, query_s, key_s, value_s,
):
    query_tile, tile = tiles
    depth, queries = query_s.shape
    count = value_s.shape[1]

    @pl.loop(0, queries // BLOCK)
    def _(b):
        slot = query_slot[b]
        query_s[:, tile_at(b, BLOCK)] = own_ref[slot >> 1, 0:depth, half_at(slot)] * low(score_scale)

    @pl.loop(0, count // BLOCK)
    def _(b):
        slot = key_slot[b]
        block = all_ref[slot >> 1, depth : 2 * depth, half_at(slot)]
        key_s[tile_at(b, BLOCK), :] = block.T
        value_s[:, tile_at(b, BLOCK)] = all_ref[slot >> 1, 2 * depth : 3 * depth, half_at(slot)]

    chains = SELF_CHAINS
    lanes = query_tile // chains

    @pl.loop(0, queries // query_tile)
    def _(t):
        here = [pl.ds(pl.multiple_of(t * query_tile + i * lanes, lanes), lanes) for i in range(chains)]
        result, lse = forward_tiles(
            plan, t, [query_s[:, at] for at in here], [range_ref[0:1, at] for at in here],
            [range_ref[1:2, at] for at in here],
            lambda j: key_s[tile_at(j, tile), :], lambda j, i: value_s[:, tile_at(j, tile)],
            tile, depth,
        )
        for i in range(chains):
            exact_ref[:, here[i]] = result[i]
            lse_ref[0:1, here[i]] = lse[i]

    @pl.loop(0, queries // BLOCK)
    def _(b):
        slot = query_slot[b]
        out_ref[slot >> 1, :, half_at(slot)] = exact_ref[:, tile_at(b, BLOCK)].astype(low)


def self_backward_kernel(
    tiles, joined, plan, query_slot, key_slot, range_ref, own_ref, all_ref, grad_ref, exact_ref, lse_ref,
    *rest,
):
    if joined:
        carried_ref, dq_ref, *rest = rest
        dkv_ref = dq_ref
        dq_ref[:, dq_ref.shape[1] - carried_ref.shape[1] :, :] = carried_ref[...]
    else:
        dq_ref, dkv_ref, *rest = rest
    rows_ref, query_s, grad_s, key_s, keyt_s, value_s, dq_s, dk_s, dv_s = rest
    query_tile, tile = tiles
    depth, queries = query_s.shape
    count = keyt_s.shape[1]

    @pl.loop(0, queries // BLOCK)
    def _(b):
        slot = query_slot[b]
        query_s[:, tile_at(b, BLOCK)] = own_ref[slot >> 1, 0:depth, half_at(slot)] * low(score_scale)
        grad_s[:, tile_at(b, BLOCK)] = grad_ref[slot >> 1, :, half_at(slot)]

    @pl.loop(0, count // BLOCK)
    def _(b):
        slot = key_slot[b]
        block = all_ref[slot >> 1, depth : 2 * depth, half_at(slot)]
        keyt_s[:, tile_at(b, BLOCK)] = block
        key_s[tile_at(b, BLOCK), :] = block.T
        value_s[tile_at(b, BLOCK), :] = all_ref[slot >> 1, 2 * depth : 3 * depth, half_at(slot)].T

    dk_s[...] = jnp.zeros_like(dk_s)
    dv_s[...] = jnp.zeros_like(dv_s)

    @pl.loop(0, queries // query_tile)
    def _(t):
        here = tile_at(t, query_tile)
        query, grad = query_s[:, here], grad_s[:, here]
        start, stop = range_ref[0:1, here], range_ref[1:2, here]
        lse = lse_ref[0:1, here]
        delta = jnp.sum(grad.astype(full) * exact_ref[:, here], axis=0, keepdims=True)

        def step(j, dq, masked):
            there = tile_at(j, tile)
            scores = contract(key_s[there, :], query, 1, 0)
            if masked:
                scores = masked_scores(scores, j, tile, start, stop)
            probs = jnp.exp(scores - lse)
            dprobs = contract(value_s[there, :], grad, 1, 0)
            dscores = (probs * (dprobs - delta)).astype(low)
            dv_s[:, there] += contract(grad, probs.astype(low), 1, 1)
            dk_s[:, there] += contract(query, dscores, 1, 1)
            return dq + contract(keyt_s[:, there], dscores, 1, 0)

        dq_s[:, here] = over_tiles(plan, t, step, jnp.zeros((depth, query_tile), full))

    @pl.loop(0, queries // BLOCK)
    def _(b):
        slot = query_slot[b]
        dq = (dq_s[:, tile_at(b, BLOCK)] * score_scale).astype(low)
        dq_ref[slot >> 1, 0:depth, half_at(slot)] = dq
        rows_ref[0:depth, tile_at(slot, BLOCK)] = dq

    @pl.loop(0, count // BLOCK)
    def _(b):
        slot = key_slot[b]
        dk = dk_s[:, tile_at(b, BLOCK)].astype(dkv_ref.dtype)
        dv = dv_s[:, tile_at(b, BLOCK)].astype(dkv_ref.dtype)
        at = depth if joined else 0
        dkv_ref[slot >> 1, at : at + depth, half_at(slot)] = dk
        dkv_ref[slot >> 1, at + depth : at + 2 * depth, half_at(slot)] = dv
        if count == queries:
            rows_ref[depth : 2 * depth, tile_at(slot, BLOCK)] = dk.astype(low)
            rows_ref[2 * depth : 3 * depth, tile_at(slot, BLOCK)] = dv.astype(low)


def one_head(values, head, depth):
    rows = lax.broadcasted_iota(jnp.int32, values.shape, 0)
    inside = (rows >= head * depth) & (rows < (head + 1) * depth)
    return jnp.where(inside, values, jnp.zeros_like(values))


def cross_forward_kernel(
    tile, plan, range_ref, query_ref, key_ref, value_ref, out_ref, exact_ref, lse_ref, value_s
):
    depth = value_s.shape[0] // 2

    eye = identity(2 * depth)

    def turn(j, _):
        value_s[:, tile_at(j, tile)] = flipped(eye, value_ref[tile_at(j, tile), :])
        return 0

    lax.fori_loop(plan[0, 0], plan[3, 0], turn, 0)
    query = query_ref[...] * low(score_scale)
    rows = [pl.ds(head * depth, depth) for head in range(2)]
    result, lse = forward_tiles(
        plan, 0, [one_head(query, head, depth) for head in range(2)],
        range_ref[0:1, :], range_ref[1:2, :],
        lambda j: key_ref[tile_at(j, tile), :],
        lambda j, i: value_s[rows[i], tile_at(j, tile)],
        tile, depth,
    )
    for head in range(2):
        exact_ref[rows[head], :] = result[head]
        out_ref[rows[head], :] = result[head].astype(low)
        lse_ref[0, head : head + 1, :] = lse[head]


def cross_backward_kernel(
    tiles, plan, query_slot, range_ref, query_ref, keys_values_ref, grad_ref,
    dq_ref, dkv_ref, packed_ref, query_s, grad_s, keyt_s, dkv_s,
):
    query_tile, tile = tiles
    depth = query_ref.shape[1]
    queries = query_s.shape[1]
    eye = identity(2 * depth)

    @pl.loop(0, queries // BLOCK)
    def _(b):
        slot = query_slot[b]
        at, there = tile_at(b, BLOCK), half_at(slot)
        query_s[:, at] = query_ref[slot >> 1, :, there] * low(score_scale)
        grad_s[:, at] = grad_ref[slot >> 1, :, there]

    @pl.loop(0, keyt_s.shape[1] // tile)
    def _(j):
        at = tile_at(j, tile)
        keyt_s[:, at] = flipped(eye, keys_values_ref[at, :])[0:depth]

    dkv_s[...] = jnp.zeros_like(dkv_s)
    blank = jnp.zeros((depth, query_tile), low)

    @pl.loop(0, queries // query_tile)
    def _(t):
        here = tile_at(t, query_tile)
        grad = grad_s[0:depth, here]
        start, stop = range_ref[0:1, here], range_ref[1:2, here]
        extra = grad_s[depth : depth + 16, here].astype(full)
        lse = extra[0:1] + extra[1:2] + extra[2:3]
        delta = extra[3:4] + extra[4:5] + extra[5:6]
        wide_query = jnp.concatenate([query_s[:, here], blank], axis=0)
        wide_grad = jnp.concatenate([blank, grad], axis=0)
        sides = jnp.concatenate([wide_query, wide_grad], axis=1)

        def step(j, dq, masked):
            there = tile_at(j, tile)
            keys_values = keys_values_ref[there, :]
            scores = contract(keys_values, wide_query, 1, 0)
            if masked:
                scores = masked_scores(scores, j, tile, start, stop)
            probs = jnp.exp(scores - lse)
            dprobs = contract(keys_values, wide_grad, 1, 0)
            dscores = (probs * (dprobs - delta)).astype(low)
            both = jnp.concatenate([dscores, probs.astype(low)], axis=1)
            dkv_s[there, :] += contract(both, sides, 1, 1)
            return dq + contract(keyt_s[:, there], dscores, 1, 0)

        dq = over_tiles(plan, t, step, jnp.zeros((depth, query_tile), full))
        query_s[:, here] = (dq * score_scale).astype(low)

    @pl.loop(0, queries // BLOCK)
    def _(b):
        slot = query_slot[b]
        dq_ref[slot >> 1, :, half_at(slot)] = query_s[:, tile_at(b, BLOCK)]

    total = dkv_s[...].astype(dkv_ref.dtype)
    dkv_ref[...] = total
    devices, half, _ = packed_ref.shape
    total = total.reshape(devices, 2, half, 2 * depth)
    packed_ref[:, :, 0 : 2 * depth] = total[:, 0].astype(low)
    packed_ref[:, :, 2 * depth : 4 * depth] = total[:, 1].astype(low)


def smem():
    return pl.BlockSpec(memory_space=pltpu.SMEM)


def vmem():
    return pl.BlockSpec(memory_space=pltpu.VMEM)


def params():
    return pltpu.CompilerParams(vmem_limit_bytes=VMEM_BYTES)


def self_tiles(queries):
    return min(SELF_TILES[0], queries), min(SELF_TILES[1], queries)


def self_forward(plan, query_slot, key_slot, ranges, own, everyone):
    heads, three, rows = own.shape
    depth = three // 3
    queries, count = heads * rows, everyone.shape[0] * rows
    tile = self_tiles(queries)
    return pl.pallas_call(
        functools.partial(self_forward_kernel, tile),
        out_shape=(
            jax.ShapeDtypeStruct((heads, depth, rows), low),
            jax.ShapeDtypeStruct((depth, queries), full),
            jax.ShapeDtypeStruct((8, queries), full),
        ),
        in_specs=[smem()] * 3 + [vmem()] * 3,
        out_specs=(vmem(),) * 3,
        scratch_shapes=[
            pltpu.VMEM((depth, queries), low),
            pltpu.VMEM((count, depth), low),
            pltpu.VMEM((depth, count), low),
        ],
        compiler_params=params(),
        cost_estimate=pl.CostEstimate(flops=1, bytes_accessed=1, transcendentals=0),
        name="self_forward",
    )(plan, query_slot, key_slot, ranges, own, everyone)


def self_backward(plan, query_slot, key_slot, ranges, own, everyone, grad, exact, lse, kv_type, carried):
    heads, three, rows = own.shape
    depth = three // 3
    queries, count = heads * rows, everyone.shape[0] * rows
    tile = self_tiles(queries)
    joined = heads == everyone.shape[0]
    if joined:
        shapes = (jax.ShapeDtypeStruct((heads, 3 * depth + carried.shape[1], rows), low),)
        extra = (carried,)
    else:
        shapes = (
            jax.ShapeDtypeStruct((heads, depth, rows), low),
            jax.ShapeDtypeStruct((everyone.shape[0], 2 * depth, rows), kv_type),
        )
        extra = ()
    return pl.pallas_call(
        functools.partial(self_backward_kernel, tile, joined),
        out_shape=shapes + (jax.ShapeDtypeStruct((3 * depth, queries), low),),
        in_specs=[smem()] * 3 + [vmem()] * (6 + len(extra)),
        out_specs=(vmem(),) * (len(shapes) + 1),
        scratch_shapes=[
            pltpu.VMEM((depth, queries), low),
            pltpu.VMEM((depth, queries), low),
            pltpu.VMEM((count, depth), low),
            pltpu.VMEM((depth, count), low),
            pltpu.VMEM((count, depth), low),
            pltpu.VMEM((depth, queries), full),
            pltpu.VMEM((depth, count), full),
            pltpu.VMEM((depth, count), full),
        ],
        compiler_params=params(),
        cost_estimate=pl.CostEstimate(flops=1, bytes_accessed=1, transcendentals=0),
        name="self_backward",
    )(plan, query_slot, key_slot, ranges, own, everyone, grad, exact, lse, *extra)


def cross_tiles(queries, count):
    return min(512, queries), min(512, count)


def cross_tile(count):
    return min(CROSS_TILE, count)


def pair_spec(rows, cols):
    return pl.BlockSpec((rows, cols), lambda i: (i, 0))


def cross_forward(plan, ranges, query, keys_values):
    width, rows = query.shape
    count = keys_values.shape[0]
    pairs = H // 2
    wide = width // pairs
    return pl.pallas_call(
        functools.partial(cross_forward_kernel, cross_tile(count)),
        grid=(pairs,),
        out_shape=(
            jax.ShapeDtypeStruct((width, rows), low),
            jax.ShapeDtypeStruct((width, rows), full),
            jax.ShapeDtypeStruct((pairs, 8, rows), full),
        ),
        in_specs=[
            smem(),
            vmem(),
            pair_spec(wide, rows),
            pl.BlockSpec((count, wide), lambda i: (0, i)),
            pl.BlockSpec((count, wide), lambda i: (0, pairs + i)),
        ],
        out_specs=(
            pair_spec(wide, rows),
            pair_spec(wide, rows),
            pl.BlockSpec((1, 8, rows), lambda i: (i, 0, 0)),
        ),
        scratch_shapes=[pltpu.VMEM((wide, count), low)],
        compiler_params=params(),
        cost_estimate=pl.CostEstimate(flops=1, bytes_accessed=1, transcendentals=0),
        name="cross_forward",
    )(plan, ranges, query, keys_values, keys_values)


def cross_backward(plan, query_slot, ranges, query, keys_values, grad, kv_type, parts):
    heads, depth, rows = query.shape
    queries, count = heads * rows, keys_values.shape[0]
    return pl.pallas_call(
        functools.partial(cross_backward_kernel, cross_tiles(queries, count)),
        out_shape=(
            jax.ShapeDtypeStruct((heads, depth, rows), low),
            jax.ShapeDtypeStruct((count, 2 * depth), kv_type),
            jax.ShapeDtypeStruct((parts, count // parts // 2, 4 * depth), low),
        ),
        in_specs=[smem()] * 2 + [vmem()] * 4,
        out_specs=(vmem(),) * 3,
        scratch_shapes=[
            pltpu.VMEM((depth, queries), low),
            pltpu.VMEM((grad.shape[1], queries), low),
            pltpu.VMEM((depth, count), low),
            pltpu.VMEM((count, 2 * depth), full),
        ],
        compiler_params=params(),
        cost_estimate=pl.CostEstimate(flops=1, bytes_accessed=1, transcendentals=0),
        name="cross_backward",
    )(plan, query_slot, ranges, query, keys_values, grad)


def copy_kernel(_, value_ref, square_ref, row_ref):
    square_ref[...] = value_ref[...]
    row_ref[...] = value_ref[...]


def strided_columns(value, first, step, wide):
    rows, cols = value.shape
    count = cols // (step * wide)
    return pl.pallas_call(
        copy_kernel,
        out_shape=(
            jax.ShapeDtypeStruct((2 * rows, count // 2 * wide), value.dtype),
            jax.ShapeDtypeStruct((rows, count * wide), value.dtype),
        ),
        grid_spec=pltpu.PrefetchScalarGridSpec(
            num_scalar_prefetch=1,
            grid=(count,),
            in_specs=[pl.BlockSpec((rows, wide), lambda i, at: (0, i * step + at[0]))],
            out_specs=(
                pl.BlockSpec((rows, wide), lambda i, at: (i // 2, i % 2)),
                pl.BlockSpec((rows, wide), lambda i, at: (0, i)),
            ),
        ),
        compiler_params=params(),
        name="strided_columns",
    )(first.astype(jnp.int32).reshape(1), value)


def owned_kernel(depth, pieces_ref, qkv_ref, ckv_ref):
    _, heads, groups, share, _ = pieces_ref.shape
    width = heads * depth
    for head in range(heads):
        total = 0.0
        for p in range(pieces_ref.shape[0]):
            for g in range(groups):
                total = total + pieces_ref[p, head, g].astype(full)
        at = head * depth
        for i in range(3):
            qkv_ref[:, i * width + at : i * width + at + depth] = total[:, i * depth : (i + 1) * depth]
        for i in range(2):
            ckv_ref[:, i * width + at : i * width + at + depth] = total[:, (3 + i) * depth : (4 + i) * depth]


def owned_columns(pieces, depth):
    _, heads, _, share, _ = pieces.shape
    width = heads * depth
    return pl.pallas_call(
        functools.partial(owned_kernel, depth),
        out_shape=(
            jax.ShapeDtypeStruct((share, 3 * width), full),
            jax.ShapeDtypeStruct((share, 2 * width), full),
        ),
        in_specs=[vmem()],
        out_specs=(vmem(),) * 2,
        compiler_params=params(),
        name="owned_columns",
    )(pieces)


def after(value, *others):
    return lax.optimization_barrier((value,) + others)[0]


class Exchange:
    def __init__(self):
        self.fsdp = lax.axis_size("fsdp")
        self.chips = lax.axis_size(CHIP)
        self.core = lax.axis_index("core")
        self.row = lax.axis_index("fsdp")
        self.chip = lax.axis_index(CHIP)
        self.paired = self.fsdp == 2
        self.cube = self.paired and self.chips == 8
        self.near, self.far = (self.chip >> 1) & 1, self.chip >> 2
        self.corner = 2 * (self.chip & 1) + self.core

    def swap(self, value, axis):
        return lax.ppermute(value, axis, [(0, 1), (1, 0)])

    def swap_chip(self, value, bit):
        return lax.ppermute(value, CHIP, [(i, i ^ bit) for i in range(self.chips)])

    def own_piece(self, shard):
        piece = shard.shape[0] // 2
        return lax.dynamic_slice_in_dim(shard, self.core * piece, piece, 0)

    def fetch(self, mine, begin=()):
        if not self.paired:
            return lax.all_gather(mine, ("fsdp", "core"), axis=0, tiled=True)
        return self.swap(after(mine, *begin) if begin else mine, "fsdp")

    def place(self, base, across, corner):
        if not self.paired:
            return across
        piece = across.shape[0]
        start = (1 - self.row) * 2 * piece
        whole = lax.dynamic_update_slice_in_dim(base, across, start + self.core * piece, 0)
        return lax.dynamic_update_slice_in_dim(whole, corner, start + (1 - self.core) * piece, 0)

    def place_all(self, bases, across):
        corner = self.swap(across, "core") if self.paired else across
        placed, at = [], 0
        for base in bases:
            cols = slice(at, at + base.shape[1])
            placed.append(self.place(base, across[:, cols], corner[:, cols]))
            at += base.shape[1]
        return placed

    def gather_last(self, shard):
        if not self.paired:
            return lax.all_gather(shard, "fsdp", axis=shard.ndim - 1, tiled=True)
        other = self.swap(shard, "fsdp")
        return jnp.where(
            self.row == 0,
            jnp.concatenate([shard, other], axis=-1),
            jnp.concatenate([other, shard], axis=-1),
        )


    def hidden_parts(self, shard, axis):
        size = shard.shape[axis]
        if not self.cube:
            wide = size // 2
            return lax.dynamic_slice_in_dim(shard, self.core * wide, wide, axis)
        wide = size // 8
        parts = [
            lax.dynamic_slice_in_dim(shard, (4 * z + self.corner) * wide, wide, axis) for z in range(2)
        ]
        return jnp.concatenate(parts, axis=axis)

    def up_part(self, shard):
        rows, hidden = shard.shape
        if self.cube:
            return strided_columns(shard, self.corner, 4, hidden // 16)
        split = shard.reshape(rows, self.fsdp, 2, hidden // (2 * self.fsdp))
        mine = lax.dynamic_index_in_dim(split, self.core, 2, keepdims=False)
        return mine, mine

    def swap_beside(self, value):
        return self.swap_chip(value, 1) if self.cube else self.swap(value, "fsdp")

    def quad_gather(self, value, hold=()):
        if not self.paired:
            return lax.all_gather(value, QUAD, axis=0, tiled=True), ()
        across = self.swap_beside(value)
        held = after(across, *hold)
        beside = self.swap(value, "core")
        corner = self.swap(held, "core")
        return jnp.concatenate([value, beside, held, corner], axis=0), (across,)

    def quad_sum(self, value):
        if not self.paired:
            total = lax.psum_scatter(value, QUAD, scatter_dimension=0, tiled=True)
            return total.astype(full), total
        rows = value.shape[0] // 4
        parts = value.reshape(2, 2, rows, value.shape[1])
        theirs = self.swap(parts[:, 1], "core")
        both = parts[:, 0].astype(full) + theirs.astype(full)
        got = self.swap_beside(both[1].astype(low))
        return (both[0], got), theirs

    def quad_direct(self, value):
        if not self.paired:
            return lax.psum_scatter(value, QUAD, scatter_dimension=0, tiled=True).astype(full)
        rows = value.shape[0] // 4
        mine, beside, across, corner = [value[i * rows : (i + 1) * rows] for i in range(4)]
        if self.cube:
            moves = [(i, i ^ 3) for i in range(2 * self.chips)]
            far = lax.ppermute(corner, CTX, moves)
        else:
            far = lax.ppermute(corner, QUAD, [(i, 3 - i) for i in range(4)])
        return mine, self.swap(beside, "core"), self.swap_beside(across), far

    def quad_total(self, pending, hold):
        if not self.paired:
            return pending
        mine = after(pending[0], *hold)
        return sum(piece.astype(full) for piece in (mine,) + pending[1:])

    def quad_end(self, pending, hold=()):
        if not self.paired:
            return pending
        mine, got = pending
        return (after(mine, *hold) if hold else mine) + got.astype(full)

    def send_half(self, value, axis, bit, swap, *others):
        if others:
            value = after(value, *others)
        sent = lax.dynamic_index_in_dim(value, 1 - bit, axis, keepdims=False)
        kept = lax.dynamic_index_in_dim(value, bit, axis, keepdims=False)
        return sent, (kept, swap(sent))

    def add(self, halves, *others):
        kept, got = halves
        if others:
            kept = after(kept, *others)
        return kept.astype(full) + got.astype(full)

    def chip_step(self, value, number, *others):
        bit = (self.chip >> number) & 1
        return self.send_half(value, 2 - number, bit, lambda v: self.swap_chip(v, 1 << number), *others)

    def chip_shape(self, value):
        return value.reshape((2, 2, 2, value.shape[0] // 8) + value.shape[1:])

    def chip_scatter(self, value):
        return lax.psum_scatter(value, CHIP, scatter_dimension=0, tiled=True).astype(full)

    def device_shape(self, value):
        rows, cols = value.shape
        return value.reshape(self.chips, 2, self.fsdp, rows // (self.chips * 2 * self.fsdp), cols)

    def device_scatter(self, values):
        stacked = jnp.stack([self.device_shape(v) for v in values], axis=3)
        stacked = lax.psum_scatter(stacked, "core", scatter_dimension=1, tiled=True)
        stacked = lax.psum_scatter(stacked, "fsdp", scatter_dimension=2, tiled=True)
        stacked = lax.psum_scatter(stacked, CHIP, scatter_dimension=0, tiled=True)
        return [stacked[0, 0, 0, i].astype(full) for i in range(len(values))]

    def to_owner(self, value):
        chips, fsdp = self.chips, self.fsdp
        moves = []
        for chip in range(chips):
            for core in range(2):
                for row in range(fsdp):
                    moves.append(
                        ((chip * 2 + core) * fsdp + row, (row * 2 + core) * chips + chip)
                    )
        return lax.ppermute(value, ALL, moves)

    def quad_columns(self, value):
        quad = 2 * self.fsdp
        rows, wide = value.shape
        share = rows // quad
        value = lax.all_to_all(value, QUAD, 0, 1, tiled=True)
        value = value.reshape(share, 2, self.fsdp, wide).transpose(0, 2, 1, 3)
        return value.reshape(share, quad * wide)

    def corner_columns(self, value, hold):
        def block(bits):
            return lax.dynamic_index_in_dim(value, self.corner ^ bits, 0, keepdims=False)

        got = [
            block(0),
            self.swap(block(1), "core"),
            self.swap_chip(block(2), 1),
            lax.ppermute(block(3), CTX, [(i, i ^ 3) for i in range(2 * self.chips)]),
        ]
        got = [after(piece, *hold) for piece in got]
        got = [jnp.where(self.core == 0, got[i], got[i ^ 1]) for i in range(4)]
        got = [jnp.where(self.chip & 1 == 0, got[i], got[i ^ 2]) for i in range(4)]
        got = [piece.astype(full) for piece in got]
        step = value.shape[2] // 4
        return jnp.concatenate(
            [got[i][:, z * step : (z + 1) * step] for z in range(4) for i in range(4)], axis=1
        )

    def hidden_vector(self, value, hidden):
        devices = self.chips * 2 * self.fsdp
        if not self.cube:
            spread = jnp.zeros((hidden,), full)
            at = (self.row * 2 + self.core) * value.shape[0]
            return lax.dynamic_update_slice_in_dim(spread, value, at, 0).reshape(devices, -1)
        spread = jnp.zeros((4, 4, hidden // 16), full)
        spread = lax.dynamic_update_slice_in_dim(spread, value.reshape(4, 1, -1), self.corner, 1)
        return spread.reshape(devices, -1)


def per_device(
    tokens, encoder, cotangent, seq_lengths, source_lengths, pair_order, pair_flip,
    ln_gain, ln_bias, attn_bias, self_qkv, self_out, cross_q, cross_kv, cross_out,
    w_up, up_bias, w_down, down_bias,
):
    move = Exchange()
    resid = tokens[0].astype(full)
    source = encoder[0]
    grad_low = cotangent[0]
    rows, width = resid.shape
    src_rows = source.shape[0]
    depth = width // H
    ctx_count = lax.axis_size(CTX)
    parts = lax.axis_size("part")
    devices = ctx_count * move.fsdp
    here = lax.axis_index(CTX)
    part = lax.axis_index("part")

    plan = attention_plan(
        pair_order[0], pair_flip[0], seq_lengths[0], source_lengths[0],
        here, part, parts, rows, src_rows * ctx_count,
    )
    query_slot, key_slot, self_plan, cross_plan, group_plan, self_ranges, cross_ranges, group_ranges = plan

    small = [ln_gain, ln_bias, attn_bias.reshape(6, -1), down_bias[None]]
    bias_up = move.hidden_parts(up_bias, 0)
    if move.cube:
        small.append(bias_up.reshape(2, -1))
    small = move.gather_last(jnp.concatenate(small, axis=0)).astype(full)
    if move.cube:
        half = small.shape[1] // 2
        bias_up = jnp.concatenate([small[13, :half], small[14, :half], small[13, half:], small[14, half:]])
    bias_up = bias_up.astype(full)
    gains, shifts, biases, bias_down = small[0:3], small[3:6], small[6:12].reshape(2, 3, width), small[12]
    shards = (cross_kv, self_out, cross_q, cross_out)
    middle = jnp.concatenate([move.own_piece(w) for w in shards], axis=1)
    qkv_piece = move.own_piece(self_qkv)
    bases = [jnp.concatenate([w, w], axis=0) if move.paired else w for w in shards]
    qkv_base = jnp.concatenate([self_qkv, self_qkv], axis=0) if move.paired else self_qkv
    up_mine, up_local = move.up_part(w_up)
    down_mine = move.hidden_parts(w_down, 0)
    if move.cube:
        shard_rows = w_up.shape[0]
        branch_piece = jnp.concatenate([up_mine, down_mine], axis=0)
        up_base = jnp.concatenate([up_local, up_local], axis=0)
        down_base = jnp.concatenate([down_mine, down_mine], axis=0)
        later = (up_base, down_base, branch_piece)
    else:
        later = ()

    got_qkv = move.fetch(qkv_piece)
    group_source = lax.all_gather(source, HEADS, axis=0, tiled=True)

    norm_one, back_one = jax.vjp(layer_norm, resid, gains[0], shifts[0])
    normed_one = norm_one.astype(low)
    w_qkv, = move.place_all([qkv_base], after(got_qkv, *plan, *bases, middle, up_mine))
    projected = contract(w_qkv, normed_one, 0, 1)
    shift_qkv = jnp.concatenate([biases[0, 0], jnp.zeros((width,), full), biases[0, 1]])
    projected = (projected + shift_qkv[:, None]).astype(low)
    projected = projected.reshape(3, H, depth, rows).transpose(1, 0, 2, 3).reshape(H, 3 * depth, rows)
    own_heads = lax.all_to_all(projected, HEADS, 0, 0, tiled=True)

    got_middle = move.fetch(middle, (got_qkv,))
    self_in = after(own_heads, *later)
    all_heads = self_in if parts == 1 else lax.all_gather(self_in, "part", axis=0, tiled=True)
    self_args = (self_plan, query_slot, key_slot, self_ranges, self_in, all_heads)
    self_low, self_exact, self_lse = self_forward(*self_args)
    self_att = lax.all_to_all(self_low, HEADS, 0, 0, tiled=True).reshape(width, rows)
    w_ckv, w_out, w_cq, w_cout = move.place_all(bases, after(got_middle, self_low))
    grad_quad, got_quad = move.quad_gather(after(grad_low, self_low), (self_att,))

    every_source = group_source
    if parts > 1:
        every_source = lax.all_gather(group_source, "part", axis=0, tiled=True)
    shift_ckv = jnp.concatenate([jnp.zeros((width,), full), biases[1, 1]])
    src_kv = (jnp.dot(every_source, w_ckv, preferred_element_type=full) + shift_ckv).astype(low)
    mixed_one = resid + contract(self_att, w_out, 0, 0) + biases[0, 2]

    norm_two, back_two = jax.vjp(layer_norm, mixed_one, gains[1], shifts[1])
    normed_two = norm_two.astype(low)
    cross_query = (contract(w_cq, normed_two, 0, 1) + biases[1, 0][:, None]).astype(low)
    cross_query = after(cross_query, *got_quad) if move.cube else cross_query
    group_one = lax.all_gather(after(norm_one, self_att).astype(low), HEADS, axis=0, tiled=True)
    cross_att, cross_exact, cross_lse = cross_forward(cross_plan, cross_ranges, cross_query, src_kv)
    mixed_two = mixed_one + contract(cross_att, w_cout, 0, 0) + biases[1, 2]

    head = lax.axis_index(HEADS)
    head_cols = [
        lax.dynamic_slice_in_dim(w_ckv, i * width + head * depth, depth, 1) for i in range(2)
    ]
    head_shift = jnp.concatenate(
        [jnp.zeros((depth,), full), lax.dynamic_slice_in_dim(biases[1, 1], head * depth, depth, 0)]
    )
    head_kv = jnp.dot(after(every_source, cross_att), jnp.concatenate(head_cols, axis=1), preferred_element_type=full)
    head_kv = (head_kv + head_shift).astype(low)

    norm_three, back_three = jax.vjp(layer_norm, mixed_two, gains[2], shifts[2])
    three_low = norm_three.astype(low)
    if move.cube:
        got_branch = move.swap(after(branch_piece, got_middle), "fsdp")
        theirs = after(got_branch, cross_att)
        start = (1 - move.row) * shard_rows
        half = up_mine.shape[1]
        w_upper = lax.dynamic_update_slice(up_base, theirs[:shard_rows], (start, 0))
        w_upper = lax.dynamic_update_slice(w_upper, theirs[shard_rows : 2 * shard_rows], (start, half))
        w_lower = lax.dynamic_update_slice_in_dim(
            down_base, theirs[2 * shard_rows :], (1 - move.row) * down_mine.shape[0], 0
        )
    else:
        w_upper = lax.all_to_all(up_mine, "fsdp", 1, 0, tiled=True).reshape(width, -1)
        w_lower = down_mine
    wide = w_upper.shape[1]
    quad_three, _ = move.quad_gather(three_low)
    if move.cube:
        quad_three = after(quad_three, got_branch, head_kv)
    hidden_pre = jnp.dot(quad_three, w_upper, preferred_element_type=full) + bias_up
    head_query = after(cross_query.reshape(H, depth, rows), quad_three)
    head_query = lax.all_to_all(head_query, HEADS, 0, 0, tiled=True)
    activated, back_gelu = jax.vjp(gelu_tanh, hidden_pre)
    act_low = activated.astype(low)
    grad_act = contract(grad_quad, w_lower, 1, 1)
    grad_hidden = back_gelu(grad_act)[0].astype(low)
    grad_three, met = move.quad_sum(contract(after(grad_hidden, head_query), w_upper, 1, 1).astype(low))

    grad_out = grad_low.astype(full)
    grad_b_lower = column_sums(grad_low)
    grad_w_lower = contract(after(act_low, met), grad_quad, 0, 0).astype(low)
    grad_b_upper = column_sums(grad_hidden)
    sent = ()
    if move.cube:
        lower = grad_w_lower.reshape(2, 2, 2, -1, width)
        sent_a, lower = move.send_half(lower, 2, move.row, lambda v: move.swap(v, "fsdp"))
        sent = (sent_a,)
    grad_three = move.quad_end(grad_three, sent)
    grad_ln_three, gain_three, shift_three = back_three(grad_three)
    grad_two = grad_out + grad_ln_three

    grad_two_low = grad_two.astype(low)
    grad_b_cout = column_sums(grad_two_low)
    grad_cross_att = contract(w_cout, grad_two_low, 1, 1).astype(low)
    cross_rows = grad_cross_att.reshape(H, depth, rows)
    deltas = jnp.sum(cross_rows.astype(full) * cross_exact.reshape(H, depth, rows), axis=1)
    lse_rows = cross_lse[:, 0:2].reshape(H, rows)
    extra = jnp.stack(in_thirds(lse_rows) + in_thirds(deltas), axis=1)
    extra = jnp.pad(extra, ((0, 0), (0, 10), (0, 0)))
    cross_rows = jnp.concatenate([cross_rows, extra], axis=1)
    grad_head = lax.all_to_all(cross_rows, HEADS, 0, 0, tiled=True)
    grad_w_upper = contract(after(quad_three, grad_cross_att), grad_hidden, 0, 0).astype(low)
    branch = jnp.dot(after(act_low, grad_cross_att), w_lower, preferred_element_type=full).astype(low)
    branch_sum = move.quad_direct(branch)
    sent_b = grad_w_upper
    if move.cube:
        upper = grad_w_upper.reshape(2, 2, 4, 2, -1, wide)
        sent_b, upper = move.send_half(upper, 3, move.row, lambda v: move.swap(v, "fsdp"))
    head_in = after(grad_head, head_query, head_kv, sent_b, group_one)
    head_cq, head_dkv_rows, packed_dkv = cross_backward(
        group_plan, query_slot, group_ranges, head_query, head_kv, head_in,
        low if parts == 1 else full, ctx_count,
    )
    if parts > 1:
        head_dkv_rows = lax.psum_scatter(head_dkv_rows, "part", scatter_dimension=0, tiled=True).astype(low)
    head_cq_sent = after(head_cq, lower[1]) if move.cube else head_cq
    grad_cq = lax.all_to_all(head_cq_sent, HEADS, 0, 0, tiled=True).reshape(width, rows)
    if move.cube:
        lower = move.add(lower, head_cq).astype(low)
        _, lower = move.send_half(lower, 1, move.near, lambda v: move.swap_chip(v, 2))
    grad_b_cq = jnp.sum(grad_cq.astype(full), axis=1)
    grad_ln_two, gain_two, shift_two = back_two(contract(grad_cq, w_cq, 0, 1))
    grad_one = grad_two + grad_ln_two

    grad_one_low = grad_one.astype(low)
    grad_b_out = column_sums(grad_one_low)
    grad_self_att = contract(w_out, grad_one_low, 1, 1).astype(low).reshape(H, depth, rows)
    grad_heads = lax.all_to_all(grad_self_att, HEADS, 0, 0, tiled=True)
    grad_w_cout = contract(after(cross_att, head_cq), grad_two_low, 1, 0).astype(low)
    grad_w_cq = contract(after(normed_two, grad_self_att), grad_cq, 0, 1).astype(low)
    grad_w_out = contract(after(self_att, grad_self_att), grad_one_low, 1, 0).astype(low)
    if move.cube:
        square = []
        for one in (grad_w_cout, grad_w_cq, grad_w_out):
            _, both = move.send_half(move.device_shape(one), 1, move.core, lambda v: move.swap(v, "core"))
            square.append(move.add(both).astype(low))
        sent_c, square = move.send_half(jnp.stack(square, axis=1), 2, move.row, lambda v: move.swap(v, "fsdp"))
        upper = move.add(upper, grad_self_att).astype(low)
        sent_b, upper = move.send_half(upper, 1, move.near, lambda v: move.swap_chip(v, 2))
        grad_heads = after(grad_heads, sent_b, sent_c)
    *head_grads, head_rows = self_backward(
        *self_args, grad_heads, self_exact, self_lse, low if parts == 1 else full, packed_dkv
    )
    if parts > 1:
        head_dkv = lax.psum_scatter(head_grads[1], "part", scatter_dimension=0, tiled=True).astype(low)
        head_grad = jnp.concatenate([head_grads[0], head_dkv], axis=1)
        head_rows = head_grad.transpose(1, 0, 2).reshape(3 * depth, H * rows)
        own_dkv = lax.all_to_all(head_dkv_rows.reshape(H, src_rows, 2 * depth), HEADS, 0, 0, tiled=True)
    else:
        head_grad = head_grads[0]
    if move.cube:
        head_grad = after(head_grad, upper[1], square[1])
    grad_qkv = lax.all_to_all(head_grad, HEADS, 0, 0, tiled=True)
    if parts == 1:
        packed = grad_qkv[:, 3 * depth :]
        own_dkv = jnp.concatenate([packed[:, :, : 2 * depth], packed[:, :, 2 * depth :]], axis=1)
        grad_qkv = grad_qkv[:, : 3 * depth]
    if move.cube:
        upper = move.add(upper, head_rows).astype(low)
        sent_b, upper = move.send_half(upper, 0, move.far, lambda v: move.swap_chip(v, 4))
        square = move.add(square, head_rows).astype(low)
        square = square.reshape((2, 2, 2) + square.shape[1:])
        sent_c, square = move.send_half(square, 2, move.chip & 1, lambda v: move.swap_chip(v, 1))
        soon = (sent_b, sent_c)
    else:
        soon = (head_rows,)
    head_w = contract(after(head_rows, *soon), group_one, 1, 0).astype(low)
    head_c = contract(group_source, after(head_dkv_rows, *soon), 0, 0).astype(low)
    flown = ()
    if move.cube:
        square = move.add(square, head_w).astype(low)
        sent_a, square = move.send_half(square, 1, move.near, lambda v: move.swap_chip(v, 2))
        flown = (sent_a,)
    grad_qkv = grad_qkv.reshape(H, 3, depth, rows).transpose(1, 0, 2, 3).reshape(3 * width, rows)
    grad_ln_one, gain_one, shift_one = back_one(contract(after(grad_qkv, *flown), w_qkv, 0, 1))
    grad_input = grad_one + grad_ln_one

    own_dk = own_dkv[:, :, :depth].transpose(1, 0, 2).reshape(src_rows, width)
    own_dv = own_dkv[:, :, depth:].transpose(1, 0, 2).reshape(src_rows, width)
    head_all = jnp.concatenate([head_w.T, head_c], axis=1)
    grad_source = contract(jnp.concatenate([own_dk, own_dv], axis=1), w_ckv, 1, 1)
    cols = head_all.shape[1]
    share = width // devices

    if not move.cube:
        lower_own = move.to_owner(move.chip_scatter(grad_w_lower).astype(low)).astype(full)
        upper_own = move.quad_columns(move.chip_scatter(grad_w_upper).astype(low)).astype(full)
        cout_own, cq_own, out_own = move.device_scatter([grad_w_cout, grad_w_cq, grad_w_out])

    head_sums = jnp.sum(head_rows.astype(full), axis=1)
    spread = [
        lax.dynamic_update_slice_in_dim(jnp.zeros((width,), full), part, head * depth, 0)
        for part in (head_sums[:depth], head_sums[2 * depth :], column_sums(head_dkv_rows[:, depth:]))
    ]
    early = [gain_two, gain_three, shift_two, shift_three, spread[0], spread[1],
             grad_b_out, grad_b_cq, spread[2], grad_b_cout, grad_b_lower]

    def by_owner(vectors):
        stacked = jnp.stack(vectors).reshape(len(vectors), devices, share)
        return stacked.transpose(1, 0, 2).reshape(devices, len(vectors) * share)

    def in_rows(values):
        count = -(-values.shape[1] // cols)
        values = jnp.pad(values, ((0, 0), (0, count * cols - values.shape[1])))
        return values.astype(low).reshape(devices, count, cols)

    hidden = wide * 2 * move.fsdp
    early_rows = in_rows(
        jnp.concatenate([by_owner(early), move.hidden_vector(grad_b_upper, hidden)], axis=1)
    )
    late_rows = in_rows(by_owner([gain_one, shift_one]))
    outgoing = jnp.concatenate(
        [head_all.reshape(devices, share, cols), early_rows, late_rows], axis=1
    )
    incoming = lax.all_to_all(outgoing, ALL, 0, 0, tiled=True)
    result = mixed_two + move.quad_total(branch_sum, soon) + bias_down
    if move.cube:
        lower = move.add(lower, outgoing).astype(low)
        _, lower = move.send_half(lower, 0, move.far, lambda v: move.swap_chip(v, 4))
        lower_own = move.add(lower, incoming)
        upper_own = move.corner_columns(move.add(upper, grad_ln_one).astype(low), (incoming,))
        square = move.add(square, outgoing).astype(low)
        _, square = move.send_half(square, 0, move.far, lambda v: move.swap_chip(v, 4))
        cout_own, cq_own, out_own = tuple(move.add(square, incoming))
    heads_in = incoming[:, :share].reshape(parts, H, move.fsdp, share, cols)
    qkv_own, ckv_own = owned_columns(heads_in, depth)
    tail = jnp.sum(incoming[:, share:].astype(full), axis=0)
    at = early_rows.shape[1]
    first = tail[:at].reshape(-1)
    vec = first[: 11 * share].reshape(11, share)
    bup_own = first[11 * share : 11 * share + hidden // devices]
    last = tail[at:].reshape(-1)[: 2 * share].reshape(2, share)
    return (
        result.astype(low)[None],
        grad_input[None],
        grad_source[None],
        jnp.stack([last[0], vec[0], vec[1]]),
        jnp.stack([last[1], vec[2], vec[3]]),
        vec[4:10].reshape(2, 3, share),
        qkv_own,
        out_own,
        cq_own,
        ckv_own,
        cout_own,
        upper_own,
        bup_own,
        lower_own,
        vec[10],
    )


def solution(mesh):
    ctx, fsdp = mesh.shape["ctx"], mesh.shape["fsdp"]
    inner = Mesh(mesh.devices.reshape(ctx // H, H // 2, 2, fsdp), ALL)
    tokens = P("fsdp", CTX, None)
    group = P("fsdp", None)
    owned = P(ALL, None)
    return jax.shard_map(
        per_device,
        mesh=inner,
        in_specs=(tokens,) * 3
        + (group,) * 4
        + (P(None, "fsdp"), P(None, "fsdp"), P(None, None, "fsdp"))
        + (group,) * 6
        + (P("fsdp"), group, P("fsdp")),
        out_specs=(tokens,) * 3
        + (P(None, ALL), P(None, ALL), P(None, None, ALL))
        + (owned,) * 6
        + (P(ALL), owned, P(ALL)),
        check_vma=False,
    )
```

```python
import functools

import jax
import jax.numpy as jnp
from jax import lax
from jax.experimental import pallas as pl
from jax.experimental.pallas import tpu as pltpu
from jax.sharding import Mesh
from jax.sharding import PartitionSpec as P

H = 16
BLOCK = 128

CHIP = ("part", "hc")
HEADS = ("hc", "core")
CTX = ("part", "hc", "core")
QUAD = ("core", "fsdp")
ALL = ("part", "hc", "core", "fsdp")

ln_eps = 1e-05
score_scale = 0.125
low = jnp.bfloat16
full = jnp.float32
SELF_TILES = (512, 512)
SELF_CHAINS = 1
CROSS_TILE = 1024
VMEM_BYTES = 56 * 1024 * 1024


def layer_norm(v, gain, shift):
    centred = v - jnp.mean(v, axis=-1, keepdims=True)
    spread = jnp.mean(centred * centred, axis=-1, keepdims=True)
    return centred * lax.rsqrt(spread + ln_eps) * gain + shift


def gelu_tanh(v):
    return 0.5 * v * (1.0 + jnp.tanh(0.7978845608028654 * (v + 0.044715 * v * v * v)))


def in_thirds(value):
    terms = []
    for _ in range(3):
        term = lax.reduce_precision(value, 8, 7)
        terms.append(term.astype(low))
        value = value - term
    return terms


def contract(left, right, left_dim, right_dim):
    return lax.dot_general(
        left, right, (((left_dim,), (right_dim,)), ((), ())), preferred_element_type=full
    )


def column_sums(values):
    return jnp.sum(values.astype(full), axis=0)


def plan_kernel(
    query_tile, self_key_tile, cross_key_tile, group_key_tile, cross_rows,
    order, flip, lengths, source_lengths, where,
    query_slot, key_slot, self_plan, cross_plan, group_plan, self_ranges, cross_ranges, group_ranges,
    block_of,
):
    pairs, documents = order.shape[0], lengths.shape[0]
    here, part = where[0], where[1]
    ends, source_ends = [], []
    for d in range(documents):
        ends.append(lengths[d] + (ends[-1] if d else 0))
        source_ends.append(source_lengths[d] + (source_ends[-1] if d else 0))

    def start_of(places):
        start = jnp.zeros_like(places)
        for end in ends:
            start = jnp.where(places >= end, end, start)
        return start

    def source_of(places):
        start, stop = jnp.zeros_like(places), jnp.zeros_like(places) + source_ends[0]
        for d in range(documents - 1):
            start = jnp.where(places >= ends[d], source_ends[d], start)
            stop = jnp.where(places >= ends[d], source_ends[d + 1], stop)
        return start, stop

    def stored(i):
        number = order[i >> 1]
        upper = (flip[i >> 1] + i) & 1 == 1
        return jnp.where(upper, 2 * pairs - 1 - number, number)

    @pl.loop(0, 2 * pairs)
    def _(i):
        key_slot[stored(i)] = i

    blocks = query_slot.shape[0]
    lanes = lax.broadcasted_iota(jnp.int32, (1, BLOCK), 1)

    def take(b, count):
        slot = key_slot[b] - part * blocks
        inside = (slot >= 0) & (slot < blocks)

        @pl.when(inside)
        def _():
            query_slot[count] = slot
            block_of[count] = b
            places = lanes + b * BLOCK
            self_ranges[0:1, tile_at(count, BLOCK)] = start_of(places)
            self_ranges[1:2, tile_at(count, BLOCK)] = places + 1
            start, stop = source_of(places)
            group_ranges[0:1, tile_at(count, BLOCK)] = start
            group_ranges[1:2, tile_at(count, BLOCK)] = stop

        return count + jnp.where(inside, 1, 0)

    lax.fori_loop(0, 2 * pairs, take, jnp.int32(0))

    def write(plan, t, low_start, high_start, low_stop, high_stop, key_tile):
        first = lax.div(low_start, key_tile)
        last = lax.div(high_stop + key_tile - 1, key_tile)
        inner = jnp.clip(lax.div(high_start + key_tile - 1, key_tile), first, last)
        plan[0, t] = first
        plan[1, t] = inner
        plan[2, t] = jnp.clip(lax.div(low_stop, key_tile), inner, last)
        plan[3, t] = last

    step = query_tile // BLOCK

    @pl.loop(0, blocks // step)
    def _(t):
        begin = block_of[t * step] * BLOCK
        end = block_of[t * step + step - 1] * BLOCK + BLOCK - 1
        write(self_plan, t, start_of(begin), start_of(end), begin + 1, end + 1, self_key_tile)
        first, last = source_of(begin), source_of(end)
        write(group_plan, t, first[0], last[0], first[1], last[1], group_key_tile)

    edges = []
    for k in range(cross_rows // BLOCK):
        begin = stored(here * (cross_rows // BLOCK) + k) * BLOCK
        low_edge, high_edge = source_of(begin), source_of(begin + BLOCK - 1)
        if k:
            edges = [
                jnp.minimum(edges[0], low_edge[0]), jnp.maximum(edges[1], high_edge[0]),
                jnp.minimum(edges[2], low_edge[1]), jnp.maximum(edges[3], high_edge[1]),
            ]
        else:
            edges = [low_edge[0], high_edge[0], low_edge[1], high_edge[1]]
        start, stop = source_of(lanes + begin)
        cross_ranges[0:1, k * BLOCK : (k + 1) * BLOCK] = start
        cross_ranges[1:2, k * BLOCK : (k + 1) * BLOCK] = stop
    write(cross_plan, 0, *edges, cross_key_tile)


def attention_plan(order, flip, lengths, source_lengths, here, part, parts, rows, sources):
    blocks = 2 * order.shape[0]
    mine = blocks // parts
    query_tile, key_tile = self_tiles(mine * BLOCK)
    group_key_tile = cross_tiles(mine * BLOCK, sources)[1]
    tiles = mine * BLOCK // query_tile
    shapes = ((mine,), (blocks,), (4, tiles), (4, 1), (4, tiles), (2, mine * BLOCK), (2, rows), (2, mine * BLOCK))
    return pl.pallas_call(
        functools.partial(plan_kernel, query_tile, key_tile, cross_tile(sources), group_key_tile, rows),
        out_shape=tuple(jax.ShapeDtypeStruct(shape, jnp.int32) for shape in shapes),
        in_specs=[smem()] * 5,
        out_specs=(smem(),) * 5 + (vmem(),) * 3,
        scratch_shapes=[pltpu.SMEM((mine,), jnp.int32)],
        compiler_params=params(),
        name="attention_plan",
    )(order, flip, lengths, source_lengths, jnp.stack([here, part]).astype(jnp.int32))


def over_tiles(plan, tile_number, step, carry):
    first, inner = plan[0, tile_number], plan[1, tile_number]
    outer, last = plan[2, tile_number], plan[3, tile_number]
    carry = lax.fori_loop(inner, outer, functools.partial(step, masked=False), carry)
    before = inner - first

    def edge(index, state):
        number = jnp.where(index < before, first + index, outer + index - before)
        return step(number, state, masked=True)

    return lax.fori_loop(0, before + last - outer, edge, carry)


def masked_scores(scores, number, tile, start, stop):
    keys = number * tile + lax.broadcasted_iota(jnp.int32, scores.shape, 0)
    return jnp.where((keys >= start) & (keys < stop), scores, -jnp.inf)


def forward_tiles(plan, number, queries, start, stop, keys_of, values_of, tile, depth):
    chains = range(len(queries))
    width = queries[0].shape[1]
    start, stop = as_list(start, len(queries)), as_list(stop, len(queries))

    def step(j, carry, masked):
        top, total, accum = carry
        scores = [contract(keys_of(j), queries[i], 1, 0) for i in chains]
        if masked:
            scores = [masked_scores(scores[i], j, tile, start[i], stop[i]) for i in chains]
        newtop = [jnp.maximum(top[i], jnp.max(scores[i], axis=0, keepdims=True)) for i in chains]
        weights = [jnp.exp(scores[i] - newtop[i]) for i in chains]
        factor = [jnp.exp(top[i] - newtop[i]) for i in chains]
        total = [total[i] * factor[i] + jnp.sum(weights[i], axis=0, keepdims=True) for i in chains]
        accum = [
            accum[i] * factor[i] + contract(values_of(j, i), weights[i].astype(low), 1, 0)
            for i in chains
        ]
        return newtop, total, accum

    carry = (
        [jnp.full((1, width), -1e30, full) for _ in chains],
        [jnp.zeros((1, width), full) for _ in chains],
        [jnp.zeros((depth, width), full) for _ in chains],
    )
    top, total, accum = over_tiles(plan, number, step, carry)
    return [accum[i] / total[i] for i in chains], [top[i] + jnp.log(total[i]) for i in chains]


def as_list(value, count):
    return value if isinstance(value, list) else [value] * count


def identity(size):
    rows = lax.broadcasted_iota(jnp.int32, (size, size), 0)
    cols = lax.broadcasted_iota(jnp.int32, (size, size), 1)
    return jnp.where(rows == cols, 1.0, 0.0).astype(low)


def flipped(eye, block):
    return contract(eye, block, 1, 1).astype(low)


def tile_at(number, size):
    return pl.ds(pl.multiple_of(number * size, size), size)


def half_at(slot):
    return pl.ds(pl.multiple_of((slot & 1) * BLOCK, BLOCK), BLOCK)


def self_forward_kernel(
    tiles, plan, query_slot, key_slot, range_ref, own_ref, all_ref,
    out_ref, exact_ref, lse_ref, query_s, key_s, value_s,
):
    query_tile, tile = tiles
    depth, queries = query_s.shape
    count = value_s.shape[1]

    @pl.loop(0, queries // BLOCK)
    def _(b):
        slot = query_slot[b]
        query_s[:, tile_at(b, BLOCK)] = own_ref[slot >> 1, 0:depth, half_at(slot)] * low(score_scale)

    @pl.loop(0, count // BLOCK)
    def _(b):
        slot = key_slot[b]
        block = all_ref[slot >> 1, depth : 2 * depth, half_at(slot)]
        key_s[tile_at(b, BLOCK), :] = block.T
        value_s[:, tile_at(b, BLOCK)] = all_ref[slot >> 1, 2 * depth : 3 * depth, half_at(slot)]

    chains = SELF_CHAINS
    lanes = query_tile // chains

    @pl.loop(0, queries // query_tile)
    def _(t):
        here = [pl.ds(pl.multiple_of(t * query_tile + i * lanes, lanes), lanes) for i in range(chains)]
        result, lse = forward_tiles(
            plan, t, [query_s[:, at] for at in here], [range_ref[0:1, at] for at in here],
            [range_ref[1:2, at] for at in here],
            lambda j: key_s[tile_at(j, tile), :], lambda j, i: value_s[:, tile_at(j, tile)],
            tile, depth,
        )
        for i in range(chains):
            exact_ref[:, here[i]] = result[i]
            lse_ref[0:1, here[i]] = lse[i]

    @pl.loop(0, queries // BLOCK)
    def _(b):
        slot = query_slot[b]
        out_ref[slot >> 1, :, half_at(slot)] = exact_ref[:, tile_at(b, BLOCK)].astype(low)


def self_backward_kernel(
    tiles, joined, plan, query_slot, key_slot, range_ref, own_ref, all_ref, grad_ref, exact_ref, lse_ref,
    *rest,
):
    if joined:
        carried_ref, dq_ref, *rest = rest
        dkv_ref = dq_ref
        dq_ref[:, dq_ref.shape[1] - carried_ref.shape[1] :, :] = carried_ref[...]
    else:
        dq_ref, dkv_ref, *rest = rest
    rows_ref, query_s, grad_s, key_s, keyt_s, value_s, dq_s, dk_s, dv_s = rest
    query_tile, tile = tiles
    depth, queries = query_s.shape
    count = keyt_s.shape[1]

    @pl.loop(0, queries // BLOCK)
    def _(b):
        slot = query_slot[b]
        query_s[:, tile_at(b, BLOCK)] = own_ref[slot >> 1, 0:depth, half_at(slot)] * low(score_scale)
        grad_s[:, tile_at(b, BLOCK)] = grad_ref[slot >> 1, :, half_at(slot)]

    @pl.loop(0, count // BLOCK)
    def _(b):
        slot = key_slot[b]
        block = all_ref[slot >> 1, depth : 2 * depth, half_at(slot)]
        keyt_s[:, tile_at(b, BLOCK)] = block
        key_s[tile_at(b, BLOCK), :] = block.T
        value_s[tile_at(b, BLOCK), :] = all_ref[slot >> 1, 2 * depth : 3 * depth, half_at(slot)].T

    dk_s[...] = jnp.zeros_like(dk_s)
    dv_s[...] = jnp.zeros_like(dv_s)

    @pl.loop(0, queries // query_tile)
    def _(t):
        here = tile_at(t, query_tile)
        query, grad = query_s[:, here], grad_s[:, here]
        start, stop = range_ref[0:1, here], range_ref[1:2, here]
        lse = lse_ref[0:1, here]
        delta = jnp.sum(grad.astype(full) * exact_ref[:, here], axis=0, keepdims=True)

        def step(j, dq, masked):
            there = tile_at(j, tile)
            scores = contract(key_s[there, :], query, 1, 0)
            if masked:
                scores = masked_scores(scores, j, tile, start, stop)
            probs = jnp.exp(scores - lse)
            dprobs = contract(value_s[there, :], grad, 1, 0)
            dscores = (probs * (dprobs - delta)).astype(low)
            dv_s[:, there] += contract(grad, probs.astype(low), 1, 1)
            dk_s[:, there] += contract(query, dscores, 1, 1)
            return dq + contract(keyt_s[:, there], dscores, 1, 0)

        dq_s[:, here] = over_tiles(plan, t, step, jnp.zeros((depth, query_tile), full))

    @pl.loop(0, queries // BLOCK)
    def _(b):
        slot = query_slot[b]
        dq = (dq_s[:, tile_at(b, BLOCK)] * score_scale).astype(low)
        dq_ref[slot >> 1, 0:depth, half_at(slot)] = dq
        rows_ref[0:depth, tile_at(slot, BLOCK)] = dq

    @pl.loop(0, count // BLOCK)
    def _(b):
        slot = key_slot[b]
        dk = dk_s[:, tile_at(b, BLOCK)].astype(dkv_ref.dtype)
        dv = dv_s[:, tile_at(b, BLOCK)].astype(dkv_ref.dtype)
        at = depth if joined else 0
        dkv_ref[slot >> 1, at : at + depth, half_at(slot)] = dk
        dkv_ref[slot >> 1, at + depth : at + 2 * depth, half_at(slot)] = dv
        if count == queries:
            rows_ref[depth : 2 * depth, tile_at(slot, BLOCK)] = dk.astype(low)
            rows_ref[2 * depth : 3 * depth, tile_at(slot, BLOCK)] = dv.astype(low)


def one_head(values, head, depth):
    rows = lax.broadcasted_iota(jnp.int32, values.shape, 0)
    inside = (rows >= head * depth) & (rows < (head + 1) * depth)
    return jnp.where(inside, values, jnp.zeros_like(values))


def cross_forward_kernel(
    tile, plan, range_ref, query_ref, key_ref, value_ref, out_ref, exact_ref, lse_ref, value_s
):
    depth = value_s.shape[0] // 2

    eye = identity(2 * depth)

    def turn(j, _):
        value_s[:, tile_at(j, tile)] = flipped(eye, value_ref[tile_at(j, tile), :])
        return 0

    lax.fori_loop(plan[0, 0], plan[3, 0], turn, 0)
    query = query_ref[...] * low(score_scale)
    rows = [pl.ds(head * depth, depth) for head in range(2)]
    result, lse = forward_tiles(
        plan, 0, [one_head(query, head, depth) for head in range(2)],
        range_ref[0:1, :], range_ref[1:2, :],
        lambda j: key_ref[tile_at(j, tile), :],
        lambda j, i: value_s[rows[i], tile_at(j, tile)],
        tile, depth,
    )
    for head in range(2):
        exact_ref[rows[head], :] = result[head]
        out_ref[rows[head], :] = result[head].astype(low)
        lse_ref[0, head : head + 1, :] = lse[head]


def cross_backward_kernel(
    tiles, plan, query_slot, range_ref, query_ref, keys_values_ref, grad_ref,
    dq_ref, dkv_ref, packed_ref, query_s, grad_s, keyt_s, dkv_s,
):
    query_tile, tile = tiles
    depth = query_ref.shape[1]
    queries = query_s.shape[1]
    eye = identity(2 * depth)

    @pl.loop(0, queries // BLOCK)
    def _(b):
        slot = query_slot[b]
        at, there = tile_at(b, BLOCK), half_at(slot)
        query_s[:, at] = query_ref[slot >> 1, :, there] * low(score_scale)
        grad_s[:, at] = grad_ref[slot >> 1, :, there]

    @pl.loop(0, keyt_s.shape[1] // tile)
    def _(j):
        at = tile_at(j, tile)
        keyt_s[:, at] = flipped(eye, keys_values_ref[at, :])[0:depth]

    dkv_s[...] = jnp.zeros_like(dkv_s)
    blank = jnp.zeros((depth, query_tile), low)

    @pl.loop(0, queries // query_tile)
    def _(t):
        here = tile_at(t, query_tile)
        grad = grad_s[0:depth, here]
        start, stop = range_ref[0:1, here], range_ref[1:2, here]
        extra = grad_s[depth : depth + 16, here].astype(full)
        lse = extra[0:1] + extra[1:2] + extra[2:3]
        delta = extra[3:4] + extra[4:5] + extra[5:6]
        wide_query = jnp.concatenate([query_s[:, here], blank], axis=0)
        wide_grad = jnp.concatenate([blank, grad], axis=0)
        sides = jnp.concatenate([wide_query, wide_grad], axis=1)

        def step(j, dq, masked):
            there = tile_at(j, tile)
            keys_values = keys_values_ref[there, :]
            scores = contract(keys_values, wide_query, 1, 0)
            if masked:
                scores = masked_scores(scores, j, tile, start, stop)
            probs = jnp.exp(scores - lse)
            dprobs = contract(keys_values, wide_grad, 1, 0)
            dscores = (probs * (dprobs - delta)).astype(low)
            both = jnp.concatenate([dscores, probs.astype(low)], axis=1)
            dkv_s[there, :] += contract(both, sides, 1, 1)
            return dq + contract(keyt_s[:, there], dscores, 1, 0)

        dq = over_tiles(plan, t, step, jnp.zeros((depth, query_tile), full))
        query_s[:, here] = (dq * score_scale).astype(low)

    @pl.loop(0, queries // BLOCK)
    def _(b):
        slot = query_slot[b]
        dq_ref[slot >> 1, :, half_at(slot)] = query_s[:, tile_at(b, BLOCK)]

    total = dkv_s[...].astype(dkv_ref.dtype)
    dkv_ref[...] = total
    devices, half, _ = packed_ref.shape
    total = total.reshape(devices, 2, half, 2 * depth)
    packed_ref[:, :, 0 : 2 * depth] = total[:, 0].astype(low)
    packed_ref[:, :, 2 * depth : 4 * depth] = total[:, 1].astype(low)


def smem():
    return pl.BlockSpec(memory_space=pltpu.SMEM)


def vmem():
    return pl.BlockSpec(memory_space=pltpu.VMEM)


def params():
    return pltpu.CompilerParams(vmem_limit_bytes=VMEM_BYTES)


def self_tiles(queries):
    return min(SELF_TILES[0], queries), min(SELF_TILES[1], queries)


def self_forward(plan, query_slot, key_slot, ranges, own, everyone):
    heads, three, rows = own.shape
    depth = three // 3
    queries, count = heads * rows, everyone.shape[0] * rows
    tile = self_tiles(queries)
    return pl.pallas_call(
        functools.partial(self_forward_kernel, tile),
        out_shape=(
            jax.ShapeDtypeStruct((heads, depth, rows), low),
            jax.ShapeDtypeStruct((depth, queries), full),
            jax.ShapeDtypeStruct((8, queries), full),
        ),
        in_specs=[smem()] * 3 + [vmem()] * 3,
        out_specs=(vmem(),) * 3,
        scratch_shapes=[
            pltpu.VMEM((depth, queries), low),
            pltpu.VMEM((count, depth), low),
            pltpu.VMEM((depth, count), low),
        ],
        compiler_params=params(),
        cost_estimate=pl.CostEstimate(flops=1, bytes_accessed=1, transcendentals=0),
        name="self_forward",
    )(plan, query_slot, key_slot, ranges, own, everyone)


def self_backward(plan, query_slot, key_slot, ranges, own, everyone, grad, exact, lse, kv_type, carried):
    heads, three, rows = own.shape
    depth = three // 3
    queries, count = heads * rows, everyone.shape[0] * rows
    tile = self_tiles(queries)
    joined = heads == everyone.shape[0]
    if joined:
        shapes = (jax.ShapeDtypeStruct((heads, 3 * depth + carried.shape[1], rows), low),)
        extra = (carried,)
    else:
        shapes = (
            jax.ShapeDtypeStruct((heads, depth, rows), low),
            jax.ShapeDtypeStruct((everyone.shape[0], 2 * depth, rows), kv_type),
        )
        extra = ()
    return pl.pallas_call(
        functools.partial(self_backward_kernel, tile, joined),
        out_shape=shapes + (jax.ShapeDtypeStruct((3 * depth, queries), low),),
        in_specs=[smem()] * 3 + [vmem()] * (6 + len(extra)),
        out_specs=(vmem(),) * (len(shapes) + 1),
        scratch_shapes=[
            pltpu.VMEM((depth, queries), low),
            pltpu.VMEM((depth, queries), low),
            pltpu.VMEM((count, depth), low),
            pltpu.VMEM((depth, count), low),
            pltpu.VMEM((count, depth), low),
            pltpu.VMEM((depth, queries), full),
            pltpu.VMEM((depth, count), full),
            pltpu.VMEM((depth, count), full),
        ],
        compiler_params=params(),
        cost_estimate=pl.CostEstimate(flops=1, bytes_accessed=1, transcendentals=0),
        name="self_backward",
    )(plan, query_slot, key_slot, ranges, own, everyone, grad, exact, lse, *extra)


def cross_tiles(queries, count):
    return min(512, queries), min(512, count)


def cross_tile(count):
    return min(CROSS_TILE, count)


def pair_spec(rows, cols):
    return pl.BlockSpec((rows, cols), lambda i: (i, 0))


def cross_forward(plan, ranges, query, keys_values):
    width, rows = query.shape
    count = keys_values.shape[0]
    pairs = H // 2
    wide = width // pairs
    return pl.pallas_call(
        functools.partial(cross_forward_kernel, cross_tile(count)),
        grid=(pairs,),
        out_shape=(
            jax.ShapeDtypeStruct((width, rows), low),
            jax.ShapeDtypeStruct((width, rows), full),
            jax.ShapeDtypeStruct((pairs, 8, rows), full),
        ),
        in_specs=[
            smem(),
            vmem(),
            pair_spec(wide, rows),
            pl.BlockSpec((count, wide), lambda i: (0, i)),
            pl.BlockSpec((count, wide), lambda i: (0, pairs + i)),
        ],
        out_specs=(
            pair_spec(wide, rows),
            pair_spec(wide, rows),
            pl.BlockSpec((1, 8, rows), lambda i: (i, 0, 0)),
        ),
        scratch_shapes=[pltpu.VMEM((wide, count), low)],
        compiler_params=params(),
        cost_estimate=pl.CostEstimate(flops=1, bytes_accessed=1, transcendentals=0),
        name="cross_forward",
    )(plan, ranges, query, keys_values, keys_values)


def cross_backward(plan, query_slot, ranges, query, keys_values, grad, kv_type, parts):
    heads, depth, rows = query.shape
    queries, count = heads * rows, keys_values.shape[0]
    return pl.pallas_call(
        functools.partial(cross_backward_kernel, cross_tiles(queries, count)),
        out_shape=(
            jax.ShapeDtypeStruct((heads, depth, rows), low),
            jax.ShapeDtypeStruct((count, 2 * depth), kv_type),
            jax.ShapeDtypeStruct((parts, count // parts // 2, 4 * depth), low),
        ),
        in_specs=[smem()] * 2 + [vmem()] * 4,
        out_specs=(vmem(),) * 3,
        scratch_shapes=[
            pltpu.VMEM((depth, queries), low),
            pltpu.VMEM((grad.shape[1], queries), low),
            pltpu.VMEM((depth, count), low),
            pltpu.VMEM((count, 2 * depth), full),
        ],
        compiler_params=params(),
        cost_estimate=pl.CostEstimate(flops=1, bytes_accessed=1, transcendentals=0),
        name="cross_backward",
    )(plan, query_slot, ranges, query, keys_values, grad)


def copy_kernel(_, value_ref, square_ref, row_ref):
    square_ref[...] = value_ref[...]
    row_ref[...] = value_ref[...]


def strided_columns(value, first, step, wide):
    rows, cols = value.shape
    count = cols // (step * wide)
    return pl.pallas_call(
        copy_kernel,
        out_shape=(
            jax.ShapeDtypeStruct((2 * rows, count // 2 * wide), value.dtype),
            jax.ShapeDtypeStruct((rows, count * wide), value.dtype),
        ),
        grid_spec=pltpu.PrefetchScalarGridSpec(
            num_scalar_prefetch=1,
            grid=(count,),
            in_specs=[pl.BlockSpec((rows, wide), lambda i, at: (0, i * step + at[0]))],
            out_specs=(
                pl.BlockSpec((rows, wide), lambda i, at: (i // 2, i % 2)),
                pl.BlockSpec((rows, wide), lambda i, at: (0, i)),
            ),
        ),
        compiler_params=params(),
        name="strided_columns",
    )(first.astype(jnp.int32).reshape(1), value)


def owned_kernel(depth, pieces_ref, qkv_ref, ckv_ref):
    _, heads, groups, share, _ = pieces_ref.shape
    width = heads * depth
    for head in range(heads):
        total = 0.0
        for p in range(pieces_ref.shape[0]):
            for g in range(groups):
                total = total + pieces_ref[p, head, g].astype(full)
        at = head * depth
        for i in range(3):
            qkv_ref[:, i * width + at : i * width + at + depth] = total[:, i * depth : (i + 1) * depth]
        for i in range(2):
            ckv_ref[:, i * width + at : i * width + at + depth] = total[:, (3 + i) * depth : (4 + i) * depth]


def owned_columns(pieces, depth):
    _, heads, _, share, _ = pieces.shape
    width = heads * depth
    return pl.pallas_call(
        functools.partial(owned_kernel, depth),
        out_shape=(
            jax.ShapeDtypeStruct((share, 3 * width), full),
            jax.ShapeDtypeStruct((share, 2 * width), full),
        ),
        in_specs=[vmem()],
        out_specs=(vmem(),) * 2,
        compiler_params=params(),
        name="owned_columns",
    )(pieces)


def after(value, *others):
    return lax.optimization_barrier((value,) + others)[0]


class Exchange:
    def __init__(self):
        self.fsdp = lax.axis_size("fsdp")
        self.chips = lax.axis_size(CHIP)
        self.core = lax.axis_index("core")
        self.row = lax.axis_index("fsdp")
        self.chip = lax.axis_index(CHIP)
        self.paired = self.fsdp == 2
        self.cube = self.paired and self.chips == 8
        self.near, self.far = (self.chip >> 1) & 1, self.chip >> 2
        self.corner = 2 * (self.chip & 1) + self.core

    def swap(self, value, axis):
        return lax.ppermute(value, axis, [(0, 1), (1, 0)])

    def swap_chip(self, value, bit):
        return lax.ppermute(value, CHIP, [(i, i ^ bit) for i in range(self.chips)])

    def own_piece(self, shard):
        piece = shard.shape[0] // 2
        return lax.dynamic_slice_in_dim(shard, self.core * piece, piece, 0)

    def fetch(self, mine, begin=()):
        if not self.paired:
            return lax.all_gather(mine, ("fsdp", "core"), axis=0, tiled=True)
        return self.swap(after(mine, *begin) if begin else mine, "fsdp")

    def place(self, base, across, corner):
        if not self.paired:
            return across
        piece = across.shape[0]
        start = (1 - self.row) * 2 * piece
        whole = lax.dynamic_update_slice_in_dim(base, across, start + self.core * piece, 0)
        return lax.dynamic_update_slice_in_dim(whole, corner, start + (1 - self.core) * piece, 0)

    def place_all(self, bases, across):
        corner = self.swap(across, "core") if self.paired else across
        placed, at = [], 0
        for base in bases:
            cols = slice(at, at + base.shape[1])
            placed.append(self.place(base, across[:, cols], corner[:, cols]))
            at += base.shape[1]
        return placed

    def gather_last(self, shard):
        if not self.paired:
            return lax.all_gather(shard, "fsdp", axis=shard.ndim - 1, tiled=True)
        other = self.swap(shard, "fsdp")
        return jnp.where(
            self.row == 0,
            jnp.concatenate([shard, other], axis=-1),
            jnp.concatenate([other, shard], axis=-1),
        )


    def hidden_parts(self, shard, axis):
        size = shard.shape[axis]
        if not self.cube:
            wide = size // 2
            return lax.dynamic_slice_in_dim(shard, self.core * wide, wide, axis)
        wide = size // 8
        parts = [
            lax.dynamic_slice_in_dim(shard, (4 * z + self.corner) * wide, wide, axis) for z in range(2)
        ]
        return jnp.concatenate(parts, axis=axis)

    def up_part(self, shard):
        rows, hidden = shard.shape
        if self.cube:
            return strided_columns(shard, self.corner, 4, hidden // 16)
        split = shard.reshape(rows, self.fsdp, 2, hidden // (2 * self.fsdp))
        mine = lax.dynamic_index_in_dim(split, self.core, 2, keepdims=False)
        return mine, mine

    def swap_beside(self, value):
        return self.swap_chip(value, 1) if self.cube else self.swap(value, "fsdp")

    def quad_gather(self, value, hold=()):
        if not self.paired:
            return lax.all_gather(value, QUAD, axis=0, tiled=True), ()
        across = self.swap_beside(value)
        held = after(across, *hold)
        beside = self.swap(value, "core")
        corner = self.swap(held, "core")
        return jnp.concatenate([value, beside, held, corner], axis=0), (across,)

    def quad_sum(self, value):
        if not self.paired:
            total = lax.psum_scatter(value, QUAD, scatter_dimension=0, tiled=True)
            return total.astype(full), total
        rows = value.shape[0] // 4
        parts = value.reshape(2, 2, rows, value.shape[1])
        theirs = self.swap(parts[:, 1], "core")
        both = parts[:, 0].astype(full) + theirs.astype(full)
        got = self.swap_beside(both[1].astype(low))
        return (both[0], got), theirs

    def quad_direct(self, value):
        if not self.paired:
            return lax.psum_scatter(value, QUAD, scatter_dimension=0, tiled=True).astype(full)
        rows = value.shape[0] // 4
        mine, beside, across, corner = [value[i * rows : (i + 1) * rows] for i in range(4)]
        if self.cube:
            moves = [(i, i ^ 3) for i in range(2 * self.chips)]
            far = lax.ppermute(corner, CTX, moves)
        else:
            far = lax.ppermute(corner, QUAD, [(i, 3 - i) for i in range(4)])
        return mine, self.swap(beside, "core"), self.swap_beside(across), far

    def quad_total(self, pending, hold):
        if not self.paired:
            return pending
        mine = after(pending[0], *hold)
        return sum(piece.astype(full) for piece in (mine,) + pending[1:])

    def quad_end(self, pending, hold=()):
        if not self.paired:
            return pending
        mine, got = pending
        return (after(mine, *hold) if hold else mine) + got.astype(full)

    def send_half(self, value, axis, bit, swap, *others):
        if others:
            value = after(value, *others)
        sent = lax.dynamic_index_in_dim(value, 1 - bit, axis, keepdims=False)
        kept = lax.dynamic_index_in_dim(value, bit, axis, keepdims=False)
        return sent, (kept, swap(sent))

    def add(self, halves, *others):
        kept, got = halves
        if others:
            kept = after(kept, *others)
        return kept.astype(full) + got.astype(full)

    def chip_step(self, value, number, *others):
        bit = (self.chip >> number) & 1
        return self.send_half(value, 2 - number, bit, lambda v: self.swap_chip(v, 1 << number), *others)

    def chip_shape(self, value):
        return value.reshape((2, 2, 2, value.shape[0] // 8) + value.shape[1:])

    def chip_scatter(self, value):
        return lax.psum_scatter(value, CHIP, scatter_dimension=0, tiled=True).astype(full)

    def device_shape(self, value):
        rows, cols = value.shape
        return value.reshape(self.chips, 2, self.fsdp, rows // (self.chips * 2 * self.fsdp), cols)

    def device_scatter(self, values):
        stacked = jnp.stack([self.device_shape(v) for v in values], axis=3)
        stacked = lax.psum_scatter(stacked, "core", scatter_dimension=1, tiled=True)
        stacked = lax.psum_scatter(stacked, "fsdp", scatter_dimension=2, tiled=True)
        stacked = lax.psum_scatter(stacked, CHIP, scatter_dimension=0, tiled=True)
        return [stacked[0, 0, 0, i].astype(full) for i in range(len(values))]

    def to_owner(self, value):
        chips, fsdp = self.chips, self.fsdp
        moves = []
        for chip in range(chips):
            for core in range(2):
                for row in range(fsdp):
                    moves.append(
                        ((chip * 2 + core) * fsdp + row, (row * 2 + core) * chips + chip)
                    )
        return lax.ppermute(value, ALL, moves)

    def quad_columns(self, value):
        quad = 2 * self.fsdp
        rows, wide = value.shape
        share = rows // quad
        value = lax.all_to_all(value, QUAD, 0, 1, tiled=True)
        value = value.reshape(share, 2, self.fsdp, wide).transpose(0, 2, 1, 3)
        return value.reshape(share, quad * wide)

    def corner_columns(self, value, hold):
        def block(bits):
            return lax.dynamic_index_in_dim(value, self.corner ^ bits, 0, keepdims=False)

        got = [
            block(0),
            self.swap(block(1), "core"),
            self.swap_chip(block(2), 1),
            lax.ppermute(block(3), CTX, [(i, i ^ 3) for i in range(2 * self.chips)]),
        ]
        got = [after(piece, *hold) for piece in got]
        got = [jnp.where(self.core == 0, got[i], got[i ^ 1]) for i in range(4)]
        got = [jnp.where(self.chip & 1 == 0, got[i], got[i ^ 2]) for i in range(4)]
        got = [piece.astype(full) for piece in got]
        step = value.shape[2] // 4
        return jnp.concatenate(
            [got[i][:, z * step : (z + 1) * step] for z in range(4) for i in range(4)], axis=1
        )

    def hidden_vector(self, value, hidden):
        devices = self.chips * 2 * self.fsdp
        if not self.cube:
            spread = jnp.zeros((hidden,), full)
            at = (self.row * 2 + self.core) * value.shape[0]
            return lax.dynamic_update_slice_in_dim(spread, value, at, 0).reshape(devices, -1)
        spread = jnp.zeros((4, 4, hidden // 16), full)
        spread = lax.dynamic_update_slice_in_dim(spread, value.reshape(4, 1, -1), self.corner, 1)
        return spread.reshape(devices, -1)


def per_device(
    tokens, encoder, cotangent, seq_lengths, source_lengths, pair_order, pair_flip,
    ln_gain, ln_bias, attn_bias, self_qkv, self_out, cross_q, cross_kv, cross_out,
    w_up, up_bias, w_down, down_bias,
):
    move = Exchange()
    resid = tokens[0].astype(full)
    source = encoder[0]
    grad_low = cotangent[0]
    rows, width = resid.shape
    src_rows = source.shape[0]
    depth = width // H
    ctx_count = lax.axis_size(CTX)
    parts = lax.axis_size("part")
    devices = ctx_count * move.fsdp
    here = lax.axis_index(CTX)
    part = lax.axis_index("part")

    plan = attention_plan(
        pair_order[0], pair_flip[0], seq_lengths[0], source_lengths[0],
        here, part, parts, rows, src_rows * ctx_count,
    )
    query_slot, key_slot, self_plan, cross_plan, group_plan, self_ranges, cross_ranges, group_ranges = plan

    small = [ln_gain, ln_bias, attn_bias.reshape(6, -1), down_bias[None]]
    bias_up = move.hidden_parts(up_bias, 0)
    if move.cube:
        small.append(bias_up.reshape(2, -1))
    small = move.gather_last(jnp.concatenate(small, axis=0)).astype(full)
    if move.cube:
        half = small.shape[1] // 2
        bias_up = jnp.concatenate([small[13, :half], small[14, :half], small[13, half:], small[14, half:]])
    bias_up = bias_up.astype(full)
    gains, shifts, biases, bias_down = small[0:3], small[3:6], small[6:12].reshape(2, 3, width), small[12]
    shards = (cross_kv, self_out, cross_q, cross_out)
    middle = jnp.concatenate([move.own_piece(w) for w in shards], axis=1)
    qkv_piece = move.own_piece(self_qkv)
    bases = [jnp.concatenate([w, w], axis=0) if move.paired else w for w in shards]
    qkv_base = jnp.concatenate([self_qkv, self_qkv], axis=0) if move.paired else self_qkv
    up_mine, up_local = move.up_part(w_up)
    down_mine = move.hidden_parts(w_down, 0)
    if move.cube:
        shard_rows = w_up.shape[0]
        branch_piece = jnp.concatenate([up_mine, down_mine], axis=0)
        up_base = jnp.concatenate([up_local, up_local], axis=0)
        down_base = jnp.concatenate([down_mine, down_mine], axis=0)
        later = (up_base, down_base, branch_piece)
    else:
        later = ()

    got_qkv = move.fetch(qkv_piece)
    group_source = lax.all_gather(source, HEADS, axis=0, tiled=True)

    norm_one, back_one = jax.vjp(layer_norm, resid, gains[0], shifts[0])
    normed_one = norm_one.astype(low)
    w_qkv, = move.place_all([qkv_base], after(got_qkv, *plan, *bases, middle, up_mine))
    projected = contract(w_qkv, normed_one, 0, 1)
    shift_qkv = jnp.concatenate([biases[0, 0], jnp.zeros((width,), full), biases[0, 1]])
    projected = (projected + shift_qkv[:, None]).astype(low)
    projected = projected.reshape(3, H, depth, rows).transpose(1, 0, 2, 3).reshape(H, 3 * depth, rows)
    own_heads = lax.all_to_all(projected, HEADS, 0, 0, tiled=True)

    got_middle = move.fetch(middle, (got_qkv,))
    self_in = after(own_heads, *later)
    all_heads = self_in if parts == 1 else lax.all_gather(self_in, "part", axis=0, tiled=True)
    self_args = (self_plan, query_slot, key_slot, self_ranges, self_in, all_heads)
    self_low, self_exact, self_lse = self_forward(*self_args)
    self_att = lax.all_to_all(self_low, HEADS, 0, 0, tiled=True).reshape(width, rows)
    w_ckv, w_out, w_cq, w_cout = move.place_all(bases, after(got_middle, self_low))
    grad_quad, got_quad = move.quad_gather(after(grad_low, self_low), (self_att,))

    every_source = group_source
    if parts > 1:
        every_source = lax.all_gather(group_source, "part", axis=0, tiled=True)
    shift_ckv = jnp.concatenate([jnp.zeros((width,), full), biases[1, 1]])
    src_kv = (jnp.dot(every_source, w_ckv, preferred_element_type=full) + shift_ckv).astype(low)
    mixed_one = resid + contract(self_att, w_out, 0, 0) + biases[0, 2]

    norm_two, back_two = jax.vjp(layer_norm, mixed_one, gains[1], shifts[1])
    normed_two = norm_two.astype(low)
    cross_query = (contract(w_cq, normed_two, 0, 1) + biases[1, 0][:, None]).astype(low)
    cross_query = after(cross_query, *got_quad) if move.cube else cross_query
    group_one = lax.all_gather(after(norm_one, self_att).astype(low), HEADS, axis=0, tiled=True)
    cross_att, cross_exact, cross_lse = cross_forward(cross_plan, cross_ranges, cross_query, src_kv)
    mixed_two = mixed_one + contract(cross_att, w_cout, 0, 0) + biases[1, 2]

    head = lax.axis_index(HEADS)
    head_cols = [
        lax.dynamic_slice_in_dim(w_ckv, i * width + head * depth, depth, 1) for i in range(2)
    ]
    head_shift = jnp.concatenate(
        [jnp.zeros((depth,), full), lax.dynamic_slice_in_dim(biases[1, 1], head * depth, depth, 0)]
    )
    head_kv = jnp.dot(after(every_source, cross_att), jnp.concatenate(head_cols, axis=1), preferred_element_type=full)
    head_kv = (head_kv + head_shift).astype(low)

    norm_three, back_three = jax.vjp(layer_norm, mixed_two, gains[2], shifts[2])
    three_low = norm_three.astype(low)
    if move.cube:
        got_branch = move.swap(after(branch_piece, got_middle), "fsdp")
        theirs = after(got_branch, cross_att)
        start = (1 - move.row) * shard_rows
        half = up_mine.shape[1]
        w_upper = lax.dynamic_update_slice(up_base, theirs[:shard_rows], (start, 0))
        w_upper = lax.dynamic_update_slice(w_upper, theirs[shard_rows : 2 * shard_rows], (start, half))
        w_lower = lax.dynamic_update_slice_in_dim(
            down_base, theirs[2 * shard_rows :], (1 - move.row) * down_mine.shape[0], 0
        )
    else:
        w_upper = lax.all_to_all(up_mine, "fsdp", 1, 0, tiled=True).reshape(width, -1)
        w_lower = down_mine
    wide = w_upper.shape[1]
    quad_three, _ = move.quad_gather(three_low)
    if move.cube:
        quad_three = after(quad_three, got_branch, head_kv)
    hidden_pre = jnp.dot(quad_three, w_upper, preferred_element_type=full) + bias_up
    head_query = after(cross_query.reshape(H, depth, rows), quad_three)
    head_query = lax.all_to_all(head_query, HEADS, 0, 0, tiled=True)
    activated, back_gelu = jax.vjp(gelu_tanh, hidden_pre)
    act_low = activated.astype(low)
    grad_act = contract(grad_quad, w_lower, 1, 1)
    grad_hidden = back_gelu(grad_act)[0].astype(low)
    grad_three, met = move.quad_sum(contract(after(grad_hidden, head_query), w_upper, 1, 1).astype(low))

    grad_out = grad_low.astype(full)
    grad_b_lower = column_sums(grad_low)
    grad_w_lower = contract(after(act_low, met), grad_quad, 0, 0).astype(low)
    grad_b_upper = column_sums(grad_hidden)
    sent = ()
    if move.cube:
        lower = grad_w_lower.reshape(2, 2, 2, -1, width)
        sent_a, lower = move.send_half(lower, 2, move.row, lambda v: move.swap(v, "fsdp"))
        sent = (sent_a,)
    grad_three = move.quad_end(grad_three, sent)
    grad_ln_three, gain_three, shift_three = back_three(grad_three)
    grad_two = grad_out + grad_ln_three

    grad_two_low = grad_two.astype(low)
    grad_b_cout = column_sums(grad_two_low)
    grad_cross_att = contract(w_cout, grad_two_low, 1, 1).astype(low)
    cross_rows = grad_cross_att.reshape(H, depth, rows)
    deltas = jnp.sum(cross_rows.astype(full) * cross_exact.reshape(H, depth, rows), axis=1)
    lse_rows = cross_lse[:, 0:2].reshape(H, rows)
    extra = jnp.stack(in_thirds(lse_rows) + in_thirds(deltas), axis=1)
    extra = jnp.pad(extra, ((0, 0), (0, 10), (0, 0)))
    cross_rows = jnp.concatenate([cross_rows, extra], axis=1)
    grad_head = lax.all_to_all(cross_rows, HEADS, 0, 0, tiled=True)
    grad_w_upper = contract(after(quad_three, grad_cross_att), grad_hidden, 0, 0).astype(low)
    branch = jnp.dot(after(act_low, grad_cross_att), w_lower, preferred_element_type=full).astype(low)
    branch_sum = move.quad_direct(branch)
    sent_b = grad_w_upper
    if move.cube:
        upper = grad_w_upper.reshape(2, 2, 4, 2, -1, wide)
        sent_b, upper = move.send_half(upper, 3, move.row, lambda v: move.swap(v, "fsdp"))
    head_in = after(grad_head, head_query, head_kv, sent_b, group_one)
    head_cq, head_dkv_rows, packed_dkv = cross_backward(
        group_plan, query_slot, group_ranges, head_query, head_kv, head_in,
        low if parts == 1 else full, ctx_count,
    )
    if parts > 1:
        head_dkv_rows = lax.psum_scatter(head_dkv_rows, "part", scatter_dimension=0, tiled=True).astype(low)
    head_cq_sent = after(head_cq, lower[1]) if move.cube else head_cq
    grad_cq = lax.all_to_all(head_cq_sent, HEADS, 0, 0, tiled=True).reshape(width, rows)
    if move.cube:
        lower = move.add(lower, head_cq).astype(low)
        _, lower = move.send_half(lower, 1, move.near, lambda v: move.swap_chip(v, 2))
    grad_b_cq = jnp.sum(grad_cq.astype(full), axis=1)
    grad_ln_two, gain_two, shift_two = back_two(contract(grad_cq, w_cq, 0, 1))
    grad_one = grad_two + grad_ln_two

    grad_one_low = grad_one.astype(low)
    grad_b_out = column_sums(grad_one_low)
    grad_self_att = contract(w_out, grad_one_low, 1, 1).astype(low).reshape(H, depth, rows)
    grad_heads = lax.all_to_all(grad_self_att, HEADS, 0, 0, tiled=True)
    grad_w_cout = contract(after(cross_att, head_cq), grad_two_low, 1, 0).astype(low)
    grad_w_cq = contract(after(normed_two, grad_self_att), grad_cq, 0, 1).astype(low)
    grad_w_out = contract(after(self_att, grad_self_att), grad_one_low, 1, 0).astype(low)
    if move.cube:
        square = []
        for one in (grad_w_cout, grad_w_cq, grad_w_out):
            _, both = move.send_half(move.device_shape(one), 1, move.core, lambda v: move.swap(v, "core"))
            square.append(move.add(both).astype(low))
        sent_c, square = move.send_half(jnp.stack(square, axis=1), 2, move.row, lambda v: move.swap(v, "fsdp"))
        upper = move.add(upper, grad_self_att).astype(low)
        sent_b, upper = move.send_half(upper, 1, move.near, lambda v: move.swap_chip(v, 2))
        grad_heads = after(grad_heads, sent_b, sent_c)
    *head_grads, head_rows = self_backward(
        *self_args, grad_heads, self_exact, self_lse, low if parts == 1 else full, packed_dkv
    )
    if parts > 1:
        head_dkv = lax.psum_scatter(head_grads[1], "part", scatter_dimension=0, tiled=True).astype(low)
        head_grad = jnp.concatenate([head_grads[0], head_dkv], axis=1)
        head_rows = head_grad.transpose(1, 0, 2).reshape(3 * depth, H * rows)
        own_dkv = lax.all_to_all(head_dkv_rows.reshape(H, src_rows, 2 * depth), HEADS, 0, 0, tiled=True)
    else:
        head_grad = head_grads[0]
    if move.cube:
        head_grad = after(head_grad, upper[1], square[1])
    grad_qkv = lax.all_to_all(head_grad, HEADS, 0, 0, tiled=True)
    if parts == 1:
        packed = grad_qkv[:, 3 * depth :]
        own_dkv = jnp.concatenate([packed[:, :, : 2 * depth], packed[:, :, 2 * depth :]], axis=1)
        grad_qkv = grad_qkv[:, : 3 * depth]
    if move.cube:
        upper = move.add(upper, head_rows).astype(low)
        sent_b, upper = move.send_half(upper, 0, move.far, lambda v: move.swap_chip(v, 4))
        square = move.add(square, head_rows).astype(low)
        square = square.reshape((2, 2, 2) + square.shape[1:])
        sent_c, square = move.send_half(square, 2, move.chip & 1, lambda v: move.swap_chip(v, 1))
        soon = (sent_b, sent_c)
    else:
        soon = (head_rows,)
    head_w = contract(after(head_rows, *soon), group_one, 1, 0).astype(low)
    head_c = contract(group_source, after(head_dkv_rows, *soon), 0, 0).astype(low)
    flown = ()
    if move.cube:
        square = move.add(square, head_w).astype(low)
        sent_a, square = move.send_half(square, 1, move.near, lambda v: move.swap_chip(v, 2))
        lower = move.add(lower, head_c).astype(low)
        sent_b, lower = move.send_half(lower, 0, move.far, lambda v: move.swap_chip(v, 4))
        flown = (sent_a, sent_b)
    grad_qkv = grad_qkv.reshape(H, 3, depth, rows).transpose(1, 0, 2, 3).reshape(3 * width, rows)
    grad_ln_one, gain_one, shift_one = back_one(contract(after(grad_qkv, *flown), w_qkv, 0, 1))
    grad_input = grad_one + grad_ln_one

    own_dk = own_dkv[:, :, :depth].transpose(1, 0, 2).reshape(src_rows, width)
    own_dv = own_dkv[:, :, depth:].transpose(1, 0, 2).reshape(src_rows, width)
    head_all = jnp.concatenate([head_w.T, head_c], axis=1)
    grad_source = contract(jnp.concatenate([own_dk, own_dv], axis=1), w_ckv, 1, 1)
    cols = head_all.shape[1]
    share = width // devices

    if not move.cube:
        lower_own = move.to_owner(move.chip_scatter(grad_w_lower).astype(low)).astype(full)
        upper_own = move.quad_columns(move.chip_scatter(grad_w_upper).astype(low)).astype(full)
        cout_own, cq_own, out_own = move.device_scatter([grad_w_cout, grad_w_cq, grad_w_out])

    head_sums = jnp.sum(head_rows.astype(full), axis=1)
    spread = [
        lax.dynamic_update_slice_in_dim(jnp.zeros((width,), full), part, head * depth, 0)
        for part in (head_sums[:depth], head_sums[2 * depth :], column_sums(head_dkv_rows[:, depth:]))
    ]
    early = [gain_two, gain_three, shift_two, shift_three, spread[0], spread[1],
             grad_b_out, grad_b_cq, spread[2], grad_b_cout, grad_b_lower]

    def by_owner(vectors):
        stacked = jnp.stack(vectors).reshape(len(vectors), devices, share)
        return stacked.transpose(1, 0, 2).reshape(devices, len(vectors) * share)

    def in_rows(values):
        count = -(-values.shape[1] // cols)
        values = jnp.pad(values, ((0, 0), (0, count * cols - values.shape[1])))
        return values.astype(low).reshape(devices, count, cols)

    hidden = wide * 2 * move.fsdp
    early_rows = in_rows(
        jnp.concatenate([by_owner(early), move.hidden_vector(grad_b_upper, hidden)], axis=1)
    )
    late_rows = in_rows(by_owner([gain_one, shift_one]))
    outgoing = jnp.concatenate(
        [head_all.reshape(devices, share, cols), early_rows, late_rows], axis=1
    )
    incoming = lax.all_to_all(outgoing, ALL, 0, 0, tiled=True)
    result = mixed_two + move.quad_total(branch_sum, soon) + bias_down
    if move.cube:
        lower_own = move.add(lower, incoming)
        upper_own = move.corner_columns(move.add(upper, grad_ln_one).astype(low), (incoming,))
        square = move.add(square, outgoing).astype(low)
        _, square = move.send_half(square, 0, move.far, lambda v: move.swap_chip(v, 4))
        cout_own, cq_own, out_own = tuple(move.add(square, incoming))
    heads_in = incoming[:, :share].reshape(parts, H, move.fsdp, share, cols)
    qkv_own, ckv_own = owned_columns(heads_in, depth)
    tail = jnp.sum(incoming[:, share:].astype(full), axis=0)
    at = early_rows.shape[1]
    first = tail[:at].reshape(-1)
    vec = first[: 11 * share].reshape(11, share)
    bup_own = first[11 * share : 11 * share + hidden // devices]
    last = tail[at:].reshape(-1)[: 2 * share].reshape(2, share)
    return (
        result.astype(low)[None],
        grad_input[None],
        grad_source[None],
        jnp.stack([last[0], vec[0], vec[1]]),
        jnp.stack([last[1], vec[2], vec[3]]),
        vec[4:10].reshape(2, 3, share),
        qkv_own,
        out_own,
        cq_own,
        ckv_own,
        cout_own,
        upper_own,
        bup_own,
        lower_own,
        vec[10],
    )


def solution(mesh):
    ctx, fsdp = mesh.shape["ctx"], mesh.shape["fsdp"]
    inner = Mesh(mesh.devices.reshape(ctx // H, H // 2, 2, fsdp), ALL)
    tokens = P("fsdp", CTX, None)
    group = P("fsdp", None)
    owned = P(ALL, None)
    return jax.shard_map(
        per_device,
        mesh=inner,
        in_specs=(tokens,) * 3
        + (group,) * 4
        + (P(None, "fsdp"), P(None, "fsdp"), P(None, None, "fsdp"))
        + (group,) * 6
        + (P("fsdp"), group, P("fsdp")),
        out_specs=(tokens,) * 3
        + (P(None, ALL), P(None, ALL), P(None, None, ALL))
        + (owned,) * 6
        + (P(ALL), owned, P(ALL)),
        check_vma=False,
    )
```

```python
import functools

import jax
import jax.numpy as jnp
from jax import lax
from jax.experimental import pallas as pl
from jax.experimental.pallas import tpu as pltpu
from jax.sharding import Mesh
from jax.sharding import PartitionSpec as P

H = 16
BLOCK = 128

CHIP = ("part", "hc")
HEADS = ("hc", "core")
CTX = ("part", "hc", "core")
QUAD = ("core", "fsdp")
ALL = ("part", "hc", "core", "fsdp")

ln_eps = 1e-05
score_scale = 0.125
low = jnp.bfloat16
full = jnp.float32
SELF_TILES = (512, 512)
SELF_CHAINS = 1
CROSS_TILE = 1024
VMEM_BYTES = 56 * 1024 * 1024


def layer_norm(v, gain, shift):
    centred = v - jnp.mean(v, axis=-1, keepdims=True)
    spread = jnp.mean(centred * centred, axis=-1, keepdims=True)
    return centred * lax.rsqrt(spread + ln_eps) * gain + shift


def gelu_tanh(v):
    return 0.5 * v * (1.0 + jnp.tanh(0.7978845608028654 * (v + 0.044715 * v * v * v)))


def in_thirds(value):
    terms = []
    for _ in range(3):
        term = lax.reduce_precision(value, 8, 7)
        terms.append(term.astype(low))
        value = value - term
    return terms


def contract(left, right, left_dim, right_dim):
    return lax.dot_general(
        left, right, (((left_dim,), (right_dim,)), ((), ())), preferred_element_type=full
    )


def column_sums(values):
    return jnp.sum(values.astype(full), axis=0)


def plan_kernel(
    query_tile, self_key_tile, cross_key_tile, group_key_tile, cross_rows,
    order, flip, lengths, source_lengths, where,
    query_slot, key_slot, self_plan, cross_plan, group_plan, self_ranges, cross_ranges, group_ranges,
    block_of,
):
    pairs, documents = order.shape[0], lengths.shape[0]
    here, part = where[0], where[1]
    ends, source_ends = [], []
    for d in range(documents):
        ends.append(lengths[d] + (ends[-1] if d else 0))
        source_ends.append(source_lengths[d] + (source_ends[-1] if d else 0))

    def start_of(places):
        start = jnp.zeros_like(places)
        for end in ends:
            start = jnp.where(places >= end, end, start)
        return start

    def source_of(places):
        start, stop = jnp.zeros_like(places), jnp.zeros_like(places) + source_ends[0]
        for d in range(documents - 1):
            start = jnp.where(places >= ends[d], source_ends[d], start)
            stop = jnp.where(places >= ends[d], source_ends[d + 1], stop)
        return start, stop

    def stored(i):
        number = order[i >> 1]
        upper = (flip[i >> 1] + i) & 1 == 1
        return jnp.where(upper, 2 * pairs - 1 - number, number)

    @pl.loop(0, 2 * pairs)
    def _(i):
        key_slot[stored(i)] = i

    blocks = query_slot.shape[0]
    lanes = lax.broadcasted_iota(jnp.int32, (1, BLOCK), 1)

    def take(b, count):
        slot = key_slot[b] - part * blocks
        inside = (slot >= 0) & (slot < blocks)

        @pl.when(inside)
        def _():
            query_slot[count] = slot
            block_of[count] = b
            places = lanes + b * BLOCK
            self_ranges[0:1, tile_at(count, BLOCK)] = start_of(places)
            self_ranges[1:2, tile_at(count, BLOCK)] = places + 1
            start, stop = source_of(places)
            group_ranges[0:1, tile_at(count, BLOCK)] = start
            group_ranges[1:2, tile_at(count, BLOCK)] = stop

        return count + jnp.where(inside, 1, 0)

    lax.fori_loop(0, 2 * pairs, take, jnp.int32(0))

    def write(plan, t, low_start, high_start, low_stop, high_stop, key_tile):
        first = lax.div(low_start, key_tile)
        last = lax.div(high_stop + key_tile - 1, key_tile)
        inner = jnp.clip(lax.div(high_start + key_tile - 1, key_tile), first, last)
        plan[0, t] = first
        plan[1, t] = inner
        plan[2, t] = jnp.clip(lax.div(low_stop, key_tile), inner, last)
        plan[3, t] = last

    step = query_tile // BLOCK

    @pl.loop(0, blocks // step)
    def _(t):
        begin = block_of[t * step] * BLOCK
        end = block_of[t * step + step - 1] * BLOCK + BLOCK - 1
        write(self_plan, t, start_of(begin), start_of(end), begin + 1, end + 1, self_key_tile)
        first, last = source_of(begin), source_of(end)
        write(group_plan, t, first[0], last[0], first[1], last[1], group_key_tile)

    edges = []
    for k in range(cross_rows // BLOCK):
        begin = stored(here * (cross_rows // BLOCK) + k) * BLOCK
        low_edge, high_edge = source_of(begin), source_of(begin + BLOCK - 1)
        if k:
            edges = [
                jnp.minimum(edges[0], low_edge[0]), jnp.maximum(edges[1], high_edge[0]),
                jnp.minimum(edges[2], low_edge[1]), jnp.maximum(edges[3], high_edge[1]),
            ]
        else:
            edges = [low_edge[0], high_edge[0], low_edge[1], high_edge[1]]
        start, stop = source_of(lanes + begin)
        cross_ranges[0:1, k * BLOCK : (k + 1) * BLOCK] = start
        cross_ranges[1:2, k * BLOCK : (k + 1) * BLOCK] = stop
    write(cross_plan, 0, *edges, cross_key_tile)


def attention_plan(order, flip, lengths, source_lengths, here, part, parts, rows, sources):
    blocks = 2 * order.shape[0]
    mine = blocks // parts
    query_tile, key_tile = self_tiles(mine * BLOCK)
    group_key_tile = cross_tiles(mine * BLOCK, sources)[1]
    tiles = mine * BLOCK // query_tile
    shapes = ((mine,), (blocks,), (4, tiles), (4, 1), (4, tiles), (2, mine * BLOCK), (2, rows), (2, mine * BLOCK))
    return pl.pallas_call(
        functools.partial(plan_kernel, query_tile, key_tile, cross_tile(sources), group_key_tile, rows),
        out_shape=tuple(jax.ShapeDtypeStruct(shape, jnp.int32) for shape in shapes),
        in_specs=[smem()] * 5,
        out_specs=(smem(),) * 5 + (vmem(),) * 3,
        scratch_shapes=[pltpu.SMEM((mine,), jnp.int32)],
        compiler_params=params(),
        name="attention_plan",
    )(order, flip, lengths, source_lengths, jnp.stack([here, part]).astype(jnp.int32))


def over_tiles(plan, tile_number, step, carry):
    first, inner = plan[0, tile_number], plan[1, tile_number]
    outer, last = plan[2, tile_number], plan[3, tile_number]
    carry = lax.fori_loop(inner, outer, functools.partial(step, masked=False), carry)
    before = inner - first

    def edge(index, state):
        number = jnp.where(index < before, first + index, outer + index - before)
        return step(number, state, masked=True)

    return lax.fori_loop(0, before + last - outer, edge, carry)


def masked_scores(scores, number, tile, start, stop):
    keys = number * tile + lax.broadcasted_iota(jnp.int32, scores.shape, 0)
    return jnp.where((keys >= start) & (keys < stop), scores, -jnp.inf)


def forward_tiles(plan, number, queries, start, stop, keys_of, values_of, tile, depth):
    chains = range(len(queries))
    width = queries[0].shape[1]
    start, stop = as_list(start, len(queries)), as_list(stop, len(queries))

    def step(j, carry, masked):
        top, total, accum = carry
        scores = [contract(keys_of(j), queries[i], 1, 0) for i in chains]
        if masked:
            scores = [masked_scores(scores[i], j, tile, start[i], stop[i]) for i in chains]
        newtop = [jnp.maximum(top[i], jnp.max(scores[i], axis=0, keepdims=True)) for i in chains]
        weights = [jnp.exp(scores[i] - newtop[i]) for i in chains]
        factor = [jnp.exp(top[i] - newtop[i]) for i in chains]
        total = [total[i] * factor[i] + jnp.sum(weights[i], axis=0, keepdims=True) for i in chains]
        accum = [
            accum[i] * factor[i] + contract(values_of(j, i), weights[i].astype(low), 1, 0)
            for i in chains
        ]
        return newtop, total, accum

    carry = (
        [jnp.full((1, width), -1e30, full) for _ in chains],
        [jnp.zeros((1, width), full) for _ in chains],
        [jnp.zeros((depth, width), full) for _ in chains],
    )
    top, total, accum = over_tiles(plan, number, step, carry)
    return [accum[i] / total[i] for i in chains], [top[i] + jnp.log(total[i]) for i in chains]


def as_list(value, count):
    return value if isinstance(value, list) else [value] * count


def identity(size):
    rows = lax.broadcasted_iota(jnp.int32, (size, size), 0)
    cols = lax.broadcasted_iota(jnp.int32, (size, size), 1)
    return jnp.where(rows == cols, 1.0, 0.0).astype(low)


def flipped(eye, block):
    return contract(eye, block, 1, 1).astype(low)


def tile_at(number, size):
    return pl.ds(pl.multiple_of(number * size, size), size)


def half_at(slot):
    return pl.ds(pl.multiple_of((slot & 1) * BLOCK, BLOCK), BLOCK)


def self_forward_kernel(
    tiles, plan, query_slot, key_slot, range_ref, own_ref, all_ref,
    out_ref, exact_ref, lse_ref, query_s, key_s, value_s,
):
    query_tile, tile = tiles
    depth, queries = query_s.shape
    count = value_s.shape[1]

    @pl.loop(0, queries // BLOCK)
    def _(b):
        slot = query_slot[b]
        query_s[:, tile_at(b, BLOCK)] = own_ref[slot >> 1, 0:depth, half_at(slot)] * low(score_scale)

    @pl.loop(0, count // BLOCK)
    def _(b):
        slot = key_slot[b]
        block = all_ref[slot >> 1, depth : 2 * depth, half_at(slot)]
        key_s[tile_at(b, BLOCK), :] = block.T
        value_s[:, tile_at(b, BLOCK)] = all_ref[slot >> 1, 2 * depth : 3 * depth, half_at(slot)]

    chains = SELF_CHAINS
    lanes = query_tile // chains

    @pl.loop(0, queries // query_tile)
    def _(t):
        here = [pl.ds(pl.multiple_of(t * query_tile + i * lanes, lanes), lanes) for i in range(chains)]
        result, lse = forward_tiles(
            plan, t, [query_s[:, at] for at in here], [range_ref[0:1, at] for at in here],
            [range_ref[1:2, at] for at in here],
            lambda j: key_s[tile_at(j, tile), :], lambda j, i: value_s[:, tile_at(j, tile)],
            tile, depth,
        )
        for i in range(chains):
            exact_ref[:, here[i]] = result[i]
            lse_ref[0:1, here[i]] = lse[i]

    @pl.loop(0, queries // BLOCK)
    def _(b):
        slot = query_slot[b]
        out_ref[slot >> 1, :, half_at(slot)] = exact_ref[:, tile_at(b, BLOCK)].astype(low)


def self_backward_kernel(
    tiles, joined, plan, query_slot, key_slot, range_ref, own_ref, all_ref, grad_ref, exact_ref, lse_ref,
    *rest,
):
    if joined:
        carried_ref, dq_ref, *rest = rest
        dkv_ref = dq_ref
        dq_ref[:, dq_ref.shape[1] - carried_ref.shape[1] :, :] = carried_ref[...]
    else:
        dq_ref, dkv_ref, *rest = rest
    rows_ref, query_s, grad_s, key_s, keyt_s, value_s, dq_s, dk_s, dv_s = rest
    query_tile, tile = tiles
    depth, queries = query_s.shape
    count = keyt_s.shape[1]

    @pl.loop(0, queries // BLOCK)
    def _(b):
        slot = query_slot[b]
        query_s[:, tile_at(b, BLOCK)] = own_ref[slot >> 1, 0:depth, half_at(slot)] * low(score_scale)
        grad_s[:, tile_at(b, BLOCK)] = grad_ref[slot >> 1, :, half_at(slot)]

    @pl.loop(0, count // BLOCK)
    def _(b):
        slot = key_slot[b]
        block = all_ref[slot >> 1, depth : 2 * depth, half_at(slot)]
        keyt_s[:, tile_at(b, BLOCK)] = block
        key_s[tile_at(b, BLOCK), :] = block.T
        value_s[tile_at(b, BLOCK), :] = all_ref[slot >> 1, 2 * depth : 3 * depth, half_at(slot)].T

    dk_s[...] = jnp.zeros_like(dk_s)
    dv_s[...] = jnp.zeros_like(dv_s)

    @pl.loop(0, queries // query_tile)
    def _(t):
        here = tile_at(t, query_tile)
        query, grad = query_s[:, here], grad_s[:, here]
        start, stop = range_ref[0:1, here], range_ref[1:2, here]
        lse = lse_ref[0:1, here]
        delta = jnp.sum(grad.astype(full) * exact_ref[:, here], axis=0, keepdims=True)

        def step(j, dq, masked):
            there = tile_at(j, tile)
            scores = contract(key_s[there, :], query, 1, 0)
            if masked:
                scores = masked_scores(scores, j, tile, start, stop)
            probs = jnp.exp(scores - lse)
            dprobs = contract(value_s[there, :], grad, 1, 0)
            dscores = (probs * (dprobs - delta)).astype(low)
            dv_s[:, there] += contract(grad, probs.astype(low), 1, 1)
            dk_s[:, there] += contract(query, dscores, 1, 1)
            return dq + contract(keyt_s[:, there], dscores, 1, 0)

        dq_s[:, here] = over_tiles(plan, t, step, jnp.zeros((depth, query_tile), full))

    @pl.loop(0, queries // BLOCK)
    def _(b):
        slot = query_slot[b]
        dq = (dq_s[:, tile_at(b, BLOCK)] * score_scale).astype(low)
        dq_ref[slot >> 1, 0:depth, half_at(slot)] = dq
        rows_ref[0:depth, tile_at(slot, BLOCK)] = dq

    @pl.loop(0, count // BLOCK)
    def _(b):
        slot = key_slot[b]
        dk = dk_s[:, tile_at(b, BLOCK)].astype(dkv_ref.dtype)
        dv = dv_s[:, tile_at(b, BLOCK)].astype(dkv_ref.dtype)
        at = depth if joined else 0
        dkv_ref[slot >> 1, at : at + depth, half_at(slot)] = dk
        dkv_ref[slot >> 1, at + depth : at + 2 * depth, half_at(slot)] = dv
        if count == queries:
            rows_ref[depth : 2 * depth, tile_at(slot, BLOCK)] = dk.astype(low)
            rows_ref[2 * depth : 3 * depth, tile_at(slot, BLOCK)] = dv.astype(low)


def one_head(values, head, depth):
    rows = lax.broadcasted_iota(jnp.int32, values.shape, 0)
    inside = (rows >= head * depth) & (rows < (head + 1) * depth)
    return jnp.where(inside, values, jnp.zeros_like(values))


def cross_forward_kernel(
    tile, plan, range_ref, query_ref, key_ref, value_ref, out_ref, exact_ref, lse_ref, value_s
):
    depth = value_s.shape[0] // 2

    eye = identity(2 * depth)

    def turn(j, _):
        value_s[:, tile_at(j, tile)] = flipped(eye, value_ref[tile_at(j, tile), :])
        return 0

    lax.fori_loop(plan[0, 0], plan[3, 0], turn, 0)
    query = query_ref[...] * low(score_scale)
    rows = [pl.ds(head * depth, depth) for head in range(2)]
    result, lse = forward_tiles(
        plan, 0, [one_head(query, head, depth) for head in range(2)],
        range_ref[0:1, :], range_ref[1:2, :],
        lambda j: key_ref[tile_at(j, tile), :],
        lambda j, i: value_s[rows[i], tile_at(j, tile)],
        tile, depth,
    )
    for head in range(2):
        exact_ref[rows[head], :] = result[head]
        out_ref[rows[head], :] = result[head].astype(low)
        lse_ref[0, head : head + 1, :] = lse[head]


def cross_backward_kernel(
    tiles, plan, query_slot, range_ref, query_ref, keys_values_ref, grad_ref,
    dq_ref, dkv_ref, packed_ref, query_s, grad_s, keyt_s, dkv_s,
):
    query_tile, tile = tiles
    depth = query_ref.shape[1]
    queries = query_s.shape[1]
    eye = identity(2 * depth)

    @pl.loop(0, queries // BLOCK)
    def _(b):
        slot = query_slot[b]
        at, there = tile_at(b, BLOCK), half_at(slot)
        query_s[:, at] = query_ref[slot >> 1, :, there] * low(score_scale)
        grad_s[:, at] = grad_ref[slot >> 1, :, there]

    @pl.loop(0, keyt_s.shape[1] // tile)
    def _(j):
        at = tile_at(j, tile)
        keyt_s[:, at] = flipped(eye, keys_values_ref[at, :])[0:depth]

    dkv_s[...] = jnp.zeros_like(dkv_s)
    blank = jnp.zeros((depth, query_tile), low)

    @pl.loop(0, queries // query_tile)
    def _(t):
        here = tile_at(t, query_tile)
        grad = grad_s[0:depth, here]
        start, stop = range_ref[0:1, here], range_ref[1:2, here]
        extra = grad_s[depth : depth + 16, here].astype(full)
        lse = extra[0:1] + extra[1:2] + extra[2:3]
        delta = extra[3:4] + extra[4:5] + extra[5:6]
        wide_query = jnp.concatenate([query_s[:, here], blank], axis=0)
        wide_grad = jnp.concatenate([blank, grad], axis=0)
        sides = jnp.concatenate([wide_query, wide_grad], axis=1)

        def step(j, dq, masked):
            there = tile_at(j, tile)
            keys_values = keys_values_ref[there, :]
            scores = contract(keys_values, wide_query, 1, 0)
            if masked:
                scores = masked_scores(scores, j, tile, start, stop)
            probs = jnp.exp(scores - lse)
            dprobs = contract(keys_values, wide_grad, 1, 0)
            dscores = (probs * (dprobs - delta)).astype(low)
            both = jnp.concatenate([dscores, probs.astype(low)], axis=1)
            dkv_s[there, :] += contract(both, sides, 1, 1)
            return dq + contract(keyt_s[:, there], dscores, 1, 0)

        dq = over_tiles(plan, t, step, jnp.zeros((depth, query_tile), full))
        query_s[:, here] = (dq * score_scale).astype(low)

    @pl.loop(0, queries // BLOCK)
    def _(b):
        slot = query_slot[b]
        dq_ref[slot >> 1, :, half_at(slot)] = query_s[:, tile_at(b, BLOCK)]

    total = dkv_s[...].astype(dkv_ref.dtype)
    dkv_ref[...] = total
    devices, half, _ = packed_ref.shape
    total = total.reshape(devices, 2, half, 2 * depth)
    packed_ref[:, :, 0 : 2 * depth] = total[:, 0].astype(low)
    packed_ref[:, :, 2 * depth : 4 * depth] = total[:, 1].astype(low)


def smem():
    return pl.BlockSpec(memory_space=pltpu.SMEM)


def vmem():
    return pl.BlockSpec(memory_space=pltpu.VMEM)


def params():
    return pltpu.CompilerParams(vmem_limit_bytes=VMEM_BYTES)


def self_tiles(queries):
    return min(SELF_TILES[0], queries), min(SELF_TILES[1], queries)


def self_forward(plan, query_slot, key_slot, ranges, own, everyone):
    heads, three, rows = own.shape
    depth = three // 3
    queries, count = heads * rows, everyone.shape[0] * rows
    tile = self_tiles(queries)
    return pl.pallas_call(
        functools.partial(self_forward_kernel, tile),
        out_shape=(
            jax.ShapeDtypeStruct((heads, depth, rows), low),
            jax.ShapeDtypeStruct((depth, queries), full),
            jax.ShapeDtypeStruct((8, queries), full),
        ),
        in_specs=[smem()] * 3 + [vmem()] * 3,
        out_specs=(vmem(),) * 3,
        scratch_shapes=[
            pltpu.VMEM((depth, queries), low),
            pltpu.VMEM((count, depth), low),
            pltpu.VMEM((depth, count), low),
        ],
        compiler_params=params(),
        cost_estimate=pl.CostEstimate(flops=1, bytes_accessed=1, transcendentals=0),
        name="self_forward",
    )(plan, query_slot, key_slot, ranges, own, everyone)


def self_backward(plan, query_slot, key_slot, ranges, own, everyone, grad, exact, lse, kv_type, carried):
    heads, three, rows = own.shape
    depth = three // 3
    queries, count = heads * rows, everyone.shape[0] * rows
    tile = self_tiles(queries)
    joined = heads == everyone.shape[0]
    if joined:
        shapes = (jax.ShapeDtypeStruct((heads, 3 * depth + carried.shape[1], rows), low),)
        extra = (carried,)
    else:
        shapes = (
            jax.ShapeDtypeStruct((heads, depth, rows), low),
            jax.ShapeDtypeStruct((everyone.shape[0], 2 * depth, rows), kv_type),
        )
        extra = ()
    return pl.pallas_call(
        functools.partial(self_backward_kernel, tile, joined),
        out_shape=shapes + (jax.ShapeDtypeStruct((3 * depth, queries), low),),
        in_specs=[smem()] * 3 + [vmem()] * (6 + len(extra)),
        out_specs=(vmem(),) * (len(shapes) + 1),
        scratch_shapes=[
            pltpu.VMEM((depth, queries), low),
            pltpu.VMEM((depth, queries), low),
            pltpu.VMEM((count, depth), low),
            pltpu.VMEM((depth, count), low),
            pltpu.VMEM((count, depth), low),
            pltpu.VMEM((depth, queries), full),
            pltpu.VMEM((depth, count), full),
            pltpu.VMEM((depth, count), full),
        ],
        compiler_params=params(),
        cost_estimate=pl.CostEstimate(flops=1, bytes_accessed=1, transcendentals=0),
        name="self_backward",
    )(plan, query_slot, key_slot, ranges, own, everyone, grad, exact, lse, *extra)


def cross_tiles(queries, count):
    return min(512, queries), min(512, count)


def cross_tile(count):
    return min(CROSS_TILE, count)


def pair_spec(rows, cols):
    return pl.BlockSpec((rows, cols), lambda i: (i, 0))


def cross_forward(plan, ranges, query, keys_values):
    width, rows = query.shape
    count = keys_values.shape[0]
    pairs = H // 2
    wide = width // pairs
    return pl.pallas_call(
        functools.partial(cross_forward_kernel, cross_tile(count)),
        grid=(pairs,),
        out_shape=(
            jax.ShapeDtypeStruct((width, rows), low),
            jax.ShapeDtypeStruct((width, rows), full),
            jax.ShapeDtypeStruct((pairs, 8, rows), full),
        ),
        in_specs=[
            smem(),
            vmem(),
            pair_spec(wide, rows),
            pl.BlockSpec((count, wide), lambda i: (0, i)),
            pl.BlockSpec((count, wide), lambda i: (0, pairs + i)),
        ],
        out_specs=(
            pair_spec(wide, rows),
            pair_spec(wide, rows),
            pl.BlockSpec((1, 8, rows), lambda i: (i, 0, 0)),
        ),
        scratch_shapes=[pltpu.VMEM((wide, count), low)],
        compiler_params=params(),
        cost_estimate=pl.CostEstimate(flops=1, bytes_accessed=1, transcendentals=0),
        name="cross_forward",
    )(plan, ranges, query, keys_values, keys_values)


def cross_backward(plan, query_slot, ranges, query, keys_values, grad, kv_type, parts):
    heads, depth, rows = query.shape
    queries, count = heads * rows, keys_values.shape[0]
    return pl.pallas_call(
        functools.partial(cross_backward_kernel, cross_tiles(queries, count)),
        out_shape=(
            jax.ShapeDtypeStruct((heads, depth, rows), low),
            jax.ShapeDtypeStruct((count, 2 * depth), kv_type),
            jax.ShapeDtypeStruct((parts, count // parts // 2, 4 * depth), low),
        ),
        in_specs=[smem()] * 2 + [vmem()] * 4,
        out_specs=(vmem(),) * 3,
        scratch_shapes=[
            pltpu.VMEM((depth, queries), low),
            pltpu.VMEM((grad.shape[1], queries), low),
            pltpu.VMEM((depth, count), low),
            pltpu.VMEM((count, 2 * depth), full),
        ],
        compiler_params=params(),
        cost_estimate=pl.CostEstimate(flops=1, bytes_accessed=1, transcendentals=0),
        name="cross_backward",
    )(plan, query_slot, ranges, query, keys_values, grad)


def copy_kernel(_, value_ref, square_ref, row_ref):
    square_ref[...] = value_ref[...]
    row_ref[...] = value_ref[...]


def strided_columns(value, first, step, wide):
    rows, cols = value.shape
    count = cols // (step * wide)
    return pl.pallas_call(
        copy_kernel,
        out_shape=(
            jax.ShapeDtypeStruct((2 * rows, count // 2 * wide), value.dtype),
            jax.ShapeDtypeStruct((rows, count * wide), value.dtype),
        ),
        grid_spec=pltpu.PrefetchScalarGridSpec(
            num_scalar_prefetch=1,
            grid=(count,),
            in_specs=[pl.BlockSpec((rows, wide), lambda i, at: (0, i * step + at[0]))],
            out_specs=(
                pl.BlockSpec((rows, wide), lambda i, at: (i // 2, i % 2)),
                pl.BlockSpec((rows, wide), lambda i, at: (0, i)),
            ),
        ),
        compiler_params=params(),
        name="strided_columns",
    )(first.astype(jnp.int32).reshape(1), value)


def owned_kernel(depth, heads, groups, pieces_ref, qkv_ref, ckv_ref, rest_ref):
    parts = pieces_ref.shape[0] // (heads * groups)
    share, width = qkv_ref.shape[0], heads * depth
    everything = 0.0
    for head in range(heads):
        total = 0.0
        for p in range(parts):
            for g in range(groups):
                total = total + pieces_ref[(p * heads + head) * groups + g].astype(full)
        everything = everything + total
        at = head * depth
        for i in range(3):
            qkv_ref[:, i * width + at : i * width + at + depth] = total[:share, i * depth : (i + 1) * depth]
        for i in range(2):
            ckv_ref[:, i * width + at : i * width + at + depth] = total[:share, (3 + i) * depth : (4 + i) * depth]
    rest_ref[...] = everything[share:]


def owned_columns(pieces, share, groups, depth):
    _, rows, cols = pieces.shape
    return pl.pallas_call(
        functools.partial(owned_kernel, depth, H, groups),
        out_shape=(
            jax.ShapeDtypeStruct((share, 3 * H * depth), full),
            jax.ShapeDtypeStruct((share, 2 * H * depth), full),
            jax.ShapeDtypeStruct((rows - share, cols), full),
        ),
        in_specs=[vmem()],
        out_specs=(vmem(),) * 3,
        compiler_params=params(),
        name="owned_columns",
    )(pieces)


def after(value, *others):
    return lax.optimization_barrier((value,) + others)[0]


class Exchange:
    def __init__(self):
        self.fsdp = lax.axis_size("fsdp")
        self.chips = lax.axis_size(CHIP)
        self.core = lax.axis_index("core")
        self.row = lax.axis_index("fsdp")
        self.chip = lax.axis_index(CHIP)
        self.paired = self.fsdp == 2
        self.cube = self.paired and self.chips == 8
        self.near, self.far = (self.chip >> 1) & 1, self.chip >> 2
        self.corner = 2 * (self.chip & 1) + self.core

    def swap(self, value, axis):
        return lax.ppermute(value, axis, [(0, 1), (1, 0)])

    def swap_chip(self, value, bit):
        return lax.ppermute(value, CHIP, [(i, i ^ bit) for i in range(self.chips)])

    def own_piece(self, shard):
        piece = shard.shape[0] // 2
        return lax.dynamic_slice_in_dim(shard, self.core * piece, piece, 0)

    def fetch(self, mine, begin=()):
        if not self.paired:
            return lax.all_gather(mine, ("fsdp", "core"), axis=0, tiled=True)
        return self.swap(after(mine, *begin) if begin else mine, "fsdp")

    def place(self, base, across, corner):
        if not self.paired:
            return across
        piece = across.shape[0]
        start = (1 - self.row) * 2 * piece
        whole = lax.dynamic_update_slice_in_dim(base, across, start + self.core * piece, 0)
        return lax.dynamic_update_slice_in_dim(whole, corner, start + (1 - self.core) * piece, 0)

    def place_all(self, bases, across):
        corner = self.swap(across, "core") if self.paired else across
        placed, at = [], 0
        for base in bases:
            cols = slice(at, at + base.shape[1])
            placed.append(self.place(base, across[:, cols], corner[:, cols]))
            at += base.shape[1]
        return placed

    def gather_last(self, shard):
        if not self.paired:
            return lax.all_gather(shard, "fsdp", axis=shard.ndim - 1, tiled=True)
        other = self.swap(shard, "fsdp")
        return jnp.where(
            self.row == 0,
            jnp.concatenate([shard, other], axis=-1),
            jnp.concatenate([other, shard], axis=-1),
        )


    def hidden_parts(self, shard, axis):
        size = shard.shape[axis]
        if not self.cube:
            wide = size // 2
            return lax.dynamic_slice_in_dim(shard, self.core * wide, wide, axis)
        wide = size // 8
        parts = [
            lax.dynamic_slice_in_dim(shard, (4 * z + self.corner) * wide, wide, axis) for z in range(2)
        ]
        return jnp.concatenate(parts, axis=axis)

    def up_part(self, shard):
        rows, hidden = shard.shape
        if self.cube:
            return strided_columns(shard, self.corner, 4, hidden // 16)
        split = shard.reshape(rows, self.fsdp, 2, hidden // (2 * self.fsdp))
        mine = lax.dynamic_index_in_dim(split, self.core, 2, keepdims=False)
        return mine, mine

    def swap_beside(self, value):
        return self.swap_chip(value, 1) if self.cube else self.swap(value, "fsdp")

    def quad_gather(self, value, hold=()):
        if not self.paired:
            return lax.all_gather(value, QUAD, axis=0, tiled=True), ()
        across = self.swap_beside(value)
        held = after(across, *hold)
        beside = self.swap(value, "core")
        corner = self.swap(held, "core")
        return jnp.concatenate([value, beside, held, corner], axis=0), (across,)

    def quad_sum(self, value):
        if not self.paired:
            total = lax.psum_scatter(value, QUAD, scatter_dimension=0, tiled=True)
            return total.astype(full), total
        rows = value.shape[0] // 4
        parts = value.reshape(2, 2, rows, value.shape[1])
        theirs = self.swap(parts[:, 1], "core")
        both = parts[:, 0].astype(full) + theirs.astype(full)
        got = self.swap_beside(both[1].astype(low))
        return (both[0], got), theirs

    def quad_direct(self, value):
        if not self.paired:
            return lax.psum_scatter(value, QUAD, scatter_dimension=0, tiled=True).astype(full)
        rows = value.shape[0] // 4
        mine, beside, across, corner = [value[i * rows : (i + 1) * rows] for i in range(4)]
        if self.cube:
            moves = [(i, i ^ 3) for i in range(2 * self.chips)]
            far = lax.ppermute(corner, CTX, moves)
        else:
            far = lax.ppermute(corner, QUAD, [(i, 3 - i) for i in range(4)])
        return mine, self.swap(beside, "core"), self.swap_beside(across), far

    def quad_total(self, pending, hold):
        if not self.paired:
            return pending
        mine = after(pending[0], *hold)
        return sum(piece.astype(full) for piece in (mine,) + pending[1:])

    def quad_end(self, pending, hold=()):
        if not self.paired:
            return pending
        mine, got = pending
        return (after(mine, *hold) if hold else mine) + got.astype(full)

    def send_half(self, value, axis, bit, swap, *others):
        if others:
            value = after(value, *others)
        sent = lax.dynamic_index_in_dim(value, 1 - bit, axis, keepdims=False)
        kept = lax.dynamic_index_in_dim(value, bit, axis, keepdims=False)
        return sent, (kept, swap(sent))

    def add(self, halves, *others):
        kept, got = halves
        if others:
            kept = after(kept, *others)
        return kept.astype(full) + got.astype(full)

    def chip_step(self, value, number, *others):
        bit = (self.chip >> number) & 1
        return self.send_half(value, 2 - number, bit, lambda v: self.swap_chip(v, 1 << number), *others)

    def chip_shape(self, value):
        return value.reshape((2, 2, 2, value.shape[0] // 8) + value.shape[1:])

    def chip_scatter(self, value):
        return lax.psum_scatter(value, CHIP, scatter_dimension=0, tiled=True).astype(full)

    def device_shape(self, value):
        rows, cols = value.shape
        return value.reshape(self.chips, 2, self.fsdp, rows // (self.chips * 2 * self.fsdp), cols)

    def device_scatter(self, values):
        stacked = jnp.stack([self.device_shape(v) for v in values], axis=3)
        stacked = lax.psum_scatter(stacked, "core", scatter_dimension=1, tiled=True)
        stacked = lax.psum_scatter(stacked, "fsdp", scatter_dimension=2, tiled=True)
        stacked = lax.psum_scatter(stacked, CHIP, scatter_dimension=0, tiled=True)
        return [stacked[0, 0, 0, i].astype(full) for i in range(len(values))]

    def to_owner(self, value):
        chips, fsdp = self.chips, self.fsdp
        moves = []
        for chip in range(chips):
            for core in range(2):
                for row in range(fsdp):
                    moves.append(
                        ((chip * 2 + core) * fsdp + row, (row * 2 + core) * chips + chip)
                    )
        return lax.ppermute(value, ALL, moves)

    def quad_columns(self, value):
        quad = 2 * self.fsdp
        rows, wide = value.shape
        share = rows // quad
        value = lax.all_to_all(value, QUAD, 0, 1, tiled=True)
        value = value.reshape(share, 2, self.fsdp, wide).transpose(0, 2, 1, 3)
        return value.reshape(share, quad * wide)

    def corner_columns(self, value, hold):
        def block(bits):
            return lax.dynamic_index_in_dim(value, self.corner ^ bits, 0, keepdims=False)

        got = [
            block(0),
            self.swap(block(1), "core"),
            self.swap_chip(block(2), 1),
            lax.ppermute(block(3), CTX, [(i, i ^ 3) for i in range(2 * self.chips)]),
        ]
        got = [after(piece, *hold) for piece in got]
        got = [jnp.where(self.core == 0, got[i], got[i ^ 1]) for i in range(4)]
        got = [jnp.where(self.chip & 1 == 0, got[i], got[i ^ 2]) for i in range(4)]
        got = [piece.astype(full) for piece in got]
        step = value.shape[2] // 4
        return jnp.concatenate(
            [got[i][:, z * step : (z + 1) * step] for z in range(4) for i in range(4)], axis=1
        )

    def hidden_vector(self, value, hidden):
        devices = self.chips * 2 * self.fsdp
        if not self.cube:
            spread = jnp.zeros((hidden,), full)
            at = (self.row * 2 + self.core) * value.shape[0]
            return lax.dynamic_update_slice_in_dim(spread, value, at, 0).reshape(devices, -1)
        spread = jnp.zeros((4, 4, hidden // 16), full)
        spread = lax.dynamic_update_slice_in_dim(spread, value.reshape(4, 1, -1), self.corner, 1)
        return spread.reshape(devices, -1)


def per_device(
    tokens, encoder, cotangent, seq_lengths, source_lengths, pair_order, pair_flip,
    ln_gain, ln_bias, attn_bias, self_qkv, self_out, cross_q, cross_kv, cross_out,
    w_up, up_bias, w_down, down_bias,
):
    move = Exchange()
    resid = tokens[0].astype(full)
    source = encoder[0]
    grad_low = cotangent[0]
    rows, width = resid.shape
    src_rows = source.shape[0]
    depth = width // H
    ctx_count = lax.axis_size(CTX)
    parts = lax.axis_size("part")
    devices = ctx_count * move.fsdp
    here = lax.axis_index(CTX)
    part = lax.axis_index("part")

    plan = attention_plan(
        pair_order[0], pair_flip[0], seq_lengths[0], source_lengths[0],
        here, part, parts, rows, src_rows * ctx_count,
    )
    query_slot, key_slot, self_plan, cross_plan, group_plan, self_ranges, cross_ranges, group_ranges = plan

    small = [ln_gain, ln_bias, attn_bias.reshape(6, -1), down_bias[None]]
    bias_up = move.hidden_parts(up_bias, 0)
    if move.cube:
        small.append(bias_up.reshape(2, -1))
    small = move.gather_last(jnp.concatenate(small, axis=0)).astype(full)
    if move.cube:
        half = small.shape[1] // 2
        bias_up = jnp.concatenate([small[13, :half], small[14, :half], small[13, half:], small[14, half:]])
    bias_up = bias_up.astype(full)
    gains, shifts, biases, bias_down = small[0:3], small[3:6], small[6:12].reshape(2, 3, width), small[12]
    shards = (cross_kv, self_out, cross_q, cross_out)
    middle = jnp.concatenate([move.own_piece(w) for w in shards], axis=1)
    qkv_piece = move.own_piece(self_qkv)
    bases = [jnp.concatenate([w, w], axis=0) if move.paired else w for w in shards]
    qkv_base = jnp.concatenate([self_qkv, self_qkv], axis=0) if move.paired else self_qkv
    up_mine, up_local = move.up_part(w_up)
    down_mine = move.hidden_parts(w_down, 0)
    if move.cube:
        shard_rows = w_up.shape[0]
        branch_piece = jnp.concatenate([up_mine, down_mine], axis=0)
        up_base = jnp.concatenate([up_local, up_local], axis=0)
        down_base = jnp.concatenate([down_mine, down_mine], axis=0)
        later = (up_base, down_base, branch_piece)
    else:
        later = ()

    got_qkv = move.fetch(qkv_piece)
    group_source = lax.all_gather(source, HEADS, axis=0, tiled=True)

    norm_one, back_one = jax.vjp(layer_norm, resid, gains[0], shifts[0])
    normed_one = norm_one.astype(low)
    w_qkv, = move.place_all([qkv_base], after(got_qkv, *plan, *bases, middle, up_mine))
    projected = contract(w_qkv, normed_one, 0, 1)
    shift_qkv = jnp.concatenate([biases[0, 0], jnp.zeros((width,), full), biases[0, 1]])
    projected = (projected + shift_qkv[:, None]).astype(low)
    projected = projected.reshape(3, H, depth, rows).transpose(1, 0, 2, 3).reshape(H, 3 * depth, rows)
    own_heads = lax.all_to_all(projected, HEADS, 0, 0, tiled=True)

    got_middle = move.fetch(middle, (got_qkv,))
    self_in = after(own_heads, *later)
    all_heads = self_in if parts == 1 else lax.all_gather(self_in, "part", axis=0, tiled=True)
    self_args = (self_plan, query_slot, key_slot, self_ranges, self_in, all_heads)
    self_low, self_exact, self_lse = self_forward(*self_args)
    self_att = lax.all_to_all(self_low, HEADS, 0, 0, tiled=True).reshape(width, rows)
    w_ckv, w_out, w_cq, w_cout = move.place_all(bases, after(got_middle, self_low))
    grad_quad, got_quad = move.quad_gather(after(grad_low, self_low), (self_att,))

    every_source = group_source
    if parts > 1:
        every_source = lax.all_gather(group_source, "part", axis=0, tiled=True)
    shift_ckv = jnp.concatenate([jnp.zeros((width,), full), biases[1, 1]])
    src_kv = (jnp.dot(every_source, w_ckv, preferred_element_type=full) + shift_ckv).astype(low)
    mixed_one = resid + contract(self_att, w_out, 0, 0) + biases[0, 2]

    norm_two, back_two = jax.vjp(layer_norm, mixed_one, gains[1], shifts[1])
    normed_two = norm_two.astype(low)
    cross_query = (contract(w_cq, normed_two, 0, 1) + biases[1, 0][:, None]).astype(low)
    cross_query = after(cross_query, *got_quad) if move.cube else cross_query
    group_one = lax.all_gather(after(norm_one, self_att).astype(low), HEADS, axis=0, tiled=True)
    cross_att, cross_exact, cross_lse = cross_forward(cross_plan, cross_ranges, cross_query, src_kv)
    mixed_two = mixed_one + contract(cross_att, w_cout, 0, 0) + biases[1, 2]

    head = lax.axis_index(HEADS)
    head_cols = [
        lax.dynamic_slice_in_dim(w_ckv, i * width + head * depth, depth, 1) for i in range(2)
    ]
    head_shift = jnp.concatenate(
        [jnp.zeros((depth,), full), lax.dynamic_slice_in_dim(biases[1, 1], head * depth, depth, 0)]
    )
    head_kv = jnp.dot(after(every_source, cross_att), jnp.concatenate(head_cols, axis=1), preferred_element_type=full)
    head_kv = (head_kv + head_shift).astype(low)

    norm_three, back_three = jax.vjp(layer_norm, mixed_two, gains[2], shifts[2])
    three_low = norm_three.astype(low)
    if move.cube:
        got_branch = move.swap(after(branch_piece, got_middle), "fsdp")
        theirs = after(got_branch, cross_att)
        start = (1 - move.row) * shard_rows
        half = up_mine.shape[1]
        w_upper = lax.dynamic_update_slice(up_base, theirs[:shard_rows], (start, 0))
        w_upper = lax.dynamic_update_slice(w_upper, theirs[shard_rows : 2 * shard_rows], (start, half))
        w_lower = lax.dynamic_update_slice_in_dim(
            down_base, theirs[2 * shard_rows :], (1 - move.row) * down_mine.shape[0], 0
        )
    else:
        w_upper = lax.all_to_all(up_mine, "fsdp", 1, 0, tiled=True).reshape(width, -1)
        w_lower = down_mine
    wide = w_upper.shape[1]
    quad_three, _ = move.quad_gather(three_low)
    if move.cube:
        quad_three = after(quad_three, got_branch, head_kv)
    hidden_pre = jnp.dot(quad_three, w_upper, preferred_element_type=full) + bias_up
    head_query = after(cross_query.reshape(H, depth, rows), quad_three)
    head_query = lax.all_to_all(head_query, HEADS, 0, 0, tiled=True)
    activated, back_gelu = jax.vjp(gelu_tanh, hidden_pre)
    act_low = activated.astype(low)
    grad_act = contract(grad_quad, w_lower, 1, 1)
    grad_hidden = back_gelu(grad_act)[0].astype(low)
    grad_three, met = move.quad_sum(contract(after(grad_hidden, head_query), w_upper, 1, 1).astype(low))

    grad_out = grad_low.astype(full)
    grad_b_lower = column_sums(grad_low)
    grad_w_lower = contract(after(act_low, met), grad_quad, 0, 0).astype(low)
    grad_b_upper = column_sums(grad_hidden)
    sent = ()
    if move.cube:
        lower = grad_w_lower.reshape(2, 2, 2, -1, width)
        sent_a, lower = move.send_half(lower, 2, move.row, lambda v: move.swap(v, "fsdp"))
        sent = (sent_a,)
    grad_three = move.quad_end(grad_three, sent)
    grad_ln_three, gain_three, shift_three = back_three(grad_three)
    grad_two = grad_out + grad_ln_three

    grad_two_low = grad_two.astype(low)
    grad_b_cout = column_sums(grad_two_low)
    grad_cross_att = contract(w_cout, grad_two_low, 1, 1).astype(low)
    cross_rows = grad_cross_att.reshape(H, depth, rows)
    deltas = jnp.sum(cross_rows.astype(full) * cross_exact.reshape(H, depth, rows), axis=1)
    lse_rows = cross_lse[:, 0:2].reshape(H, rows)
    extra = jnp.stack(in_thirds(lse_rows) + in_thirds(deltas), axis=1)
    extra = jnp.pad(extra, ((0, 0), (0, 10), (0, 0)))
    cross_rows = jnp.concatenate([cross_rows, extra], axis=1)
    grad_head = lax.all_to_all(cross_rows, HEADS, 0, 0, tiled=True)
    grad_w_upper = contract(after(quad_three, grad_cross_att), grad_hidden, 0, 0).astype(low)
    branch = jnp.dot(after(act_low, grad_cross_att), w_lower, preferred_element_type=full).astype(low)
    branch_sum = move.quad_direct(branch)
    sent_b = grad_w_upper
    if move.cube:
        upper = grad_w_upper.reshape(2, 2, 4, 2, -1, wide)
        sent_b, upper = move.send_half(upper, 3, move.row, lambda v: move.swap(v, "fsdp"))
    head_in = after(grad_head, head_query, head_kv, sent_b, group_one)
    head_cq, head_dkv_rows, packed_dkv = cross_backward(
        group_plan, query_slot, group_ranges, head_query, head_kv, head_in,
        low if parts == 1 else full, ctx_count,
    )
    if parts > 1:
        head_dkv_rows = lax.psum_scatter(head_dkv_rows, "part", scatter_dimension=0, tiled=True).astype(low)
    head_cq_sent = after(head_cq, lower[1]) if move.cube else head_cq
    grad_cq = lax.all_to_all(head_cq_sent, HEADS, 0, 0, tiled=True).reshape(width, rows)
    if move.cube:
        lower = move.add(lower, head_cq).astype(low)
        _, lower = move.send_half(lower, 1, move.near, lambda v: move.swap_chip(v, 2))
    grad_b_cq = jnp.sum(grad_cq.astype(full), axis=1)
    grad_ln_two, gain_two, shift_two = back_two(contract(grad_cq, w_cq, 0, 1))
    grad_one = grad_two + grad_ln_two

    grad_one_low = grad_one.astype(low)
    grad_b_out = column_sums(grad_one_low)
    grad_self_att = contract(w_out, grad_one_low, 1, 1).astype(low).reshape(H, depth, rows)
    grad_heads = lax.all_to_all(grad_self_att, HEADS, 0, 0, tiled=True)
    grad_w_cout = contract(after(cross_att, head_cq), grad_two_low, 1, 0).astype(low)
    grad_w_cq = contract(after(normed_two, grad_self_att), grad_cq, 0, 1).astype(low)
    grad_w_out = contract(after(self_att, grad_self_att), grad_one_low, 1, 0).astype(low)
    if move.cube:
        square = []
        for one in (grad_w_cout, grad_w_cq, grad_w_out):
            _, both = move.send_half(move.device_shape(one), 1, move.core, lambda v: move.swap(v, "core"))
            square.append(move.add(both).astype(low))
        sent_c, square = move.send_half(jnp.stack(square, axis=1), 2, move.row, lambda v: move.swap(v, "fsdp"))
        upper = move.add(upper, grad_self_att).astype(low)
        sent_b, upper = move.send_half(upper, 1, move.near, lambda v: move.swap_chip(v, 2))
        grad_heads = after(grad_heads, sent_b, sent_c)
    *head_grads, head_rows = self_backward(
        *self_args, grad_heads, self_exact, self_lse, low if parts == 1 else full, packed_dkv
    )
    if parts > 1:
        head_dkv = lax.psum_scatter(head_grads[1], "part", scatter_dimension=0, tiled=True).astype(low)
        head_grad = jnp.concatenate([head_grads[0], head_dkv], axis=1)
        head_rows = head_grad.transpose(1, 0, 2).reshape(3 * depth, H * rows)
        own_dkv = lax.all_to_all(head_dkv_rows.reshape(H, src_rows, 2 * depth), HEADS, 0, 0, tiled=True)
    else:
        head_grad = head_grads[0]
    if move.cube:
        head_grad = after(head_grad, upper[1], square[1])
    grad_qkv = lax.all_to_all(head_grad, HEADS, 0, 0, tiled=True)
    if parts == 1:
        packed = grad_qkv[:, 3 * depth :]
        own_dkv = jnp.concatenate([packed[:, :, : 2 * depth], packed[:, :, 2 * depth :]], axis=1)
        grad_qkv = grad_qkv[:, : 3 * depth]
    if move.cube:
        upper = move.add(upper, head_rows).astype(low)
        sent_b, upper = move.send_half(upper, 0, move.far, lambda v: move.swap_chip(v, 4))
        square = move.add(square, head_rows).astype(low)
        square = square.reshape((2, 2, 2) + square.shape[1:])
        sent_c, square = move.send_half(square, 2, move.chip & 1, lambda v: move.swap_chip(v, 1))
        soon = (sent_b, sent_c)
    else:
        soon = (head_rows,)
    head_w = contract(after(head_rows, *soon), group_one, 1, 0).astype(low)
    head_c = contract(group_source, after(head_dkv_rows, *soon), 0, 0).astype(low)
    flown = ()
    if move.cube:
        square = move.add(square, head_w).astype(low)
        sent_a, square = move.send_half(square, 1, move.near, lambda v: move.swap_chip(v, 2))
        lower = move.add(lower, head_c).astype(low)
        sent_b, lower = move.send_half(lower, 0, move.far, lambda v: move.swap_chip(v, 4))
        flown = (sent_a, sent_b)
    grad_qkv = grad_qkv.reshape(H, 3, depth, rows).transpose(1, 0, 2, 3).reshape(3 * width, rows)
    grad_ln_one, gain_one, shift_one = back_one(contract(after(grad_qkv, *flown), w_qkv, 0, 1))
    grad_input = grad_one + grad_ln_one

    own_dk = own_dkv[:, :, :depth].transpose(1, 0, 2).reshape(src_rows, width)
    own_dv = own_dkv[:, :, depth:].transpose(1, 0, 2).reshape(src_rows, width)
    head_all = jnp.concatenate([head_w.T, head_c], axis=1)
    grad_source = contract(jnp.concatenate([own_dk, own_dv], axis=1), w_ckv, 1, 1)
    cols = head_all.shape[1]
    share = width // devices

    if not move.cube:
        lower_own = move.to_owner(move.chip_scatter(grad_w_lower).astype(low)).astype(full)
        upper_own = move.quad_columns(move.chip_scatter(grad_w_upper).astype(low)).astype(full)
        cout_own, cq_own, out_own = move.device_scatter([grad_w_cout, grad_w_cq, grad_w_out])

    head_sums = jnp.sum(head_rows.astype(full), axis=1)
    spread = [
        lax.dynamic_update_slice_in_dim(jnp.zeros((width,), full), part, head * depth, 0)
        for part in (head_sums[:depth], head_sums[2 * depth :], column_sums(head_dkv_rows[:, depth:]))
    ]
    early = [gain_two, gain_three, shift_two, shift_three, spread[0], spread[1],
             grad_b_out, grad_b_cq, spread[2], grad_b_cout, grad_b_lower]

    def by_owner(vectors):
        stacked = jnp.stack(vectors).reshape(len(vectors), devices, share)
        return stacked.transpose(1, 0, 2).reshape(devices, len(vectors) * share)

    def in_rows(values):
        count = -(-values.shape[1] // cols)
        values = jnp.pad(values, ((0, 0), (0, count * cols - values.shape[1])))
        return values.astype(low).reshape(devices, count, cols)

    hidden = wide * 2 * move.fsdp
    early_rows = in_rows(
        jnp.concatenate([by_owner(early), move.hidden_vector(grad_b_upper, hidden)], axis=1)
    )
    late_rows = in_rows(by_owner([gain_one, shift_one]))
    outgoing = jnp.concatenate(
        [head_all.reshape(devices, share, cols), early_rows, late_rows], axis=1
    )
    incoming = lax.all_to_all(outgoing, ALL, 0, 0, tiled=True)
    result = mixed_two + move.quad_total(branch_sum, soon) + bias_down
    if move.cube:
        lower_own = move.add(lower, incoming)
        upper_own = move.corner_columns(move.add(upper, grad_ln_one).astype(low), (incoming,))
        square = move.add(square, outgoing).astype(low)
        _, square = move.send_half(square, 0, move.far, lambda v: move.swap_chip(v, 4))
        cout_own, cq_own, out_own = tuple(move.add(square, incoming))
    qkv_own, ckv_own, tail = owned_columns(incoming, share, move.fsdp, depth)
    at = early_rows.shape[1]
    first = tail[:at].reshape(-1)
    vec = first[: 11 * share].reshape(11, share)
    bup_own = first[11 * share : 11 * share + hidden // devices]
    last = tail[at:].reshape(-1)[: 2 * share].reshape(2, share)
    return (
        result.astype(low)[None],
        grad_input[None],
        grad_source[None],
        jnp.stack([last[0], vec[0], vec[1]]),
        jnp.stack([last[1], vec[2], vec[3]]),
        vec[4:10].reshape(2, 3, share),
        qkv_own,
        out_own,
        cq_own,
        ckv_own,
        cout_own,
        upper_own,
        bup_own,
        lower_own,
        vec[10],
    )


def solution(mesh):
    ctx, fsdp = mesh.shape["ctx"], mesh.shape["fsdp"]
    inner = Mesh(mesh.devices.reshape(ctx // H, H // 2, 2, fsdp), ALL)
    tokens = P("fsdp", CTX, None)
    group = P("fsdp", None)
    owned = P(ALL, None)
    return jax.shard_map(
        per_device,
        mesh=inner,
        in_specs=(tokens,) * 3
        + (group,) * 4
        + (P(None, "fsdp"), P(None, "fsdp"), P(None, None, "fsdp"))
        + (group,) * 6
        + (P("fsdp"), group, P("fsdp")),
        out_specs=(tokens,) * 3
        + (P(None, ALL), P(None, ALL), P(None, None, ALL))
        + (owned,) * 6
        + (P(ALL), owned, P(ALL)),
        check_vma=False,
    )
```
